32 devices in a mesh: gx: 8 (over y, x, core), gy: 4 (over z).
Axes of the slice: x: 2, y: 2, z: 4, core: 2. Of those that a mesh axis runs over, the one named last changes fastest.
Arguments:
- load_cases: float32 [16, 12, 64, 128], P('gx', 'gy')
- matrix_tiles: float32 [16, 12, 64, 320], P('gx', 'gy')
- block_cols: int32 [16, 12, 5], P('gx', 'gy'), may hold values from 1 to 18, as said below
- smoother_blocks: float32 [16, 12, 4096], P('gx', 'gy')
- near_null: float32 [16, 12, 384], P('gx', 'gy'), may hold values from -0.75 to 0.75
- coarse_map: int32 [16, 12], P('gx', 'gy'), may hold values from 0 to 31, as said below
- coarse_inverse: float32 [192, 192], P(('gx', 'gy')), as said below
Outputs:
- solution: float32 [16, 12, 64, 128], P('gx', 'gy')
- residual: float32 [16, 12, 64, 128], P('gx', 'gy')
The draws below stay inside these ranges and needn't reach their ends.
Inputs may be any that keep to these rules, and one draw needn't show every extreme that they name: `block_cols`: each aggregate's 5 slots name the aggregate itself and its four grid neighbours, each once, in an order drawn for each aggregate, as row-major indices (row width 3 + 2) into the device's block of aggregates extended by one aggregate on every side. `coarse_map`: all aggregates of one device's block of 2 x 3 aggregates map to one coarse aggregate, and different blocks to different coarse aggregates. coarse_inverse is symmetric.
All inputs are finite; a program needn't handle non-finite values.
Results may differ from the reference program's by a relative error of at most 0.0003.
Values sent between devices are 32-bit elements; how exact they have to be, the bound alone decides.
A program may use at most 64 MiB of HBM per device.

```python
import math
import jax
import jax.numpy as jnp
from jax import lax

AX = 2
AY = 3
BLK = 64
SLOTS = 5
NULLS = 6
R = 128
NAX = 16
NAY = 12
NCA = 32
NC = 192


def slot_order(key):
    scores = jax.random.randint(jax.random.fold_in(key, 17), (NAX, NAY, SLOTS), 0, 1 << 20) * 8
    scores = scores + jnp.arange(SLOTS, dtype=jnp.int32)[None, None, :]
    return jnp.argsort(scores, axis=-1).astype(jnp.int32)


def draw_block_cols(key, part):
    order = slot_order(key)
    row_steps = jnp.array([0, -1, 1, 0, 0], dtype=jnp.int32)[order]
    col_steps = jnp.array([0, 0, 0, -1, 1], dtype=jnp.int32)[order]
    local_rows = (jnp.arange(NAX, dtype=jnp.int32) % AX)[:, None, None]
    local_cols = (jnp.arange(NAY, dtype=jnp.int32) % AY)[None, :, None]
    return ((local_rows + 1 + row_steps) * (AY + 2) + local_cols + 1 + col_steps).astype(jnp.int32)


def draw_coarse_map(key, part):
    shuffled = jax.random.permutation(jax.random.fold_in(key, 61), NCA).astype(jnp.int32)
    block_rows = (jnp.arange(NAX, dtype=jnp.int32) // AX)[:, None]
    block_cols_here = (jnp.arange(NAY, dtype=jnp.int32) // AY)[None, :]
    owner = (block_rows * (NAY // AY) + block_cols_here).astype(jnp.int32)
    return shuffled[owner].astype(jnp.int32)


def draw_matrix_tiles(key, part):
    order = slot_order(key)
    self_slot = (order == 0).astype(jnp.float32)[:, :, None, :, None]
    noise = jax.random.uniform(jax.random.fold_in(key, 29), (NAX, NAY, BLK, SLOTS, BLK), jnp.float32, -1.0, 1.0)
    amplitude = self_slot * (0.025 / BLK) + (1.0 - self_slot) * (0.75 / (4.0 * BLK))
    identity = (jnp.arange(BLK)[:, None] == jnp.arange(BLK)[None, :]).astype(jnp.float32)
    diagonal = self_slot * identity[None, None, :, None, :]
    return (noise * amplitude + diagonal).reshape(NAX, NAY, BLK, SLOTS * BLK)


def draw_smoother_blocks(key, part):
    noise = jax.random.uniform(jax.random.fold_in(key, 41), (NAX, NAY, BLK, BLK), jnp.float32, -1.0, 1.0)
    identity = (jnp.arange(BLK)[:, None] == jnp.arange(BLK)[None, :]).astype(jnp.float32)
    blocks = 0.9 * identity[None, None, :, :] + noise * (0.8 / BLK)
    return blocks.reshape(NAX, NAY, BLK * BLK)


def draw_load_cases(key, part):
    sample = jnp.clip(jax.random.normal(jax.random.fold_in(key, 3), (NAX, NAY, BLK, R), jnp.float32), -6.0, 6.0)
    row_scale = jnp.exp(jax.random.uniform(jax.random.fold_in(key, 5), (NAX, NAY), jnp.float32, math.log(0.3), math.log(3.0)))
    case_scale = jnp.exp(jax.random.uniform(jax.random.fold_in(key, 6), (R,), jnp.float32, math.log(0.3), math.log(3.0)))
    grid_rows = jnp.arange(NAX, dtype=jnp.float32) / (NAX - 1)
    grid_cols = jnp.arange(NAY, dtype=jnp.float32) / (NAY - 1)
    rising = 0.6 + 0.6 * (grid_rows[:, None] + grid_cols[None, :])
    return sample * (row_scale * rising)[:, :, None, None] * case_scale[None, None, None, :]


def draw_coarse_inverse(key, part):
    sample = jnp.clip(jax.random.normal(jax.random.fold_in(key, 53), (NC, NC), jnp.float32), -6.0, 6.0)
    identity = (jnp.arange(NC)[:, None] == jnp.arange(NC)[None, :]).astype(jnp.float32)
    return (sample + sample.T) * (0.3 * (2.0 * NC) ** (-0.5)) + 0.8 * identity


def levels(stream_key, extent, cuts, low, high):
    factor_of = 1.0
    for dim, blocks in cuts:
        draws = jax.random.uniform(jax.random.fold_in(jax.random.fold_in(stream_key, 6), dim), (blocks,), jnp.float32, low / len(cuts), high / len(cuts))
        factor_of = factor_of * jnp.repeat(jnp.exp(draws), extent[dim] // blocks).reshape((-1,) + (1,) * (len(extent) - 1 - dim))
    return factor_of


def scatter_about(own_key, extent, deviation, limit, shards=(), held_as=jnp.bfloat16):
    entries = jax.random.normal(own_key, extent, jnp.float32) * deviation
    if len(shards) > 0:
        entries = levels(own_key, extent, shards, -0.22, 0.18) * entries
    return jnp.clip(entries, min=-limit, max=limit).astype(held_as)


def setup_inputs(seed: int = 0) -> dict:
    keys = jax.random.split(jax.random.key(seed), 8)
    return {
        "load_cases": draw_load_cases(jax.random.fold_in(keys[7], 71), 0),
        "matrix_tiles": draw_matrix_tiles(jax.random.fold_in(keys[7], 71), 0),
        "block_cols": draw_block_cols(jax.random.fold_in(keys[7], 71), 0),
        "smoother_blocks": draw_smoother_blocks(jax.random.fold_in(keys[7], 71), 0),
        "near_null": scatter_about(keys[4], (NAX, NAY, NULLS * BLK), BLK ** -0.5, 0.75, ((0, 8), (1, 4)), jnp.float32),
        "coarse_map": draw_coarse_map(jax.random.fold_in(keys[7], 71), 0),
        "coarse_inverse": draw_coarse_inverse(jax.random.fold_in(keys[7], 71), 0),
    }


relax_weight = 0.8
highest = lax.Precision.HIGHEST


def apply_operator(vector_field, matrix_tiles, block_cols):
    padded = jnp.pad(vector_field, ((1, 1), (1, 1), (0, 0), (0, 0)))
    grid_rows = jnp.arange(NAX, dtype=jnp.int32)
    grid_cols = jnp.arange(NAY, dtype=jnp.int32)
    row_first = (grid_rows - grid_rows % AX)[:, None, None]
    col_first = (grid_cols - grid_cols % AY)[None, :, None]
    source_rows = (row_first + block_cols // (AY + 2)).astype(jnp.int32)
    source_cols = (col_first + block_cols % (AY + 2)).astype(jnp.int32)

    def one_row(inputs):
        tile_row, rows_here, cols_here = inputs
        picked = padded[rows_here, cols_here].reshape(NAY, SLOTS * BLK, R)
        return jnp.einsum("jbk,jkr->jbr", tile_row, picked, precision=highest)

    return lax.map(one_row, (matrix_tiles, source_rows, source_cols))


def relax(defect, smoother_blocks):
    blocks = smoother_blocks.reshape(NAX, NAY, BLK, BLK)
    return relax_weight * jnp.einsum("ijab,ijbr->ijar", blocks, defect, precision=highest)


def coarse_correct(defect, near_null, coarse_map, coarse_inverse):
    modes = near_null.reshape(NAX, NAY, NULLS, BLK)
    onehot = (coarse_map[:, :, None] == jnp.arange(NCA, dtype=jnp.int32)[None, None, :]).astype(jnp.float32)
    contrib = jnp.einsum("ijkb,ijbr->ijkr", modes, defect, precision=highest)
    gathered = jnp.einsum("ijc,ijkr->ckr", onehot, contrib, precision=highest).reshape(NC, R)
    values = jnp.dot(coarse_inverse, gathered, precision=highest)
    coarse_back = jnp.einsum("ijc,ckr->ijkr", onehot, values.reshape(NCA, NULLS, R), precision=highest)
    return jnp.einsum("ijkb,ijkr->ijbr", modes, coarse_back, precision=highest)


def reference(load_cases, matrix_tiles, block_cols, smoother_blocks, near_null, coarse_map, coarse_inverse):
    def operate(vector_field):
        return apply_operator(vector_field, matrix_tiles, block_cols)

    def smooth(defect):
        return relax(defect, smoother_blocks)

    def correct(defect):
        return coarse_correct(defect, near_null, coarse_map, coarse_inverse)

    first = smooth(load_cases)
    first = first + correct(load_cases - operate(first))
    precond = first + smooth(load_cases - operate(first))
    defect = load_cases - operate(precond)
    update = smooth(defect)
    update = update + correct(defect - operate(update))
    update = update + smooth(defect - operate(update))
    precond = precond + update
    image = operate(precond)
    aligned = jnp.sum(load_cases * precond, axis=(0, 1, 2))
    curved = jnp.sum(precond * image, axis=(0, 1, 2))
    alpha = aligned / curved
    solution = alpha * precond
    residual = load_cases - alpha * image
    return (solution, residual)
```

```python
import functools

import jax
import jax.numpy as jnp
from jax import lax
from jax.experimental import pallas as pl
from jax.experimental.pallas import tpu as pltpu
from jax.sharding import PartitionSpec as P

relax_weight = 0.8
highest = lax.Precision.HIGHEST


def padded(cells, sides, width):
    for axis, dim in sides:
        count = lax.axis_size(axis)
        ends = count - 1
        head = lax.slice_in_dim(cells, 0, width, axis=dim)
        tail = lax.slice_in_dim(cells, cells.shape[dim] - width, cells.shape[dim], axis=dim)
        cells = jnp.concatenate(
            [
                lax.ppermute(tail, axis, [(i, (i + 1) % count) for i in range(ends)]),
                cells,
                lax.ppermute(head, axis, [((i + 1) % count, i) for i in range(ends)]),
            ],
            axis=dim,
        )
    return cells


def cut(v):
    hi = v.astype(jnp.bfloat16)
    return hi, (v - hi.astype(jnp.float32)).astype(jnp.bfloat16)


def stacked(v):
    hi, lo = cut(v)
    return jnp.concatenate([hi, lo, hi], axis=0)


def mm(a, b):
    return lax.dot_general(a, b, (((1,), (0,)), ((), ())), preferred_element_type=jnp.float32)


def mm_t(a, b, precision=None):
    return lax.dot_general(
        a, b, (((1,), (1,)), ((), ())), precision=precision, preferred_element_type=jnp.float32
    )


def mm3(a_cut, b):
    hi, lo = cut(b)
    return mm(a_cut[0], hi) + (mm(a_cut[0], lo) + mm(a_cut[1], hi))


def flipped(v, mask):
    bit = 1
    while bit <= mask:
        if mask & bit:
            v = v + bit - 2 * bit * lax.rem(v // bit, 2)
        bit *= 2
    return v


def far_first(nx, ny):
    def hops(pair):
        mx, my = pair
        return bin(mx >> 1).count("1") + my + 0.1 * (mx & 1)

    pairs = [(mx, my) for mx in range(nx) for my in range(ny) if mx or my]
    return sorted(pairs, key=hops, reverse=True)


def step_kernel(
    nx, ny, modes,
    b_hbm, a_hbm, cols_hbm, s_hbm, n_hbm, map_hbm, inv_hbm,
    precond_hbm, image_hbm, alpha_ref,
    b_ref, a_ref, cols_ref, s_ref, n_ref, map_ref, inv_ref, loaded,
    blocks, nulls, field, up, down, left, right, local, edge, smoother, info, info_all, near, coarse, coarse_all,
    sums, sums_all, spread, relaxed, relaxed_near, reach, solved, leaving,
    halo_send, halo_recv, near_send, near_recv, relaxed_send, relaxed_recv, col_send, col_recv,
    all_send, all_recv, direct_send, direct_recv, left_sem,
):
    rows, cols, blk, cases = b_ref.shape
    count = rows * cols
    size = count * blk
    n = nx * ny
    width = info.shape[1]
    coarse_rows = n * 8
    around = spread.shape[0]
    x, y = lax.axis_index("gx"), lax.axis_index("gy")
    me = x * ny + y
    sides = (
        (x > 0, (x - 1, y)),
        (x < nx - 1, (x + 1, y)),
        (y > 0, (x, y - 1)),
        (y < ny - 1, (x, y + 1)),
    )
    halos = (up, down, left, right)
    order_of_peers = far_first(nx, ny)
    peers_x = [flipped(x, m) for m in range(nx)]
    peers_y = [flipped(y, m) for m in range(ny)]
    barrier = pltpu.get_barrier_semaphore()

    loads = [
        pltpu.make_async_copy(src, dst, loaded.at[i])
        for i, (src, dst) in enumerate(
            (
                (s_hbm, s_ref), (b_hbm, b_ref), (n_hbm, n_ref), (inv_hbm, inv_ref),
                (map_hbm, map_ref), (cols_hbm, cols_ref), (a_hbm, a_ref),
            )
        )
    ]
    for load in loads:
        load.start()

    coarse_all[...] = jnp.zeros_like(coarse_all)
    info_all[...] = jnp.zeros_like(info_all)

    for mx, my in order_of_peers:
        pl.semaphore_signal(
            barrier, inc=1, device_id=(peers_x[mx], peers_y[my]),
            device_id_type=pl.DeviceIdType.MESH,
        )

    spread[...] = jnp.zeros_like(spread)
    reach[...] = jnp.zeros_like(reach)
    nulls[...] = jnp.zeros_like(nulls)
    info[...] = jnp.zeros_like(info)
    local[...] = jnp.zeros_like(local)
    for side, (here, _) in enumerate(sides):

        @pl.when(jnp.logical_not(here))
        def _():
            halos[side][...] = jnp.zeros_like(halos[side])
            near[side] = jnp.zeros_like(near[side])
            relaxed_near[side] = jnp.zeros_like(relaxed_near[side])

    told, told_all = info.at[0 : modes + 1], info_all.at[:, 0 : modes + 1]

    def at_column(src, dst):
        return [
            pltpu.make_async_remote_copy(
                src_ref=src, dst_ref=dst.at[me], send_sem=col_send.at[j],
                recv_sem=col_recv.at[ny - j],
                device_id=(x, lax.rem(y + j, ny)), device_id_type=pl.DeviceIdType.MESH,
            )
            for j in range(1, ny)
        ]

    def pass_on(src, dst, slot):
        def one(j, carry):
            pltpu.make_async_remote_copy(
                src_ref=src, dst_ref=dst.at[slot], send_sem=all_send, recv_sem=all_recv,
                device_id=(lax.rem(x + j, nx), y), device_id_type=pl.DeviceIdType.MESH,
            ).start()
            return carry

        lax.fori_loop(1, nx, one, 0)

    def told_start():
        for copy in at_column(told, told_all):
            copy.start()
        pass_on(told, told_all, me)

    def told_pass():
        for j in list(range(1, ny, 2)) + list(range(2, ny, 2)):
            slot = x * ny + lax.rem(y + j, ny)
            pltpu.make_async_copy(told, told, col_recv.at[j]).wait()
            pass_on(told_all.at[slot], told_all, slot)

    def wait_many(dst, tiles, sem):
        some = dst.at[pl.ds(0, tiles)]
        pltpu.make_async_copy(some, some, sem).wait()

    def to_all(src, dst, k):
        for mx, my in order_of_peers:
            pltpu.make_async_remote_copy(
                src_ref=src, dst_ref=dst.at[me], send_sem=direct_send.at[k],
                recv_sem=direct_recv.at[k], device_id=(peers_x[mx], peers_y[my]),
                device_id_type=pl.DeviceIdType.MESH,
            ).start()

    def halo_copies(k):
        now = field.at[k]
        out = (
            (now.at[0], down.at[k], 1),
            (now.at[rows - 1], up.at[k], 0),
            (now.at[:, 0], right.at[k], 3),
            (now.at[:, cols - 1], left.at[k], 2),
        )
        return [
            pltpu.make_async_remote_copy(
                src_ref=src, dst_ref=dst,
                send_sem=halo_send.at[k, side], recv_sem=halo_recv.at[k, lands],
                device_id=peer, device_id_type=pl.DeviceIdType.MESH,
            )
            for side, ((src, dst, lands), (_, peer)) in enumerate(zip(out, sides))
        ]

    def halo_start(k):
        for (here, _), copy in zip(sides, halo_copies(k)):
            pl.when(here)(copy.start)

    def halo_wait(k, side):
        buf = halos[side].at[k]
        pl.when(sides[side][0])(pltpu.make_async_copy(buf, buf, halo_recv.at[k, side]).wait)

    def to_sides(src, dst, send, recv):
        return [
            pltpu.make_async_remote_copy(
                src_ref=src, dst_ref=dst.at[lands],
                send_sem=send.at[side], recv_sem=recv.at[lands],
                device_id=peer, device_id_type=pl.DeviceIdType.MESH,
            )
            for side, (lands, (_, peer)) in enumerate(zip((1, 0, 3, 2), sides))
        ]

    def near_copies():
        return to_sides(nulls, near, near_send, near_recv)

    def relaxed_copies():
        return to_sides(relaxed, relaxed_near, relaxed_send, relaxed_recv)

    def from_sides(dst, recv):
        for side, (here, _) in enumerate(sides):
            buf = dst.at[side]
            pl.when(here)(pltpu.make_async_copy(buf, buf, recv.at[side]).wait)

    loads[0].wait()
    for i in range(rows):
        for j in range(cols):
            p = i * cols + j
            for c in range(0, blk * blk, 128):
                blocks[p, 0, c // 128 : c // 128 + 1] = s_ref[j, i : i + 1, c : c + 128]
            flat = blocks[p, 0, 0 : blk * blk // 128]
            for half in range(128 // blk):
                blocks[p, 1, pl.ds(half, blk * blk // 128, stride=128 // blk), 0:blk] = flat[
                    :, half * blk : (half + 1) * blk
                ]
    for p in range(count):
        hi, lo = cut(relax_weight * blocks[p, 1, :, 0:blk])
        smoother[p] = jnp.concatenate([hi, hi, lo], axis=1)

    def smooth(v):
        return jnp.concatenate(
            [mm(smoother[p], stacked(v[p * blk : (p + 1) * blk])) for p in range(count)], axis=0
        )

    def put(v, k):
        field[k] = v.reshape(rows, cols, blk, cases)

    loads[1].wait()
    b = b_ref[...].reshape(size, cases)
    first = smooth(b)
    put(first, 0)

    for load in loads[2:5]:
        load.wait()
    for i in range(rows):
        for j in range(cols):
            p = i * cols + j
            for k in range(modes):
                nulls[k : k + 1, p * blk : (p + 1) * blk] = n_ref[
                    j, i : i + 1, k * blk : (k + 1) * blk
                ]
    info[0:modes, 0 : inv_ref.shape[1]] = inv_ref[...]
    info[modes : modes + 1, :] = jnp.full((1, width), map_ref[0, 0].astype(jnp.float32))

    pl.semaphore_wait(barrier, n - 1)
    for (here, _), copy in zip(sides, near_copies()):
        pl.when(here)(copy.start)
    halo_start(0)
    told_start()
    info_all[pl.ds(me, 1)] = info[...][None]

    loads[5].wait()
    loads[6].wait()
    for i in range(rows):
        for j in range(cols):
            p = i * cols + j
            tiles = [a_ref[i, j, :, s * blk : (s + 1) * blk] for s in range(5)]
            names = [cols_ref[j, i, s] for s in range(5)]
            for d, (di, dj) in enumerate(((0, 0), (-1, 0), (1, 0), (0, -1), (0, 1))):
                e = (i + 1 + di) * (cols + 2) + j + 1 + dj
                tile = tiles[0] * (names[0] == e).astype(jnp.float32)
                for s in range(1, 5):
                    tile = tile + tiles[s] * (names[s] == e).astype(jnp.float32)
                hi, lo = cut(tile)
                ii, jj = i + di, j + dj
                if 0 <= ii < rows and 0 <= jj < cols:
                    q = ii * cols + jj
                    for k, part in enumerate((hi, hi, lo)):
                        at = k * size + q * blk
                        local[p * blk : (p + 1) * blk, at : at + blk] = part
                else:
                    at = (0, j, cols + j, 2 * cols + i, 2 * cols + rows + i)[d]
                    edge[at] = jnp.concatenate([hi, hi, lo], axis=1)

    def places():
        for j in range(cols):
            yield 0, j, j, j
        for j in range(cols):
            yield 1, j, cols + j, (rows - 1) * cols + j
        for i in range(rows):
            yield 2, i, 2 * cols + i, i * cols
        for i in range(rows):
            yield 3, i, 2 * cols + rows + i, i * cols + cols - 1

    def operate(v, k):
        inner = mm(local[...], stacked(v))
        parts = [inner[p * blk : (p + 1) * blk] for p in range(count)]
        for side in (2, 3, 0, 1):
            halo_wait(k, side)
            for at_side, at, e, p in places():
                if at_side == side:
                    parts[p] = parts[p] + mm(edge[e], stacked(halos[side][k, at]))
        return jnp.concatenate(parts, axis=0)

    own_n = nulls[...]
    own_hi, own_lo = cut(own_n)
    own_cat = jnp.concatenate([own_hi, own_hi, own_lo], axis=1)

    def mine(k):
        return coarse.at[k, 0:modes]

    def theirs_all(k):
        return coarse_all.at[k, :, 0:modes]

    def restrict(v, k):
        g = mm(own_cat, stacked(v))
        coarse[k] = g
        to_all(mine(k), theirs_all(k), k)
        coarse_all[k, pl.ds(me, 1)] = g[None]

    def gathered(k):
        wait_many(theirs_all(k), n - 1, direct_recv.at[k])
        return coarse_all[k].reshape(coarse_rows, cases)

    def across(v):
        hi, lo = cut(v)
        return jnp.concatenate([hi, lo, hi], axis=1)

    r = b - operate(first, 0)
    restrict(r, 0)
    t = smooth(r)
    put(t, 1)
    halo_start(1)
    told_pass()

    facing = (
        lambda at: (rows - 1) * cols + at,
        lambda at: at,
        lambda at: at * cols + cols - 1,
        lambda at: at * cols,
    )
    spread[0:8] = mm_t(across(own_n), local[...])
    from_sides(near, near_recv)
    for side, at, e, p in places():
        q = facing[side](at)
        spread[8 * (1 + side) : 8 * (2 + side), p * blk : (p + 1) * blk] = mm_t(
            across(near[side, :, q * blk : (q + 1) * blk]), edge[e]
        )
    for p in range(count):
        relaxed[:, p * blk : (p + 1) * blk] = mm_t(
            across(spread[:, p * blk : (p + 1) * blk]), smoother[p]
        )
    for (here, _), copy in zip(sides, relaxed_copies()):
        pl.when(here)(copy.start)
    reach[0:around] = spread[...] - mm_t(across(relaxed[...]), local[...])
    eye = (
        lax.broadcasted_iota(jnp.int32, (size, size), 0)
        == lax.broadcasted_iota(jnp.int32, (size, size), 1)
    ).astype(jnp.float32).astype(jnp.bfloat16)

    def turned(v):
        return tuple(mm_t(eye, part).astype(jnp.bfloat16) for part in cut(v))

    gain = turned(
        jnp.concatenate([own_n - relaxed[0:8], 0.0 - relaxed[8:around]], axis=0)
    )
    q1 = r - operate(t, 1)

    wait_many(told_all, (nx - 1) * ny, all_recv)
    inv_parts = cut(info_all[...].reshape(coarse_rows, width))
    lane3 = lax.broadcasted_iota(jnp.int32, (n, 8, width), 2).astype(jnp.float32)
    row3 = lax.broadcasted_iota(jnp.int32, (n, 8, width), 1)
    labels = jnp.broadcast_to(info_all[...][:, modes : modes + 1, :], (n, 8, width))
    where3 = labels * float(modes) + row3.astype(jnp.float32)
    order = jnp.where(lane3 == where3, 1.0, 0.0)
    order = jnp.where(row3 < modes, order, 0.0).reshape(coarse_rows, width).astype(jnp.bfloat16)
    lane4 = lax.broadcasted_iota(jnp.int32, (n, 8, coarse_rows), 2).astype(jnp.float32)
    row4 = lax.broadcasted_iota(jnp.int32, (n, 8, coarse_rows), 1)
    labels4 = jnp.broadcast_to(info_all[...][:, modes : modes + 1, 0:1], (n, 8, coarse_rows))
    pick = jnp.where(lane4 == labels4 * 8.0 + row4.astype(jnp.float32), 1.0, 0.0)
    pick = jnp.where(row4 < modes, pick, 0.0).reshape(coarse_rows, coarse_rows).astype(jnp.bfloat16)
    for k, part in enumerate(inv_parts):
        solved[k] = mm_t(mm(pick, part).astype(jnp.bfloat16), order)

    def clipped(px, py):
        return jnp.clip(px, 0, nx - 1) * ny + jnp.clip(py, 0, ny - 1)

    def cross(px, py):
        return [
            clipped(px + dx, py + dy)
            for dx, dy in ((0, 0), (-1, 0), (1, 0), (0, -1), (0, 1))
        ]

    ids = cross(x, y)
    for _, (px, py) in sides:
        ids = ids + cross(px, py)
    lacking = jnp.zeros((reach.shape[0] - 8 * len(ids), coarse_rows), jnp.float32)
    solve = tuple(
        jnp.concatenate(
            [solved[k, pl.ds(pl.multiple_of(d * 8, 8), 8)] for d in ids] + [lacking], axis=0
        ).astype(jnp.bfloat16)
        for k in range(2)
    )

    def mm3_cut(a_cut, b_cut):
        return mm(a_cut[0], b_cut[0]) + (mm(a_cut[0], b_cut[1]) + mm(a_cut[1], b_cut[0]))

    gain_cut = cut(mm3_cut(gain, tuple(part[0:around] for part in solve)))

    from_sides(relaxed_near, relaxed_recv)
    for side, at, e, p in places():
        q = facing[side](at)
        reach[around * (1 + side) : around * (2 + side), p * blk : (p + 1) * blk] = 0.0 - mm_t(
            across(relaxed_near[side, :, q * blk : (q + 1) * blk]), edge[e]
        )
    loss_cut = cut(mm3_cut(turned(reach[...]), solve))

    g = gathered(0)
    r = q1 - mm3(loss_cut, g)
    s = smooth(r)
    put(s, 2)
    halo_start(2)
    precond = first + t + mm3(gain_cut, g) + s
    r = r - operate(s, 2)
    restrict(r, 1)
    t = smooth(r)
    put(t, 3)
    halo_start(3)
    precond = precond + t
    q2 = r - operate(t, 3)
    base = b - q2
    g = gathered(1)
    precond = precond + mm3(gain_cut, g)
    image = base + mm3(loss_cut, g)
    sums[...] = jnp.concatenate(
        [
            jnp.sum(b * precond, axis=0, keepdims=True),
            jnp.sum(precond * image, axis=0, keepdims=True),
            jnp.zeros((6, cases), jnp.float32),
        ],
        axis=0,
    )
    pairs = sums_all.at[:, 0:2]
    to_all(sums.at[0:2], pairs, 2)
    sums_all[pl.ds(me, 1)] = sums[...][None]
    leaving[0] = precond.reshape(rows, cols, blk, cases)
    leaving[1] = image.reshape(rows, cols, blk, cases)
    leaves = [
        pltpu.make_async_copy(leaving.at[k], dst, left_sem.at[k])
        for k, dst in enumerate((precond_hbm, image_hbm))
    ]
    for leave in leaves:
        leave.start()

    for k in range(4):
        for (here, _), copy in zip(sides, halo_copies(k)):
            pl.when(here)(copy.wait_send)
    for (here, _), copy in zip(sides, near_copies()):
        pl.when(here)(copy.wait_send)
    for (here, _), copy in zip(sides, relaxed_copies()):
        pl.when(here)(copy.wait_send)
    for copy in at_column(told, told_all):
        copy.wait_send()
    wait_many(told_all, (nx - 1) * ny, all_send)
    for k in range(2):
        wait_many(theirs_all(k), n - 1, direct_send.at[k])
    for leave in leaves:
        leave.wait()

    wait_many(pairs, n - 1, direct_recv.at[2])
    total = jnp.sum(sums_all[:, 0:2], axis=0)
    alpha_ref[...] = total[0:1] / total[1:2]
    wait_many(pairs, n - 1, direct_send.at[2])


def finish_kernel(b_ref, p_ref, i_ref, alpha_ref, sol_ref, res_ref, held, scale, sems, scale_sem):
    rows = b_ref.shape[0]
    first = pltpu.make_async_copy(alpha_ref, scale, scale_sem)
    first.start()

    def move(k, i):
        ref = (p_ref, i_ref, b_ref, sol_ref, res_ref)[k]
        ends = (ref.at[i], held.at[k, i])
        return pltpu.make_async_copy(*(ends if k < 3 else ends[::-1]), sems.at[k, i])

    for i in range(rows):
        for k in range(3):
            move(k, i).start()
    first.wait()
    alpha = scale[...].reshape(1, 1, -1)
    for i in range(rows):
        move(0, i).wait()
        held[3, i] = alpha * held[0, i]
        move(3, i).start()
        move(1, i).wait()
        move(2, i).wait()
        held[4, i] = held[2, i] - alpha * held[1, i]
        move(4, i).start()
    for i in range(rows):
        move(3, i).wait()
        move(4, i).wait()


def fused(
    nx, ny,
    load_cases, matrix_tiles, block_cols, smoother_blocks, near_null, coarse_map, coarse_inverse
):
    rows, cols, blk, cases = load_cases.shape
    count = rows * cols
    modes = near_null.shape[2] // blk
    n = nx * ny
    width = -(-coarse_inverse.shape[1] // 128) * 128
    block_cols = jnp.transpose(block_cols, (1, 0, 2))
    smoother_blocks = jnp.transpose(smoother_blocks, (1, 0, 2))
    near_null = jnp.transpose(near_null, (1, 0, 2))
    vmem = pl.BlockSpec(memory_space=pltpu.VMEM)
    hbm = pl.BlockSpec(memory_space=pltpu.HBM)
    f32, bf16 = jnp.float32, jnp.bfloat16
    shape = jax.ShapeDtypeStruct(load_cases.shape, f32)
    precond, image, alpha = pl.pallas_call(
        functools.partial(step_kernel, nx, ny, modes),
        out_shape=(shape, shape, jax.ShapeDtypeStruct((1, cases), f32)),
        in_specs=[hbm] * 7,
        out_specs=(hbm, hbm, vmem),
        scratch_shapes=[
            pltpu.VMEM(load_cases.shape, f32),
            pltpu.VMEM(matrix_tiles.shape, f32),
            pltpu.SMEM(block_cols.shape, jnp.int32),
            pltpu.VMEM(smoother_blocks.shape, f32),
            pltpu.VMEM(near_null.shape, f32),
            pltpu.SMEM(coarse_map.shape, jnp.int32),
            pltpu.VMEM(coarse_inverse.shape, f32),
            pltpu.SemaphoreType.DMA((7,)),
            pltpu.VMEM((count, 2, blk, 128), f32),
            pltpu.VMEM((8, count * blk), f32),
            pltpu.VMEM((4, rows, cols, blk, cases), f32),
            pltpu.VMEM((4, cols, blk, cases), f32),
            pltpu.VMEM((4, cols, blk, cases), f32),
            pltpu.VMEM((4, rows, blk, cases), f32),
            pltpu.VMEM((4, rows, blk, cases), f32),
            pltpu.VMEM((count * blk, 3 * count * blk), bf16),
            pltpu.VMEM((2 * (rows + cols), blk, 3 * blk), bf16),
            pltpu.VMEM((count, blk, 3 * blk), bf16),
            pltpu.VMEM((8, width), f32),
            pltpu.VMEM((n, 8, width), f32),
            pltpu.VMEM((4, 8, count * blk), f32),
            pltpu.VMEM((2, 8, cases), f32),
            pltpu.VMEM((2, n, 8, cases), f32),
            pltpu.VMEM((8, cases), f32),
            pltpu.VMEM((n, 8, cases), f32),
            pltpu.VMEM((40, count * blk), f32),
            pltpu.VMEM((40, count * blk), f32),
            pltpu.VMEM((4, 40, count * blk), f32),
            pltpu.VMEM((256, count * blk), f32),
            pltpu.VMEM((2, n * 8, n * 8), f32),
            pltpu.VMEM((2,) + load_cases.shape, f32),
            pltpu.SemaphoreType.DMA((4, 4)),
            pltpu.SemaphoreType.DMA((4, 4)),
            pltpu.SemaphoreType.DMA((4,)),
            pltpu.SemaphoreType.DMA((4,)),
            pltpu.SemaphoreType.DMA((4,)),
            pltpu.SemaphoreType.DMA((4,)),
            pltpu.SemaphoreType.DMA((ny,)),
            pltpu.SemaphoreType.DMA((ny,)),
            pltpu.SemaphoreType.DMA,
            pltpu.SemaphoreType.DMA,
            pltpu.SemaphoreType.DMA((3,)),
            pltpu.SemaphoreType.DMA((3,)),
            pltpu.SemaphoreType.DMA((2,)),
        ],
        compiler_params=pltpu.CompilerParams(
            collective_id=0, has_side_effects=True, vmem_limit_bytes=60 * 2**20
        ),
    )(
        load_cases, matrix_tiles, block_cols, smoother_blocks, near_null, coarse_map,
        coarse_inverse,
    )
    return pl.pallas_call(
        finish_kernel,
        out_shape=(shape, shape),
        in_specs=[hbm, hbm, hbm, hbm],
        out_specs=(hbm, hbm),
        scratch_shapes=[
            pltpu.VMEM((5,) + load_cases.shape, f32),
            pltpu.VMEM((1, cases), f32),
            pltpu.SemaphoreType.DMA((5, rows)),
            pltpu.SemaphoreType.DMA,
        ],
        compiler_params=pltpu.CompilerParams(vmem_limit_bytes=60 * 2**20),
    )(load_cases, precond, image, alpha)


def per_device(
    load_cases, matrix_tiles, block_cols, smoother_blocks, near_null, coarse_map, coarse_inverse
):
    agg_rows, agg_cols, block_size, case_count = load_cases.shape
    mode_count = near_null.shape[2] // block_size
    coarse_total = coarse_inverse.shape[1]
    coarse_aggs = coarse_total // mode_count
    modes = near_null.reshape(agg_rows, agg_cols, mode_count, block_size)
    inverse_blocks = smoother_blocks.reshape(agg_rows, agg_cols, block_size, block_size)

    steps = ((0, 0), (-1, 0), (1, 0), (0, -1), (0, 1))
    tiles = matrix_tiles.reshape(agg_rows, agg_cols, block_size, -1, block_size)
    row_at = jnp.arange(agg_rows, dtype=jnp.int32)[:, None, None]
    col_at = jnp.arange(agg_cols, dtype=jnp.int32)[None, :, None]
    stencil = []
    for dx, dy in steps:
        named = block_cols == (row_at + 1 + dx) * (agg_cols + 2) + col_at + 1 + dy
        stencil.append(jnp.sum(jnp.where(named[:, :, None, :, None], tiles, 0.0), axis=3))

    def operate(vector_field):
        extended = padded(vector_field, (("gx", 0), ("gy", 1)), 1)
        total = 0.0
        for tile, (dx, dy) in zip(stencil, steps):
            cells = extended[1 + dx : 1 + dx + agg_rows, 1 + dy : 1 + dy + agg_cols]
            total = total + jnp.einsum("ijbk,ijkr->ijbr", tile, cells, precision=highest)
        return total

    def smooth(defect):
        return relax_weight * jnp.einsum(
            "ijab,ijbr->ijar", inverse_blocks, defect, precision=highest
        )

    def correct(defect):
        contrib = jnp.einsum("ijkb,ijbr->ijkr", modes, defect, precision=highest)
        own_part = jnp.sum(contrib, axis=(0, 1))
        my_label = coarse_map[0, 0]
        label_value = jnp.reshape(my_label.astype(jnp.float32), (1,))
        pieces, labels = (
            lax.all_gather(own_part[None], ("gx", "gy"), axis=0, tiled=True),
            lax.all_gather(label_value, ("gx", "gy"), axis=0, tiled=True),
        )
        label_ids = labels.astype(jnp.int32)
        placing = (label_ids[:, None] == jnp.arange(coarse_aggs, dtype=jnp.int32)[None, :]).astype(
            jnp.float32
        )
        ordered = jnp.einsum("dc,dkr->ckr", placing, pieces, precision=highest).reshape(
            coarse_total, case_count
        )
        own_rows = jnp.dot(coarse_inverse, ordered, precision=highest)
        solved = lax.all_gather(own_rows, ("gx", "gy"), axis=0, tiled=True)
        mine = lax.dynamic_slice_in_dim(solved, my_label * mode_count, mode_count, 0)
        coarse_back = jnp.broadcast_to(
            mine[None, None], (agg_rows, agg_cols, mode_count, case_count)
        )
        return jnp.einsum("ijkb,ijkr->ijbr", modes, coarse_back, precision=highest)

    first = smooth(load_cases)
    first = first + correct(load_cases - operate(first))
    precond = first + smooth(load_cases - operate(first))
    defect = load_cases - operate(precond)
    update = smooth(defect)
    update = update + correct(defect - operate(update))
    update = update + smooth(defect - operate(update))
    precond = precond + update
    local_aligned = jnp.sum(load_cases * precond, axis=(0, 1, 2))
    aligned = lax.psum(local_aligned, ("gx", "gy"))
    image = operate(precond)
    curved = lax.psum(jnp.sum(precond * image, axis=(0, 1, 2)), ("gx", "gy"))
    alpha = aligned / curved
    solution = alpha * precond
    residual = load_cases - alpha * image
    return (solution, residual)


def solution(mesh):
    nx, ny = mesh.shape["gx"], mesh.shape["gy"]
    step = functools.partial(fused, nx, ny) if nx * ny <= 128 else per_device
    placed = (
        P("gx", "gy", None, None),
        P("gx", "gy", None, None),
        P("gx", "gy", None),
        P("gx", "gy", None),
        P("gx", "gy", None),
        P("gx", "gy"),
        P(("gx", "gy"), None),
    )
    return jax.shard_map(
        step,
        mesh=mesh,
        in_specs=placed,
        out_specs=(P("gx", "gy", None, None), P("gx", "gy", None, None)),
        check_vma=False,
    )
```

```python
import functools

import jax
import jax.numpy as jnp
from jax import lax
from jax.experimental import pallas as pl
from jax.experimental.pallas import tpu as pltpu
from jax.sharding import PartitionSpec as P

relax_weight = 0.8
highest = lax.Precision.HIGHEST


def padded(cells, sides, width):
    for axis, dim in sides:
        count = lax.axis_size(axis)
        ends = count - 1
        head = lax.slice_in_dim(cells, 0, width, axis=dim)
        tail = lax.slice_in_dim(cells, cells.shape[dim] - width, cells.shape[dim], axis=dim)
        cells = jnp.concatenate(
            [
                lax.ppermute(tail, axis, [(i, (i + 1) % count) for i in range(ends)]),
                cells,
                lax.ppermute(head, axis, [((i + 1) % count, i) for i in range(ends)]),
            ],
            axis=dim,
        )
    return cells


def cut(v):
    hi = v.astype(jnp.bfloat16)
    return hi, (v - hi.astype(jnp.float32)).astype(jnp.bfloat16)


def stacked(v):
    hi, lo = cut(v)
    return jnp.concatenate([hi, lo, hi], axis=0)


def mm(a, b):
    return lax.dot_general(a, b, (((1,), (0,)), ((), ())), preferred_element_type=jnp.float32)


def mm_t(a, b, precision=None):
    return lax.dot_general(
        a, b, (((1,), (1,)), ((), ())), precision=precision, preferred_element_type=jnp.float32
    )


def mm3(a_cut, b):
    hi, lo = cut(b)
    return mm(a_cut[0], hi) + (mm(a_cut[0], lo) + mm(a_cut[1], hi))


def flipped(v, mask):
    bit = 1
    while bit <= mask:
        if mask & bit:
            v = v + bit - 2 * bit * lax.rem(v // bit, 2)
        bit *= 2
    return v


def far_first(nx, ny):
    def hops(pair):
        mx, my = pair
        return bin(mx >> 1).count("1") + my + 0.1 * (mx & 1)

    pairs = [(mx, my) for mx in range(nx) for my in range(ny) if mx or my]
    return sorted(pairs, key=hops, reverse=True)


def step_kernel(
    nx, ny, modes,
    b_hbm, a_hbm, cols_hbm, s_hbm, n_hbm, map_hbm, inv_hbm,
    precond_hbm, image_hbm, alpha_ref,
    b_ref, a_ref, cols_ref, s_ref, n_ref, map_ref, inv_ref, loaded,
    blocks, nulls, field, up, down, left, right, local, edge, smoother, info, info_all, near, coarse, coarse_all,
    sums, sums_all, spread, relaxed, relaxed_near, reach, solved, leaving,
    halo_send, halo_recv, near_send, near_recv, relaxed_send, relaxed_recv, col_send, col_recv,
    all_send, all_recv, direct_send, direct_recv, left_sem, entered,
):
    rows, cols, blk, cases = b_ref.shape
    count = rows * cols
    size = count * blk
    n = nx * ny
    width = info.shape[1]
    coarse_rows = n * 8
    around = spread.shape[0]
    x, y = lax.axis_index("gx"), lax.axis_index("gy")
    me = x * ny + y
    sides = (
        (x > 0, (x - 1, y)),
        (x < nx - 1, (x + 1, y)),
        (y > 0, (x, y - 1)),
        (y < ny - 1, (x, y + 1)),
    )
    halos = (up, down, left, right)
    order_of_peers = far_first(nx, ny)
    peers_x = [flipped(x, m) for m in range(nx)]
    peers_y = [flipped(y, m) for m in range(ny)]
    barrier = pltpu.get_barrier_semaphore()

    loads = [
        pltpu.make_async_copy(src, dst, loaded.at[i])
        for i, (src, dst) in enumerate(
            (
                (s_hbm, s_ref), (b_hbm, b_ref), (n_hbm, n_ref), (inv_hbm, inv_ref),
                (map_hbm, map_ref), (cols_hbm, cols_ref), (a_hbm, a_ref),
            )
        )
    ]
    for load in loads:
        load.start()

    coarse_all[...] = jnp.zeros_like(coarse_all)
    info_all[...] = jnp.zeros_like(info_all)

    lines = [pair for pair in order_of_peers if 0 in pair]
    for mx, my in lines:
        pl.semaphore_signal(
            barrier, inc=1, device_id=(peers_x[mx], peers_y[my]),
            device_id_type=pl.DeviceIdType.MESH,
        )

    spread[...] = jnp.zeros_like(spread)
    reach[...] = jnp.zeros_like(reach)
    nulls[...] = jnp.zeros_like(nulls)
    info[...] = jnp.zeros_like(info)
    local[...] = jnp.zeros_like(local)
    for side, (here, _) in enumerate(sides):

        @pl.when(jnp.logical_not(here))
        def _():
            halos[side][...] = jnp.zeros_like(halos[side])
            near[side] = jnp.zeros_like(near[side])
            relaxed_near[side] = jnp.zeros_like(relaxed_near[side])

    told, told_all = info.at[0 : modes + 1], info_all.at[:, 0 : modes + 1]

    def at_column(src, dst):
        return [
            pltpu.make_async_remote_copy(
                src_ref=src, dst_ref=dst.at[me], send_sem=col_send.at[j],
                recv_sem=col_recv.at[ny - j],
                device_id=(x, lax.rem(y + j, ny)), device_id_type=pl.DeviceIdType.MESH,
            )
            for j in range(1, ny)
        ]

    def pass_on(src, dst, slot):
        for mx in range(nx - 1, 0, -1):
            pltpu.make_async_remote_copy(
                src_ref=src, dst_ref=dst.at[slot], send_sem=all_send, recv_sem=all_recv,
                device_id=(peers_x[mx], y), device_id_type=pl.DeviceIdType.MESH,
            ).start()

    def told_pass():
        for j in list(range(1, ny, 2)) + list(range(2, ny, 2)):
            slot = x * ny + lax.rem(y + j, ny)
            pltpu.make_async_copy(told, told, col_recv.at[j]).wait()
            pass_on(told_all.at[slot], told_all, slot)

    def wait_many(dst, tiles, sem):
        some = dst.at[pl.ds(0, tiles)]
        pltpu.make_async_copy(some, some, sem).wait()

    def to_all(src, dst, k):
        for mx, my in order_of_peers:
            pltpu.make_async_remote_copy(
                src_ref=src, dst_ref=dst.at[me], send_sem=direct_send.at[k],
                recv_sem=direct_recv.at[k], device_id=(peers_x[mx], peers_y[my]),
                device_id_type=pl.DeviceIdType.MESH,
            ).start()

    def halo_copies(k):
        now = field.at[k]
        out = (
            (now.at[0], down.at[k], 1),
            (now.at[rows - 1], up.at[k], 0),
            (now.at[:, 0], right.at[k], 3),
            (now.at[:, cols - 1], left.at[k], 2),
        )
        return [
            pltpu.make_async_remote_copy(
                src_ref=src, dst_ref=dst,
                send_sem=halo_send.at[k, side], recv_sem=halo_recv.at[k, lands],
                device_id=peer, device_id_type=pl.DeviceIdType.MESH,
            )
            for side, ((src, dst, lands), (_, peer)) in enumerate(zip(out, sides))
        ]

    def halo_start(k):
        for (here, _), copy in zip(sides, halo_copies(k)):
            pl.when(here)(copy.start)

    def halo_wait(k, side):
        buf = halos[side].at[k]
        pl.when(sides[side][0])(pltpu.make_async_copy(buf, buf, halo_recv.at[k, side]).wait)

    def to_sides(src, dst, send, recv):
        return [
            pltpu.make_async_remote_copy(
                src_ref=src, dst_ref=dst.at[lands],
                send_sem=send.at[side], recv_sem=recv.at[lands],
                device_id=peer, device_id_type=pl.DeviceIdType.MESH,
            )
            for side, (lands, (_, peer)) in enumerate(zip((1, 0, 3, 2), sides))
        ]

    def near_copies():
        return to_sides(nulls, near, near_send, near_recv)

    def relaxed_copies():
        return to_sides(relaxed, relaxed_near, relaxed_send, relaxed_recv)

    def from_sides(dst, recv):
        for side, (here, _) in enumerate(sides):
            buf = dst.at[side]
            pl.when(here)(pltpu.make_async_copy(buf, buf, recv.at[side]).wait)

    loads[0].wait()
    for i in range(rows):
        for j in range(cols):
            p = i * cols + j
            for c in range(0, blk * blk, 128):
                blocks[p, 0, c // 128 : c // 128 + 1] = s_ref[j, i : i + 1, c : c + 128]
            flat = blocks[p, 0, 0 : blk * blk // 128]
            for half in range(128 // blk):
                blocks[p, 1, pl.ds(half, blk * blk // 128, stride=128 // blk), 0:blk] = flat[
                    :, half * blk : (half + 1) * blk
                ]
    for p in range(count):
        hi, lo = cut(relax_weight * blocks[p, 1, :, 0:blk])
        smoother[p] = jnp.concatenate([hi, hi, lo], axis=1)

    def smooth(v):
        return jnp.concatenate(
            [mm(smoother[p], stacked(v[p * blk : (p + 1) * blk])) for p in range(count)], axis=0
        )

    def put(v, k):
        field[k] = v.reshape(rows, cols, blk, cases)

    loads[1].wait()
    b = b_ref[...].reshape(size, cases)
    first = smooth(b)
    put(first, 0)

    for load in loads[2:5]:
        load.wait()
    for i in range(rows):
        for j in range(cols):
            p = i * cols + j
            for k in range(modes):
                nulls[k : k + 1, p * blk : (p + 1) * blk] = n_ref[
                    j, i : i + 1, k * blk : (k + 1) * blk
                ]
    info[0:modes, 0 : inv_ref.shape[1]] = inv_ref[...]
    info[modes : modes + 1, :] = jnp.full((1, width), map_ref[0, 0].astype(jnp.float32))

    pl.semaphore_wait(barrier, len(lines))
    for (here, _), copy in zip(sides, near_copies()):
        pl.when(here)(copy.start)
    for copy in at_column(told, told_all):
        copy.start()
    halo_start(0)
    for mx in range(1, nx):
        pl.semaphore_signal(
            entered, inc=1, device_id=(peers_x[mx], y), device_id_type=pl.DeviceIdType.MESH
        )
    pass_on(told, told_all, me)
    info_all[pl.ds(me, 1)] = info[...][None]

    loads[5].wait()
    loads[6].wait()
    for i in range(rows):
        for j in range(cols):
            p = i * cols + j
            tiles = [a_ref[i, j, :, s * blk : (s + 1) * blk] for s in range(5)]
            names = [cols_ref[j, i, s] for s in range(5)]
            for d, (di, dj) in enumerate(((0, 0), (-1, 0), (1, 0), (0, -1), (0, 1))):
                e = (i + 1 + di) * (cols + 2) + j + 1 + dj
                tile = tiles[0] * (names[0] == e).astype(jnp.float32)
                for s in range(1, 5):
                    tile = tile + tiles[s] * (names[s] == e).astype(jnp.float32)
                hi, lo = cut(tile)
                ii, jj = i + di, j + dj
                if 0 <= ii < rows and 0 <= jj < cols:
                    q = ii * cols + jj
                    for k, part in enumerate((hi, hi, lo)):
                        at = k * size + q * blk
                        local[p * blk : (p + 1) * blk, at : at + blk] = part
                else:
                    at = (0, j, cols + j, 2 * cols + i, 2 * cols + rows + i)[d]
                    edge[at] = jnp.concatenate([hi, hi, lo], axis=1)

    def places():
        for j in range(cols):
            yield 0, j, j, j
        for j in range(cols):
            yield 1, j, cols + j, (rows - 1) * cols + j
        for i in range(rows):
            yield 2, i, 2 * cols + i, i * cols
        for i in range(rows):
            yield 3, i, 2 * cols + rows + i, i * cols + cols - 1

    def operate(v, k):
        inner = mm(local[...], stacked(v))
        parts = [inner[p * blk : (p + 1) * blk] for p in range(count)]
        for side in (2, 3, 0, 1):
            halo_wait(k, side)
            for at_side, at, e, p in places():
                if at_side == side:
                    parts[p] = parts[p] + mm(edge[e], stacked(halos[side][k, at]))
        return jnp.concatenate(parts, axis=0)

    own_n = nulls[...]
    own_hi, own_lo = cut(own_n)
    own_cat = jnp.concatenate([own_hi, own_hi, own_lo], axis=1)

    def mine(k):
        return coarse.at[k, 0:modes]

    def theirs_all(k):
        return coarse_all.at[k, :, 0:modes]

    def restrict(v, k):
        g = mm(own_cat, stacked(v))
        coarse[k] = g
        to_all(mine(k), theirs_all(k), k)
        coarse_all[k, pl.ds(me, 1)] = g[None]

    def gathered(k):
        wait_many(theirs_all(k), n - 1, direct_recv.at[k])
        return coarse_all[k].reshape(coarse_rows, cases)

    def across(v):
        hi, lo = cut(v)
        return jnp.concatenate([hi, lo, hi], axis=1)

    facing = (
        lambda at: (rows - 1) * cols + at,
        lambda at: at,
        lambda at: at * cols + cols - 1,
        lambda at: at * cols,
    )
    spread[0:8] = mm_t(across(own_n), local[...])
    from_sides(near, near_recv)
    for side, at, e, p in places():
        q = facing[side](at)
        spread[8 * (1 + side) : 8 * (2 + side), p * blk : (p + 1) * blk] = mm_t(
            across(near[side, :, q * blk : (q + 1) * blk]), edge[e]
        )
    for p in range(count):
        relaxed[:, p * blk : (p + 1) * blk] = mm_t(
            across(spread[:, p * blk : (p + 1) * blk]), smoother[p]
        )
    for (here, _), copy in zip(sides, relaxed_copies()):
        pl.when(here)(copy.start)
    told_pass()

    r = b - operate(first, 0)
    pl.semaphore_wait(entered, nx - 1)
    restrict(r, 0)
    t = smooth(r)
    put(t, 1)
    halo_start(1)

    reach[0:around] = spread[...] - mm_t(across(relaxed[...]), local[...])
    eye = (
        lax.broadcasted_iota(jnp.int32, (size, size), 0)
        == lax.broadcasted_iota(jnp.int32, (size, size), 1)
    ).astype(jnp.float32).astype(jnp.bfloat16)

    def turned(v):
        return tuple(mm_t(eye, part).astype(jnp.bfloat16) for part in cut(v))

    gain = turned(
        jnp.concatenate([own_n - relaxed[0:8], 0.0 - relaxed[8:around]], axis=0)
    )
    q1 = r - operate(t, 1)

    wait_many(told_all, (nx - 1) * ny, all_recv)
    inv_parts = cut(info_all[...].reshape(coarse_rows, width))
    lane3 = lax.broadcasted_iota(jnp.int32, (n, 8, width), 2).astype(jnp.float32)
    row3 = lax.broadcasted_iota(jnp.int32, (n, 8, width), 1)
    labels = jnp.broadcast_to(info_all[...][:, modes : modes + 1, :], (n, 8, width))
    where3 = labels * float(modes) + row3.astype(jnp.float32)
    order = jnp.where(lane3 == where3, 1.0, 0.0)
    order = jnp.where(row3 < modes, order, 0.0).reshape(coarse_rows, width).astype(jnp.bfloat16)
    lane4 = lax.broadcasted_iota(jnp.int32, (n, 8, coarse_rows), 2).astype(jnp.float32)
    row4 = lax.broadcasted_iota(jnp.int32, (n, 8, coarse_rows), 1)
    labels4 = jnp.broadcast_to(info_all[...][:, modes : modes + 1, 0:1], (n, 8, coarse_rows))
    pick = jnp.where(lane4 == labels4 * 8.0 + row4.astype(jnp.float32), 1.0, 0.0)
    pick = jnp.where(row4 < modes, pick, 0.0).reshape(coarse_rows, coarse_rows).astype(jnp.bfloat16)
    for k, part in enumerate(inv_parts):
        solved[k] = mm_t(mm(pick, part).astype(jnp.bfloat16), order)

    def clipped(px, py):
        return jnp.clip(px, 0, nx - 1) * ny + jnp.clip(py, 0, ny - 1)

    def cross(px, py):
        return [
            clipped(px + dx, py + dy)
            for dx, dy in ((0, 0), (-1, 0), (1, 0), (0, -1), (0, 1))
        ]

    ids = cross(x, y)
    for _, (px, py) in sides:
        ids = ids + cross(px, py)
    lacking = jnp.zeros((reach.shape[0] - 8 * len(ids), coarse_rows), jnp.float32)
    solve = tuple(
        jnp.concatenate(
            [solved[k, pl.ds(pl.multiple_of(d * 8, 8), 8)] for d in ids] + [lacking], axis=0
        ).astype(jnp.bfloat16)
        for k in range(2)
    )

    def mm3_cut(a_cut, b_cut):
        return mm(a_cut[0], b_cut[0]) + (mm(a_cut[0], b_cut[1]) + mm(a_cut[1], b_cut[0]))

    gain_cut = cut(mm3_cut(gain, tuple(part[0:around] for part in solve)))

    from_sides(relaxed_near, relaxed_recv)
    for side, at, e, p in places():
        q = facing[side](at)
        reach[around * (1 + side) : around * (2 + side), p * blk : (p + 1) * blk] = 0.0 - mm_t(
            across(relaxed_near[side, :, q * blk : (q + 1) * blk]), edge[e]
        )
    loss_cut = cut(mm3_cut(turned(reach[...]), solve))

    g = gathered(0)
    r = q1 - mm3(loss_cut, g)
    s = smooth(r)
    put(s, 2)
    halo_start(2)
    precond = first + t + mm3(gain_cut, g) + s
    r = r - operate(s, 2)
    restrict(r, 1)
    t = smooth(r)
    put(t, 3)
    halo_start(3)
    precond = precond + t
    q2 = r - operate(t, 3)
    base = b - q2
    g = gathered(1)
    precond = precond + mm3(gain_cut, g)
    image = base + mm3(loss_cut, g)
    sums[...] = jnp.concatenate(
        [
            jnp.sum(b * precond, axis=0, keepdims=True),
            jnp.sum(precond * image, axis=0, keepdims=True),
            jnp.zeros((6, cases), jnp.float32),
        ],
        axis=0,
    )
    pairs = sums_all.at[:, 0:2]
    to_all(sums.at[0:2], pairs, 2)
    sums_all[pl.ds(me, 1)] = sums[...][None]
    leaving[0] = precond.reshape(rows, cols, blk, cases)
    leaving[1] = image.reshape(rows, cols, blk, cases)
    leaves = [
        pltpu.make_async_copy(leaving.at[k], dst, left_sem.at[k])
        for k, dst in enumerate((precond_hbm, image_hbm))
    ]
    for leave in leaves:
        leave.start()

    for k in range(4):
        for (here, _), copy in zip(sides, halo_copies(k)):
            pl.when(here)(copy.wait_send)
    for (here, _), copy in zip(sides, near_copies()):
        pl.when(here)(copy.wait_send)
    for (here, _), copy in zip(sides, relaxed_copies()):
        pl.when(here)(copy.wait_send)
    for copy in at_column(told, told_all):
        copy.wait_send()
    wait_many(told_all, (nx - 1) * ny, all_send)
    for k in range(2):
        wait_many(theirs_all(k), n - 1, direct_send.at[k])
    for leave in leaves:
        leave.wait()

    wait_many(pairs, n - 1, direct_recv.at[2])
    total = jnp.sum(sums_all[:, 0:2], axis=0)
    alpha_ref[...] = total[0:1] / total[1:2]
    wait_many(pairs, n - 1, direct_send.at[2])


def finish_kernel(b_ref, p_ref, i_ref, alpha_ref, sol_ref, res_ref, held, scale, sems, scale_sem):
    rows = b_ref.shape[0]
    first = pltpu.make_async_copy(alpha_ref, scale, scale_sem)
    first.start()

    def move(k, i):
        ref = (p_ref, i_ref, b_ref, sol_ref, res_ref)[k]
        ends = (ref.at[i], held.at[k, i])
        return pltpu.make_async_copy(*(ends if k < 3 else ends[::-1]), sems.at[k, i])

    for i in range(rows):
        for k in range(3):
            move(k, i).start()
    first.wait()
    alpha = scale[...].reshape(1, 1, -1)
    for i in range(rows):
        move(0, i).wait()
        held[3, i] = alpha * held[0, i]
        move(3, i).start()
        move(1, i).wait()
        move(2, i).wait()
        held[4, i] = held[2, i] - alpha * held[1, i]
        move(4, i).start()
    for i in range(rows):
        move(3, i).wait()
        move(4, i).wait()


def fused(
    nx, ny,
    load_cases, matrix_tiles, block_cols, smoother_blocks, near_null, coarse_map, coarse_inverse
):
    rows, cols, blk, cases = load_cases.shape
    count = rows * cols
    modes = near_null.shape[2] // blk
    n = nx * ny
    width = -(-coarse_inverse.shape[1] // 128) * 128
    block_cols = jnp.transpose(block_cols, (1, 0, 2))
    smoother_blocks = jnp.transpose(smoother_blocks, (1, 0, 2))
    near_null = jnp.transpose(near_null, (1, 0, 2))
    vmem = pl.BlockSpec(memory_space=pltpu.VMEM)
    hbm = pl.BlockSpec(memory_space=pltpu.HBM)
    f32, bf16 = jnp.float32, jnp.bfloat16
    shape = jax.ShapeDtypeStruct(load_cases.shape, f32)
    precond, image, alpha = pl.pallas_call(
        functools.partial(step_kernel, nx, ny, modes),
        out_shape=(shape, shape, jax.ShapeDtypeStruct((1, cases), f32)),
        in_specs=[hbm] * 7,
        out_specs=(hbm, hbm, vmem),
        scratch_shapes=[
            pltpu.VMEM(load_cases.shape, f32),
            pltpu.VMEM(matrix_tiles.shape, f32),
            pltpu.SMEM(block_cols.shape, jnp.int32),
            pltpu.VMEM(smoother_blocks.shape, f32),
            pltpu.VMEM(near_null.shape, f32),
            pltpu.SMEM(coarse_map.shape, jnp.int32),
            pltpu.VMEM(coarse_inverse.shape, f32),
            pltpu.SemaphoreType.DMA((7,)),
            pltpu.VMEM((count, 2, blk, 128), f32),
            pltpu.VMEM((8, count * blk), f32),
            pltpu.VMEM((4, rows, cols, blk, cases), f32),
            pltpu.VMEM((4, cols, blk, cases), f32),
            pltpu.VMEM((4, cols, blk, cases), f32),
            pltpu.VMEM((4, rows, blk, cases), f32),
            pltpu.VMEM((4, rows, blk, cases), f32),
            pltpu.VMEM((count * blk, 3 * count * blk), bf16),
            pltpu.VMEM((2 * (rows + cols), blk, 3 * blk), bf16),
            pltpu.VMEM((count, blk, 3 * blk), bf16),
            pltpu.VMEM((8, width), f32),
            pltpu.VMEM((n, 8, width), f32),
            pltpu.VMEM((4, 8, count * blk), f32),
            pltpu.VMEM((2, 8, cases), f32),
            pltpu.VMEM((2, n, 8, cases), f32),
            pltpu.VMEM((8, cases), f32),
            pltpu.VMEM((n, 8, cases), f32),
            pltpu.VMEM((40, count * blk), f32),
            pltpu.VMEM((40, count * blk), f32),
            pltpu.VMEM((4, 40, count * blk), f32),
            pltpu.VMEM((256, count * blk), f32),
            pltpu.VMEM((2, n * 8, n * 8), f32),
            pltpu.VMEM((2,) + load_cases.shape, f32),
            pltpu.SemaphoreType.DMA((4, 4)),
            pltpu.SemaphoreType.DMA((4, 4)),
            pltpu.SemaphoreType.DMA((4,)),
            pltpu.SemaphoreType.DMA((4,)),
            pltpu.SemaphoreType.DMA((4,)),
            pltpu.SemaphoreType.DMA((4,)),
            pltpu.SemaphoreType.DMA((ny,)),
            pltpu.SemaphoreType.DMA((ny,)),
            pltpu.SemaphoreType.DMA,
            pltpu.SemaphoreType.DMA,
            pltpu.SemaphoreType.DMA((3,)),
            pltpu.SemaphoreType.DMA((3,)),
            pltpu.SemaphoreType.DMA((2,)),
            pltpu.SemaphoreType.REGULAR,
        ],
        compiler_params=pltpu.CompilerParams(
            collective_id=0, has_side_effects=True, vmem_limit_bytes=60 * 2**20
        ),
    )(
        load_cases, matrix_tiles, block_cols, smoother_blocks, near_null, coarse_map,
        coarse_inverse,
    )
    return pl.pallas_call(
        finish_kernel,
        out_shape=(shape, shape),
        in_specs=[hbm, hbm, hbm, hbm],
        out_specs=(hbm, hbm),
        scratch_shapes=[
            pltpu.VMEM((5,) + load_cases.shape, f32),
            pltpu.VMEM((1, cases), f32),
            pltpu.SemaphoreType.DMA((5, rows)),
            pltpu.SemaphoreType.DMA,
        ],
        compiler_params=pltpu.CompilerParams(vmem_limit_bytes=60 * 2**20),
    )(load_cases, precond, image, alpha)


def per_device(
    load_cases, matrix_tiles, block_cols, smoother_blocks, near_null, coarse_map, coarse_inverse
):
    agg_rows, agg_cols, block_size, case_count = load_cases.shape
    mode_count = near_null.shape[2] // block_size
    coarse_total = coarse_inverse.shape[1]
    coarse_aggs = coarse_total // mode_count
    modes = near_null.reshape(agg_rows, agg_cols, mode_count, block_size)
    inverse_blocks = smoother_blocks.reshape(agg_rows, agg_cols, block_size, block_size)

    steps = ((0, 0), (-1, 0), (1, 0), (0, -1), (0, 1))
    tiles = matrix_tiles.reshape(agg_rows, agg_cols, block_size, -1, block_size)
    row_at = jnp.arange(agg_rows, dtype=jnp.int32)[:, None, None]
    col_at = jnp.arange(agg_cols, dtype=jnp.int32)[None, :, None]
    stencil = []
    for dx, dy in steps:
        named = block_cols == (row_at + 1 + dx) * (agg_cols + 2) + col_at + 1 + dy
        stencil.append(jnp.sum(jnp.where(named[:, :, None, :, None], tiles, 0.0), axis=3))

    def operate(vector_field):
        extended = padded(vector_field, (("gx", 0), ("gy", 1)), 1)
        total = 0.0
        for tile, (dx, dy) in zip(stencil, steps):
            cells = extended[1 + dx : 1 + dx + agg_rows, 1 + dy : 1 + dy + agg_cols]
            total = total + jnp.einsum("ijbk,ijkr->ijbr", tile, cells, precision=highest)
        return total

    def smooth(defect):
        return relax_weight * jnp.einsum(
            "ijab,ijbr->ijar", inverse_blocks, defect, precision=highest
        )

    def correct(defect):
        contrib = jnp.einsum("ijkb,ijbr->ijkr", modes, defect, precision=highest)
        own_part = jnp.sum(contrib, axis=(0, 1))
        my_label = coarse_map[0, 0]
        label_value = jnp.reshape(my_label.astype(jnp.float32), (1,))
        pieces, labels = (
            lax.all_gather(own_part[None], ("gx", "gy"), axis=0, tiled=True),
            lax.all_gather(label_value, ("gx", "gy"), axis=0, tiled=True),
        )
        label_ids = labels.astype(jnp.int32)
        placing = (label_ids[:, None] == jnp.arange(coarse_aggs, dtype=jnp.int32)[None, :]).astype(
            jnp.float32
        )
        ordered = jnp.einsum("dc,dkr->ckr", placing, pieces, precision=highest).reshape(
            coarse_total, case_count
        )
        own_rows = jnp.dot(coarse_inverse, ordered, precision=highest)
        solved = lax.all_gather(own_rows, ("gx", "gy"), axis=0, tiled=True)
        mine = lax.dynamic_slice_in_dim(solved, my_label * mode_count, mode_count, 0)
        coarse_back = jnp.broadcast_to(
            mine[None, None], (agg_rows, agg_cols, mode_count, case_count)
        )
        return jnp.einsum("ijkb,ijkr->ijbr", modes, coarse_back, precision=highest)

    first = smooth(load_cases)
    first = first + correct(load_cases - operate(first))
    precond = first + smooth(load_cases - operate(first))
    defect = load_cases - operate(precond)
    update = smooth(defect)
    update = update + correct(defect - operate(update))
    update = update + smooth(defect - operate(update))
    precond = precond + update
    local_aligned = jnp.sum(load_cases * precond, axis=(0, 1, 2))
    aligned = lax.psum(local_aligned, ("gx", "gy"))
    image = operate(precond)
    curved = lax.psum(jnp.sum(precond * image, axis=(0, 1, 2)), ("gx", "gy"))
    alpha = aligned / curved
    solution = alpha * precond
    residual = load_cases - alpha * image
    return (solution, residual)


def solution(mesh):
    nx, ny = mesh.shape["gx"], mesh.shape["gy"]
    step = functools.partial(fused, nx, ny) if nx * ny <= 128 else per_device
    placed = (
        P("gx", "gy", None, None),
        P("gx", "gy", None, None),
        P("gx", "gy", None),
        P("gx", "gy", None),
        P("gx", "gy", None),
        P("gx", "gy"),
        P(("gx", "gy"), None),
    )
    return jax.shard_map(
        step,
        mesh=mesh,
        in_specs=placed,
        out_specs=(P("gx", "gy", None, None), P("gx", "gy", None, None)),
        check_vma=False,
    )
```

```python
import functools

import jax
import jax.numpy as jnp
from jax import lax
from jax.experimental import pallas as pl
from jax.experimental.pallas import tpu as pltpu
from jax.sharding import PartitionSpec as P

relax_weight = 0.8
highest = lax.Precision.HIGHEST


def padded(cells, sides, width):
    for axis, dim in sides:
        count = lax.axis_size(axis)
        ends = count - 1
        head = lax.slice_in_dim(cells, 0, width, axis=dim)
        tail = lax.slice_in_dim(cells, cells.shape[dim] - width, cells.shape[dim], axis=dim)
        cells = jnp.concatenate(
            [
                lax.ppermute(tail, axis, [(i, (i + 1) % count) for i in range(ends)]),
                cells,
                lax.ppermute(head, axis, [((i + 1) % count, i) for i in range(ends)]),
            ],
            axis=dim,
        )
    return cells


def cut(v):
    hi = v.astype(jnp.bfloat16)
    return hi, (v - hi.astype(jnp.float32)).astype(jnp.bfloat16)


def stacked(v):
    hi, lo = cut(v)
    return jnp.concatenate([hi, lo, hi], axis=0)


def mm(a, b):
    return lax.dot_general(a, b, (((1,), (0,)), ((), ())), preferred_element_type=jnp.float32)


def mm_t(a, b, precision=None):
    return lax.dot_general(
        a, b, (((1,), (1,)), ((), ())), precision=precision, preferred_element_type=jnp.float32
    )


def mm3(a_cut, b):
    hi, lo = cut(b)
    return mm(a_cut[0], hi) + (mm(a_cut[0], lo) + mm(a_cut[1], hi))


def flipped(v, mask):
    bit = 1
    while bit <= mask:
        if mask & bit:
            v = v + bit - 2 * bit * lax.rem(v // bit, 2)
        bit *= 2
    return v


def far_first(nx, ny):
    def hops(pair):
        mx, my = pair
        return bin(mx >> 1).count("1") + my + 0.1 * (mx & 1)

    pairs = [(mx, my) for mx in range(nx) for my in range(ny) if mx or my]
    return sorted(pairs, key=hops, reverse=True)


def step_kernel(
    nx, ny, modes,
    b_hbm, a_hbm, cols_hbm, s_hbm, n_hbm, map_hbm, inv_hbm,
    precond_hbm, image_hbm, alpha_ref,
    b_ref, a_ref, cols_ref, s_ref, n_ref, map_ref, inv_ref, loaded,
    blocks, nulls, field, up, down, left, right, local, edge, smoother, info, info_all, near, coarse, coarse_all,
    sums, sums_all, spread, relaxed, relaxed_near, reach, solved, leaving,
    halo_send, halo_recv, near_send, near_recv, relaxed_send, relaxed_recv, col_send, col_recv,
    all_send, all_recv, direct_send, direct_recv, left_sem, entered,
):
    rows, cols, blk, cases = b_ref.shape
    count = rows * cols
    size = count * blk
    n = nx * ny
    width = info.shape[1]
    coarse_rows = n * 8
    around = spread.shape[0]
    x, y = lax.axis_index("gx"), lax.axis_index("gy")
    me = x * ny + y
    sides = (
        (x > 0, (x - 1, y)),
        (x < nx - 1, (x + 1, y)),
        (y > 0, (x, y - 1)),
        (y < ny - 1, (x, y + 1)),
    )
    halos = (up, down, left, right)
    order_of_peers = far_first(nx, ny)
    peers_x = [flipped(x, m) for m in range(nx)]
    peers_y = [flipped(y, m) for m in range(ny)]
    barrier = pltpu.get_barrier_semaphore()

    loads = [
        pltpu.make_async_copy(src, dst, loaded.at[i])
        for i, (src, dst) in enumerate(
            (
                (s_hbm, s_ref), (b_hbm, b_ref), (n_hbm, n_ref), (inv_hbm, inv_ref),
                (map_hbm, map_ref), (cols_hbm, cols_ref), (a_hbm, a_ref),
            )
        )
    ]
    for load in loads:
        load.start()

    coarse_all[...] = jnp.zeros_like(coarse_all)
    info_all[...] = jnp.zeros_like(info_all)

    lines = [pair for pair in order_of_peers if 0 in pair]
    for mx, my in lines:
        pl.semaphore_signal(
            barrier, inc=1, device_id=(peers_x[mx], peers_y[my]),
            device_id_type=pl.DeviceIdType.MESH,
        )

    spread[...] = jnp.zeros_like(spread)
    reach[...] = jnp.zeros_like(reach)
    nulls[...] = jnp.zeros_like(nulls)
    info[...] = jnp.zeros_like(info)
    local[...] = jnp.zeros_like(local)
    for side, (here, _) in enumerate(sides):

        @pl.when(jnp.logical_not(here))
        def _():
            halos[side][...] = jnp.zeros_like(halos[side])
            near[side] = jnp.zeros_like(near[side])
            relaxed_near[side] = jnp.zeros_like(relaxed_near[side])

    told, told_all = info.at[0 : modes + 1], info_all.at[:, 0 : modes + 1]

    def at_column(src, dst):
        return [
            pltpu.make_async_remote_copy(
                src_ref=src, dst_ref=dst.at[me], send_sem=col_send.at[j],
                recv_sem=col_recv.at[ny - j],
                device_id=(x, lax.rem(y + j, ny)), device_id_type=pl.DeviceIdType.MESH,
            )
            for j in range(1, ny)
        ]

    def pass_on(src, dst, slot):
        for mx in range(nx - 1, 0, -1):
            pltpu.make_async_remote_copy(
                src_ref=src, dst_ref=dst.at[slot], send_sem=all_send, recv_sem=all_recv,
                device_id=(peers_x[mx], y), device_id_type=pl.DeviceIdType.MESH,
            ).start()

    def told_pass():
        for j in list(range(1, ny, 2)) + list(range(2, ny, 2)):
            slot = x * ny + lax.rem(y + j, ny)
            pltpu.make_async_copy(told, told, col_recv.at[j]).wait()
            pass_on(told_all.at[slot], told_all, slot)

    def wait_many(dst, tiles, sem):
        some = dst.at[pl.ds(0, tiles)]
        pltpu.make_async_copy(some, some, sem).wait()

    def to_all(src, dst, k):
        for mx, my in order_of_peers:
            pltpu.make_async_remote_copy(
                src_ref=src, dst_ref=dst.at[me], send_sem=direct_send.at[k],
                recv_sem=direct_recv.at[k], device_id=(peers_x[mx], peers_y[my]),
                device_id_type=pl.DeviceIdType.MESH,
            ).start()

    def halo_copies(k):
        now = field.at[k]
        out = (
            (now.at[0], down.at[k], 1),
            (now.at[rows - 1], up.at[k], 0),
            (now.at[:, 0], right.at[k], 3),
            (now.at[:, cols - 1], left.at[k], 2),
        )
        return [
            pltpu.make_async_remote_copy(
                src_ref=src, dst_ref=dst,
                send_sem=halo_send.at[k, side], recv_sem=halo_recv.at[k, lands],
                device_id=peer, device_id_type=pl.DeviceIdType.MESH,
            )
            for side, ((src, dst, lands), (_, peer)) in enumerate(zip(out, sides))
        ]

    def halo_start(k):
        for (here, _), copy in zip(sides, halo_copies(k)):
            pl.when(here)(copy.start)

    def halo_wait(k, side):
        buf = halos[side].at[k]
        pl.when(sides[side][0])(pltpu.make_async_copy(buf, buf, halo_recv.at[k, side]).wait)

    def to_sides(src, dst, send, recv):
        return [
            pltpu.make_async_remote_copy(
                src_ref=src, dst_ref=dst.at[lands],
                send_sem=send.at[side], recv_sem=recv.at[lands],
                device_id=peer, device_id_type=pl.DeviceIdType.MESH,
            )
            for side, (lands, (_, peer)) in enumerate(zip((1, 0, 3, 2), sides))
        ]

    def near_copies():
        return to_sides(nulls, near, near_send, near_recv)

    def relaxed_copies():
        return to_sides(relaxed, relaxed_near, relaxed_send, relaxed_recv)

    def from_sides(dst, recv):
        for side, (here, _) in enumerate(sides):
            buf = dst.at[side]
            pl.when(here)(pltpu.make_async_copy(buf, buf, recv.at[side]).wait)

    loads[0].wait()
    for i in range(rows):
        for j in range(cols):
            p = i * cols + j
            for c in range(0, blk * blk, 128):
                blocks[p, 0, c // 128 : c // 128 + 1] = s_ref[j, i : i + 1, c : c + 128]
            flat = blocks[p, 0, 0 : blk * blk // 128]
            for half in range(128 // blk):
                blocks[p, 1, pl.ds(half, blk * blk // 128, stride=128 // blk), 0:blk] = flat[
                    :, half * blk : (half + 1) * blk
                ]
    for p in range(count):
        hi, lo = cut(relax_weight * blocks[p, 1, :, 0:blk])
        smoother[p] = jnp.concatenate([hi, hi, lo], axis=1)

    def smooth(v):
        return jnp.concatenate(
            [mm(smoother[p], stacked(v[p * blk : (p + 1) * blk])) for p in range(count)], axis=0
        )

    def put(v, k):
        field[k] = v.reshape(rows, cols, blk, cases)

    loads[1].wait()
    b = b_ref[...].reshape(size, cases)
    first = smooth(b)
    put(first, 0)

    for load in loads[2:5]:
        load.wait()
    for i in range(rows):
        for j in range(cols):
            p = i * cols + j
            for k in range(modes):
                nulls[k : k + 1, p * blk : (p + 1) * blk] = n_ref[
                    j, i : i + 1, k * blk : (k + 1) * blk
                ]
    info[0:modes, 0 : inv_ref.shape[1]] = inv_ref[...]
    info[modes : modes + 1, :] = jnp.full((1, width), map_ref[0, 0].astype(jnp.float32))

    pl.semaphore_wait(barrier, len(lines))
    for (here, _), copy in zip(sides, near_copies()):
        pl.when(here)(copy.start)
    for copy in at_column(told, told_all):
        copy.start()
    halo_start(0)
    for mx in range(1, nx):
        pl.semaphore_signal(
            entered, inc=1, device_id=(peers_x[mx], y), device_id_type=pl.DeviceIdType.MESH
        )
    pass_on(told, told_all, me)
    info_all[pl.ds(me, 1)] = info[...][None]

    loads[5].wait()
    loads[6].wait()
    for i in range(rows):
        for j in range(cols):
            p = i * cols + j
            tiles = [a_ref[i, j, :, s * blk : (s + 1) * blk] for s in range(5)]
            names = [cols_ref[j, i, s] for s in range(5)]
            for d, (di, dj) in enumerate(((0, 0), (-1, 0), (1, 0), (0, -1), (0, 1))):
                e = (i + 1 + di) * (cols + 2) + j + 1 + dj
                tile = tiles[0] * (names[0] == e).astype(jnp.float32)
                for s in range(1, 5):
                    tile = tile + tiles[s] * (names[s] == e).astype(jnp.float32)
                hi, lo = cut(tile)
                ii, jj = i + di, j + dj
                if 0 <= ii < rows and 0 <= jj < cols:
                    q = ii * cols + jj
                    for k, part in enumerate((hi, hi, lo)):
                        at = k * size + q * blk
                        local[p * blk : (p + 1) * blk, at : at + blk] = part
                else:
                    at = (0, j, cols + j, 2 * cols + i, 2 * cols + rows + i)[d]
                    edge[at] = jnp.concatenate([hi, hi, lo], axis=1)

    def places():
        for j in range(cols):
            yield 0, j, j, j
        for j in range(cols):
            yield 1, j, cols + j, (rows - 1) * cols + j
        for i in range(rows):
            yield 2, i, 2 * cols + i, i * cols
        for i in range(rows):
            yield 3, i, 2 * cols + rows + i, i * cols + cols - 1

    def operate(v, k):
        inner = mm(local[...], stacked(v))
        parts = [inner[p * blk : (p + 1) * blk] for p in range(count)]
        for side in (2, 3, 0, 1):
            halo_wait(k, side)
            for at_side, at, e, p in places():
                if at_side == side:
                    parts[p] = parts[p] + mm(edge[e], stacked(halos[side][k, at]))
        return jnp.concatenate(parts, axis=0)

    own_n = nulls[...]
    own_hi, own_lo = cut(own_n)
    own_cat = jnp.concatenate([own_hi, own_hi, own_lo], axis=1)

    def mine(k):
        return coarse.at[k, 0:modes]

    def theirs_all(k):
        return coarse_all.at[k, :, 0:modes]

    def restrict(v, k):
        g = mm(own_cat, stacked(v))
        coarse[k] = g
        to_all(mine(k), theirs_all(k), k)
        coarse_all[k, pl.ds(me, 1)] = g[None]

    def gathered(k):
        wait_many(theirs_all(k), n - 1, direct_recv.at[k])
        return coarse_all[k].reshape(coarse_rows, cases)

    def across(v):
        hi, lo = cut(v)
        return jnp.concatenate([hi, lo, hi], axis=1)

    facing = (
        lambda at: (rows - 1) * cols + at,
        lambda at: at,
        lambda at: at * cols + cols - 1,
        lambda at: at * cols,
    )
    spread[0:8] = mm_t(across(own_n), local[...])
    from_sides(near, near_recv)
    for side, at, e, p in places():
        q = facing[side](at)
        spread[8 * (1 + side) : 8 * (2 + side), p * blk : (p + 1) * blk] = mm_t(
            across(near[side, :, q * blk : (q + 1) * blk]), edge[e]
        )
    for p in range(count):
        relaxed[:, p * blk : (p + 1) * blk] = mm_t(
            across(spread[:, p * blk : (p + 1) * blk]), smoother[p]
        )
    for (here, _), copy in zip(sides, relaxed_copies()):
        pl.when(here)(copy.start)
    told_pass()

    r = b - operate(first, 0)
    pl.semaphore_wait(entered, nx - 1)
    restrict(r, 0)
    t = smooth(r)
    put(t, 1)
    halo_start(1)

    reach[0:around] = spread[...] - mm_t(across(relaxed[...]), local[...])
    eye = (
        lax.broadcasted_iota(jnp.int32, (size, size), 0)
        == lax.broadcasted_iota(jnp.int32, (size, size), 1)
    ).astype(jnp.float32).astype(jnp.bfloat16)

    def turned(v):
        return tuple(mm_t(eye, part).astype(jnp.bfloat16) for part in cut(v))

    gain = turned(
        jnp.concatenate([own_n - relaxed[0:8], 0.0 - relaxed[8:around]], axis=0)
    )
    wait_many(told_all, (nx - 1) * ny, all_recv)
    inv_parts = cut(info_all[...].reshape(coarse_rows, width))
    lane3 = lax.broadcasted_iota(jnp.int32, (n, 8, width), 2).astype(jnp.float32)
    row3 = lax.broadcasted_iota(jnp.int32, (n, 8, width), 1)
    labels = jnp.broadcast_to(info_all[...][:, modes : modes + 1, :], (n, 8, width))
    where3 = labels * float(modes) + row3.astype(jnp.float32)
    order = jnp.where(lane3 == where3, 1.0, 0.0)
    order = jnp.where(row3 < modes, order, 0.0).reshape(coarse_rows, width).astype(jnp.bfloat16)
    lane4 = lax.broadcasted_iota(jnp.int32, (n, 8, coarse_rows), 2).astype(jnp.float32)
    row4 = lax.broadcasted_iota(jnp.int32, (n, 8, coarse_rows), 1)
    labels4 = jnp.broadcast_to(info_all[...][:, modes : modes + 1, 0:1], (n, 8, coarse_rows))
    pick = jnp.where(lane4 == labels4 * 8.0 + row4.astype(jnp.float32), 1.0, 0.0)
    pick = jnp.where(row4 < modes, pick, 0.0).reshape(coarse_rows, coarse_rows).astype(jnp.bfloat16)
    for k, part in enumerate(inv_parts):
        solved[k] = mm_t(mm(pick, part).astype(jnp.bfloat16), order)

    def clipped(px, py):
        return jnp.clip(px, 0, nx - 1) * ny + jnp.clip(py, 0, ny - 1)

    def cross(px, py):
        return [
            clipped(px + dx, py + dy)
            for dx, dy in ((0, 0), (-1, 0), (1, 0), (0, -1), (0, 1))
        ]

    ids = cross(x, y)
    for _, (px, py) in sides:
        ids = ids + cross(px, py)
    lacking = jnp.zeros((reach.shape[0] - 8 * len(ids), coarse_rows), jnp.float32)
    solve = tuple(
        jnp.concatenate(
            [solved[k, pl.ds(pl.multiple_of(d * 8, 8), 8)] for d in ids] + [lacking], axis=0
        ).astype(jnp.bfloat16)
        for k in range(2)
    )

    def mm3_cut(a_cut, b_cut):
        return mm(a_cut[0], b_cut[0]) + (mm(a_cut[0], b_cut[1]) + mm(a_cut[1], b_cut[0]))

    gain_cut = cut(mm3_cut(gain, tuple(part[0:around] for part in solve)))

    from_sides(relaxed_near, relaxed_recv)
    for side, at, e, p in places():
        q = facing[side](at)
        reach[around * (1 + side) : around * (2 + side), p * blk : (p + 1) * blk] = 0.0 - mm_t(
            across(relaxed_near[side, :, q * blk : (q + 1) * blk]), edge[e]
        )
    loss_cut = cut(mm3_cut(turned(reach[...]), solve))

    q1 = r - operate(t, 1)
    g = gathered(0)
    r = q1 - mm3(loss_cut, g)
    s = smooth(r)
    put(s, 2)
    halo_start(2)
    precond = first + t + mm3(gain_cut, g) + s
    r = r - operate(s, 2)
    restrict(r, 1)
    t = smooth(r)
    put(t, 3)
    halo_start(3)
    precond = precond + t
    q2 = r - operate(t, 3)
    base = b - q2
    g = gathered(1)
    precond = precond + mm3(gain_cut, g)
    image = base + mm3(loss_cut, g)
    sums[...] = jnp.concatenate(
        [
            jnp.sum(b * precond, axis=0, keepdims=True),
            jnp.sum(precond * image, axis=0, keepdims=True),
            jnp.zeros((6, cases), jnp.float32),
        ],
        axis=0,
    )
    pairs = sums_all.at[:, 0:2]
    to_all(sums.at[0:2], pairs, 2)
    sums_all[pl.ds(me, 1)] = sums[...][None]
    leaving[0] = precond.reshape(rows, cols, blk, cases)
    leaving[1] = image.reshape(rows, cols, blk, cases)
    leaves = [
        pltpu.make_async_copy(leaving.at[k], dst, left_sem.at[k])
        for k, dst in enumerate((precond_hbm, image_hbm))
    ]
    for leave in leaves:
        leave.start()

    for k in range(4):
        for (here, _), copy in zip(sides, halo_copies(k)):
            pl.when(here)(copy.wait_send)
    for (here, _), copy in zip(sides, near_copies()):
        pl.when(here)(copy.wait_send)
    for (here, _), copy in zip(sides, relaxed_copies()):
        pl.when(here)(copy.wait_send)
    for copy in at_column(told, told_all):
        copy.wait_send()
    wait_many(told_all, (nx - 1) * ny, all_send)
    for k in range(2):
        wait_many(theirs_all(k), n - 1, direct_send.at[k])
    for leave in leaves:
        leave.wait()

    wait_many(pairs, n - 1, direct_recv.at[2])
    total = jnp.sum(sums_all[:, 0:2], axis=0)
    alpha_ref[...] = total[0:1] / total[1:2]
    wait_many(pairs, n - 1, direct_send.at[2])


def finish_kernel(b_ref, p_ref, i_ref, alpha_ref, sol_ref, res_ref, held, scale, sems, scale_sem):
    rows = b_ref.shape[0]
    first = pltpu.make_async_copy(alpha_ref, scale, scale_sem)
    first.start()

    def move(k, i):
        ref = (p_ref, i_ref, b_ref, sol_ref, res_ref)[k]
        ends = (ref.at[i], held.at[k, i])
        return pltpu.make_async_copy(*(ends if k < 3 else ends[::-1]), sems.at[k, i])

    for i in range(rows):
        for k in range(3):
            move(k, i).start()
    first.wait()
    alpha = scale[...].reshape(1, 1, -1)
    for i in range(rows):
        move(0, i).wait()
        held[3, i] = alpha * held[0, i]
        move(3, i).start()
        move(1, i).wait()
        move(2, i).wait()
        held[4, i] = held[2, i] - alpha * held[1, i]
        move(4, i).start()
    for i in range(rows):
        move(3, i).wait()
        move(4, i).wait()


def fused(
    nx, ny,
    load_cases, matrix_tiles, block_cols, smoother_blocks, near_null, coarse_map, coarse_inverse
):
    rows, cols, blk, cases = load_cases.shape
    count = rows * cols
    modes = near_null.shape[2] // blk
    n = nx * ny
    width = -(-coarse_inverse.shape[1] // 128) * 128
    block_cols = jnp.transpose(block_cols, (1, 0, 2))
    smoother_blocks = jnp.transpose(smoother_blocks, (1, 0, 2))
    near_null = jnp.transpose(near_null, (1, 0, 2))
    vmem = pl.BlockSpec(memory_space=pltpu.VMEM)
    hbm = pl.BlockSpec(memory_space=pltpu.HBM)
    f32, bf16 = jnp.float32, jnp.bfloat16
    shape = jax.ShapeDtypeStruct(load_cases.shape, f32)
    precond, image, alpha = pl.pallas_call(
        functools.partial(step_kernel, nx, ny, modes),
        out_shape=(shape, shape, jax.ShapeDtypeStruct((1, cases), f32)),
        in_specs=[hbm] * 7,
        out_specs=(hbm, hbm, vmem),
        scratch_shapes=[
            pltpu.VMEM(load_cases.shape, f32),
            pltpu.VMEM(matrix_tiles.shape, f32),
            pltpu.SMEM(block_cols.shape, jnp.int32),
            pltpu.VMEM(smoother_blocks.shape, f32),
            pltpu.VMEM(near_null.shape, f32),
            pltpu.SMEM(coarse_map.shape, jnp.int32),
            pltpu.VMEM(coarse_inverse.shape, f32),
            pltpu.SemaphoreType.DMA((7,)),
            pltpu.VMEM((count, 2, blk, 128), f32),
            pltpu.VMEM((8, count * blk), f32),
            pltpu.VMEM((4, rows, cols, blk, cases), f32),
            pltpu.VMEM((4, cols, blk, cases), f32),
            pltpu.VMEM((4, cols, blk, cases), f32),
            pltpu.VMEM((4, rows, blk, cases), f32),
            pltpu.VMEM((4, rows, blk, cases), f32),
            pltpu.VMEM((count * blk, 3 * count * blk), bf16),
            pltpu.VMEM((2 * (rows + cols), blk, 3 * blk), bf16),
            pltpu.VMEM((count, blk, 3 * blk), bf16),
            pltpu.VMEM((8, width), f32),
            pltpu.VMEM((n, 8, width), f32),
            pltpu.VMEM((4, 8, count * blk), f32),
            pltpu.VMEM((2, 8, cases), f32),
            pltpu.VMEM((2, n, 8, cases), f32),
            pltpu.VMEM((8, cases), f32),
            pltpu.VMEM((n, 8, cases), f32),
            pltpu.VMEM((40, count * blk), f32),
            pltpu.VMEM((40, count * blk), f32),
            pltpu.VMEM((4, 40, count * blk), f32),
            pltpu.VMEM((256, count * blk), f32),
            pltpu.VMEM((2, n * 8, n * 8), f32),
            pltpu.VMEM((2,) + load_cases.shape, f32),
            pltpu.SemaphoreType.DMA((4, 4)),
            pltpu.SemaphoreType.DMA((4, 4)),
            pltpu.SemaphoreType.DMA((4,)),
            pltpu.SemaphoreType.DMA((4,)),
            pltpu.SemaphoreType.DMA((4,)),
            pltpu.SemaphoreType.DMA((4,)),
            pltpu.SemaphoreType.DMA((ny,)),
            pltpu.SemaphoreType.DMA((ny,)),
            pltpu.SemaphoreType.DMA,
            pltpu.SemaphoreType.DMA,
            pltpu.SemaphoreType.DMA((3,)),
            pltpu.SemaphoreType.DMA((3,)),
            pltpu.SemaphoreType.DMA((2,)),
            pltpu.SemaphoreType.REGULAR,
        ],
        compiler_params=pltpu.CompilerParams(
            collective_id=0, has_side_effects=True, vmem_limit_bytes=60 * 2**20
        ),
    )(
        load_cases, matrix_tiles, block_cols, smoother_blocks, near_null, coarse_map,
        coarse_inverse,
    )
    return pl.pallas_call(
        finish_kernel,
        out_shape=(shape, shape),
        in_specs=[hbm, hbm, hbm, hbm],
        out_specs=(hbm, hbm),
        scratch_shapes=[
            pltpu.VMEM((5,) + load_cases.shape, f32),
            pltpu.VMEM((1, cases), f32),
            pltpu.SemaphoreType.DMA((5, rows)),
            pltpu.SemaphoreType.DMA,
        ],
        compiler_params=pltpu.CompilerParams(vmem_limit_bytes=60 * 2**20),
    )(load_cases, precond, image, alpha)


def per_device(
    load_cases, matrix_tiles, block_cols, smoother_blocks, near_null, coarse_map, coarse_inverse
):
    agg_rows, agg_cols, block_size, case_count = load_cases.shape
    mode_count = near_null.shape[2] // block_size
    coarse_total = coarse_inverse.shape[1]
    coarse_aggs = coarse_total // mode_count
    modes = near_null.reshape(agg_rows, agg_cols, mode_count, block_size)
    inverse_blocks = smoother_blocks.reshape(agg_rows, agg_cols, block_size, block_size)

    steps = ((0, 0), (-1, 0), (1, 0), (0, -1), (0, 1))
    tiles = matrix_tiles.reshape(agg_rows, agg_cols, block_size, -1, block_size)
    row_at = jnp.arange(agg_rows, dtype=jnp.int32)[:, None, None]
    col_at = jnp.arange(agg_cols, dtype=jnp.int32)[None, :, None]
    stencil = []
    for dx, dy in steps:
        named = block_cols == (row_at + 1 + dx) * (agg_cols + 2) + col_at + 1 + dy
        stencil.append(jnp.sum(jnp.where(named[:, :, None, :, None], tiles, 0.0), axis=3))

    def operate(vector_field):
        extended = padded(vector_field, (("gx", 0), ("gy", 1)), 1)
        total = 0.0
        for tile, (dx, dy) in zip(stencil, steps):
            cells = extended[1 + dx : 1 + dx + agg_rows, 1 + dy : 1 + dy + agg_cols]
            total = total + jnp.einsum("ijbk,ijkr->ijbr", tile, cells, precision=highest)
        return total

    def smooth(defect):
        return relax_weight * jnp.einsum(
            "ijab,ijbr->ijar", inverse_blocks, defect, precision=highest
        )

    def correct(defect):
        contrib = jnp.einsum("ijkb,ijbr->ijkr", modes, defect, precision=highest)
        own_part = jnp.sum(contrib, axis=(0, 1))
        my_label = coarse_map[0, 0]
        label_value = jnp.reshape(my_label.astype(jnp.float32), (1,))
        pieces, labels = (
            lax.all_gather(own_part[None], ("gx", "gy"), axis=0, tiled=True),
            lax.all_gather(label_value, ("gx", "gy"), axis=0, tiled=True),
        )
        label_ids = labels.astype(jnp.int32)
        placing = (label_ids[:, None] == jnp.arange(coarse_aggs, dtype=jnp.int32)[None, :]).astype(
            jnp.float32
        )
        ordered = jnp.einsum("dc,dkr->ckr", placing, pieces, precision=highest).reshape(
            coarse_total, case_count
        )
        own_rows = jnp.dot(coarse_inverse, ordered, precision=highest)
        solved = lax.all_gather(own_rows, ("gx", "gy"), axis=0, tiled=True)
        mine = lax.dynamic_slice_in_dim(solved, my_label * mode_count, mode_count, 0)
        coarse_back = jnp.broadcast_to(
            mine[None, None], (agg_rows, agg_cols, mode_count, case_count)
        )
        return jnp.einsum("ijkb,ijkr->ijbr", modes, coarse_back, precision=highest)

    first = smooth(load_cases)
    first = first + correct(load_cases - operate(first))
    precond = first + smooth(load_cases - operate(first))
    defect = load_cases - operate(precond)
    update = smooth(defect)
    update = update + correct(defect - operate(update))
    update = update + smooth(defect - operate(update))
    precond = precond + update
    local_aligned = jnp.sum(load_cases * precond, axis=(0, 1, 2))
    aligned = lax.psum(local_aligned, ("gx", "gy"))
    image = operate(precond)
    curved = lax.psum(jnp.sum(precond * image, axis=(0, 1, 2)), ("gx", "gy"))
    alpha = aligned / curved
    solution = alpha * precond
    residual = load_cases - alpha * image
    return (solution, residual)


def solution(mesh):
    nx, ny = mesh.shape["gx"], mesh.shape["gy"]
    step = functools.partial(fused, nx, ny) if nx * ny <= 128 else per_device
    placed = (
        P("gx", "gy", None, None),
        P("gx", "gy", None, None),
        P("gx", "gy", None),
        P("gx", "gy", None),
        P("gx", "gy", None),
        P("gx", "gy"),
        P(("gx", "gy"), None),
    )
    return jax.shard_map(
        step,
        mesh=mesh,
        in_specs=placed,
        out_specs=(P("gx", "gy", None, None), P("gx", "gy", None, None)),
        check_vma=False,
    )
```

```python
import functools

import jax
import jax.numpy as jnp
from jax import lax
from jax.experimental import pallas as pl
from jax.experimental.pallas import tpu as pltpu
from jax.sharding import PartitionSpec as P

relax_weight = 0.8
highest = lax.Precision.HIGHEST


def padded(cells, sides, width):
    for axis, dim in sides:
        count = lax.axis_size(axis)
        ends = count - 1
        head = lax.slice_in_dim(cells, 0, width, axis=dim)
        tail = lax.slice_in_dim(cells, cells.shape[dim] - width, cells.shape[dim], axis=dim)
        cells = jnp.concatenate(
            [
                lax.ppermute(tail, axis, [(i, (i + 1) % count) for i in range(ends)]),
                cells,
                lax.ppermute(head, axis, [((i + 1) % count, i) for i in range(ends)]),
            ],
            axis=dim,
        )
    return cells


def cut(v):
    hi = v.astype(jnp.bfloat16)
    return hi, (v - hi.astype(jnp.float32)).astype(jnp.bfloat16)


def stacked(v):
    hi, lo = cut(v)
    return jnp.concatenate([hi, lo, hi], axis=0)


def mm(a, b):
    return lax.dot_general(a, b, (((1,), (0,)), ((), ())), preferred_element_type=jnp.float32)


def mm_t(a, b, precision=None):
    return lax.dot_general(
        a, b, (((1,), (1,)), ((), ())), precision=precision, preferred_element_type=jnp.float32
    )


def mm3(a_cut, b):
    hi, lo = cut(b)
    return mm(a_cut[0], hi) + (mm(a_cut[0], lo) + mm(a_cut[1], hi))


def flipped(v, mask):
    bit = 1
    while bit <= mask:
        if mask & bit:
            v = v + bit - 2 * bit * lax.rem(v // bit, 2)
        bit *= 2
    return v


def far_first(nx, ny):
    def hops(pair):
        mx, my = pair
        return bin(mx >> 1).count("1") + my + 0.1 * (mx & 1)

    pairs = [(mx, my) for mx in range(nx) for my in range(ny) if mx or my]
    return sorted(pairs, key=hops, reverse=True)


def step_kernel(
    nx, ny, modes,
    b_hbm, a_hbm, cols_hbm, s_hbm, n_hbm, map_hbm, inv_hbm,
    solution_ref, residual_ref,
    b_ref, a_ref, cols_ref, s_ref, n_ref, map_ref, inv_ref, loaded,
    blocks, nulls, field, up, down, left, right, local, edge, smoother, info, info_all, near, coarse, coarse_all,
    sums, sums_all, spread, relaxed, relaxed_near, reach, solved,
    halo_send, halo_recv, near_send, near_recv, relaxed_send, relaxed_recv, col_send, col_recv,
    all_send, all_recv, direct_send, direct_recv, entered,
):
    rows, cols, blk, cases = b_ref.shape
    count = rows * cols
    size = count * blk
    n = nx * ny
    width = info.shape[1]
    coarse_rows = n * 8
    around = spread.shape[0]
    x, y = lax.axis_index("gx"), lax.axis_index("gy")
    me = x * ny + y
    sides = (
        (x > 0, (x - 1, y)),
        (x < nx - 1, (x + 1, y)),
        (y > 0, (x, y - 1)),
        (y < ny - 1, (x, y + 1)),
    )
    halos = (up, down, left, right)
    order_of_peers = far_first(nx, ny)
    peers_x = [flipped(x, m) for m in range(nx)]
    peers_y = [flipped(y, m) for m in range(ny)]
    barrier = pltpu.get_barrier_semaphore()

    loads = [
        pltpu.make_async_copy(src, dst, loaded.at[i])
        for i, (src, dst) in enumerate(
            (
                (s_hbm, s_ref), (b_hbm, b_ref), (n_hbm, n_ref), (inv_hbm, inv_ref),
                (map_hbm, map_ref), (cols_hbm, cols_ref), (a_hbm, a_ref),
            )
        )
    ]
    for load in loads:
        load.start()

    coarse_all[...] = jnp.zeros_like(coarse_all)
    info_all[...] = jnp.zeros_like(info_all)

    lines = [pair for pair in order_of_peers if 0 in pair]
    for mx, my in lines:
        pl.semaphore_signal(
            barrier, inc=1, device_id=(peers_x[mx], peers_y[my]),
            device_id_type=pl.DeviceIdType.MESH,
        )

    spread[...] = jnp.zeros_like(spread)
    reach[...] = jnp.zeros_like(reach)
    nulls[...] = jnp.zeros_like(nulls)
    info[...] = jnp.zeros_like(info)
    local[...] = jnp.zeros_like(local)
    for side, (here, _) in enumerate(sides):

        @pl.when(jnp.logical_not(here))
        def _():
            halos[side][...] = jnp.zeros_like(halos[side])
            near[side] = jnp.zeros_like(near[side])
            relaxed_near[side] = jnp.zeros_like(relaxed_near[side])

    told, told_all = info.at[0 : modes + 1], info_all.at[:, 0 : modes + 1]

    def at_column(src, dst):
        return [
            pltpu.make_async_remote_copy(
                src_ref=src, dst_ref=dst.at[me], send_sem=col_send.at[j],
                recv_sem=col_recv.at[ny - j],
                device_id=(x, lax.rem(y + j, ny)), device_id_type=pl.DeviceIdType.MESH,
            )
            for j in range(1, ny)
        ]

    def pass_on(src, dst, slot):
        for mx in range(nx - 1, 0, -1):
            pltpu.make_async_remote_copy(
                src_ref=src, dst_ref=dst.at[slot], send_sem=all_send, recv_sem=all_recv,
                device_id=(peers_x[mx], y), device_id_type=pl.DeviceIdType.MESH,
            ).start()

    def told_pass():
        for j in list(range(1, ny, 2)) + list(range(2, ny, 2)):
            slot = x * ny + lax.rem(y + j, ny)
            pltpu.make_async_copy(told, told, col_recv.at[j]).wait()
            pass_on(told_all.at[slot], told_all, slot)

    def wait_many(dst, tiles, sem):
        some = dst.at[pl.ds(0, tiles)]
        pltpu.make_async_copy(some, some, sem).wait()

    def to_all(src, dst, k):
        for mx, my in order_of_peers:
            pltpu.make_async_remote_copy(
                src_ref=src, dst_ref=dst.at[me], send_sem=direct_send.at[k],
                recv_sem=direct_recv.at[k], device_id=(peers_x[mx], peers_y[my]),
                device_id_type=pl.DeviceIdType.MESH,
            ).start()

    def halo_copies(k):
        now = field.at[k]
        out = (
            (now.at[0], down.at[k], 1),
            (now.at[rows - 1], up.at[k], 0),
            (now.at[:, 0], right.at[k], 3),
            (now.at[:, cols - 1], left.at[k], 2),
        )
        return [
            pltpu.make_async_remote_copy(
                src_ref=src, dst_ref=dst,
                send_sem=halo_send.at[k, side], recv_sem=halo_recv.at[k, lands],
                device_id=peer, device_id_type=pl.DeviceIdType.MESH,
            )
            for side, ((src, dst, lands), (_, peer)) in enumerate(zip(out, sides))
        ]

    def halo_start(k):
        for (here, _), copy in zip(sides, halo_copies(k)):
            pl.when(here)(copy.start)

    def halo_wait(k, side):
        buf = halos[side].at[k]
        pl.when(sides[side][0])(pltpu.make_async_copy(buf, buf, halo_recv.at[k, side]).wait)

    def to_sides(src, dst, send, recv):
        return [
            pltpu.make_async_remote_copy(
                src_ref=src, dst_ref=dst.at[lands],
                send_sem=send.at[side], recv_sem=recv.at[lands],
                device_id=peer, device_id_type=pl.DeviceIdType.MESH,
            )
            for side, (lands, (_, peer)) in enumerate(zip((1, 0, 3, 2), sides))
        ]

    def near_copies():
        return to_sides(nulls, near, near_send, near_recv)

    def relaxed_copies():
        return to_sides(relaxed, relaxed_near, relaxed_send, relaxed_recv)

    def from_sides(dst, recv):
        for side, (here, _) in enumerate(sides):
            buf = dst.at[side]
            pl.when(here)(pltpu.make_async_copy(buf, buf, recv.at[side]).wait)

    loads[0].wait()
    for i in range(rows):
        for j in range(cols):
            p = i * cols + j
            for c in range(0, blk * blk, 128):
                blocks[p, 0, c // 128 : c // 128 + 1] = s_ref[j, i : i + 1, c : c + 128]
            flat = blocks[p, 0, 0 : blk * blk // 128]
            for half in range(128 // blk):
                blocks[p, 1, pl.ds(half, blk * blk // 128, stride=128 // blk), 0:blk] = flat[
                    :, half * blk : (half + 1) * blk
                ]
    for p in range(count):
        hi, lo = cut(relax_weight * blocks[p, 1, :, 0:blk])
        smoother[p] = jnp.concatenate([hi, hi, lo], axis=1)

    def smooth(v):
        return jnp.concatenate(
            [mm(smoother[p], stacked(v[p * blk : (p + 1) * blk])) for p in range(count)], axis=0
        )

    def put(v, k):
        field[k] = v.reshape(rows, cols, blk, cases)

    loads[1].wait()
    b = b_ref[...].reshape(size, cases)
    first = smooth(b)
    put(first, 0)

    for load in loads[2:5]:
        load.wait()
    for i in range(rows):
        for j in range(cols):
            p = i * cols + j
            for k in range(modes):
                nulls[k : k + 1, p * blk : (p + 1) * blk] = n_ref[
                    j, i : i + 1, k * blk : (k + 1) * blk
                ]
    info[0:modes, 0 : inv_ref.shape[1]] = inv_ref[...]
    info[modes : modes + 1, :] = jnp.full((1, width), map_ref[0, 0].astype(jnp.float32))

    pl.semaphore_wait(barrier, len(lines))
    for (here, _), copy in zip(sides, near_copies()):
        pl.when(here)(copy.start)
    for copy in at_column(told, told_all):
        copy.start()
    halo_start(0)
    for mx in range(1, nx):
        pl.semaphore_signal(
            entered, inc=1, device_id=(peers_x[mx], y), device_id_type=pl.DeviceIdType.MESH
        )
    pass_on(told, told_all, me)
    info_all[pl.ds(me, 1)] = info[...][None]

    loads[5].wait()
    loads[6].wait()
    for i in range(rows):
        for j in range(cols):
            p = i * cols + j
            tiles = [a_ref[i, j, :, s * blk : (s + 1) * blk] for s in range(5)]
            names = [cols_ref[j, i, s] for s in range(5)]
            for d, (di, dj) in enumerate(((0, 0), (-1, 0), (1, 0), (0, -1), (0, 1))):
                e = (i + 1 + di) * (cols + 2) + j + 1 + dj
                tile = tiles[0] * (names[0] == e).astype(jnp.float32)
                for s in range(1, 5):
                    tile = tile + tiles[s] * (names[s] == e).astype(jnp.float32)
                hi, lo = cut(tile)
                ii, jj = i + di, j + dj
                if 0 <= ii < rows and 0 <= jj < cols:
                    q = ii * cols + jj
                    for k, part in enumerate((hi, hi, lo)):
                        at = k * size + q * blk
                        local[p * blk : (p + 1) * blk, at : at + blk] = part
                else:
                    at = (0, j, cols + j, 2 * cols + i, 2 * cols + rows + i)[d]
                    edge[at] = jnp.concatenate([hi, hi, lo], axis=1)

    def places():
        for j in range(cols):
            yield 0, j, j, j
        for j in range(cols):
            yield 1, j, cols + j, (rows - 1) * cols + j
        for i in range(rows):
            yield 2, i, 2 * cols + i, i * cols
        for i in range(rows):
            yield 3, i, 2 * cols + rows + i, i * cols + cols - 1

    def operate(v, k):
        inner = mm(local[...], stacked(v))
        parts = [inner[p * blk : (p + 1) * blk] for p in range(count)]
        for side in (2, 3, 0, 1):
            halo_wait(k, side)
            for at_side, at, e, p in places():
                if at_side == side:
                    parts[p] = parts[p] + mm(edge[e], stacked(halos[side][k, at]))
        return jnp.concatenate(parts, axis=0)

    own_n = nulls[...]
    own_hi, own_lo = cut(own_n)
    own_cat = jnp.concatenate([own_hi, own_hi, own_lo], axis=1)

    def mine(k):
        return coarse.at[k, 0:modes]

    def theirs_all(k):
        return coarse_all.at[k, :, 0:modes]

    def restrict(v, k):
        g = mm(own_cat, stacked(v))
        coarse[k] = g
        to_all(mine(k), theirs_all(k), k)
        coarse_all[k, pl.ds(me, 1)] = g[None]

    def gathered(k):
        wait_many(theirs_all(k), n - 1, direct_recv.at[k])
        return coarse_all[k].reshape(coarse_rows, cases)

    def across(v):
        hi, lo = cut(v)
        return jnp.concatenate([hi, lo, hi], axis=1)

    facing = (
        lambda at: (rows - 1) * cols + at,
        lambda at: at,
        lambda at: at * cols + cols - 1,
        lambda at: at * cols,
    )
    spread[0:8] = mm_t(across(own_n), local[...])
    from_sides(near, near_recv)
    for side, at, e, p in places():
        q = facing[side](at)
        spread[8 * (1 + side) : 8 * (2 + side), p * blk : (p + 1) * blk] = mm_t(
            across(near[side, :, q * blk : (q + 1) * blk]), edge[e]
        )
    for p in range(count):
        relaxed[:, p * blk : (p + 1) * blk] = mm_t(
            across(spread[:, p * blk : (p + 1) * blk]), smoother[p]
        )
    for (here, _), copy in zip(sides, relaxed_copies()):
        pl.when(here)(copy.start)
    told_pass()

    r = b - operate(first, 0)
    pl.semaphore_wait(entered, nx - 1)
    restrict(r, 0)
    t = smooth(r)
    put(t, 1)
    halo_start(1)

    reach[0:around] = spread[...] - mm_t(across(relaxed[...]), local[...])
    eye = (
        lax.broadcasted_iota(jnp.int32, (size, size), 0)
        == lax.broadcasted_iota(jnp.int32, (size, size), 1)
    ).astype(jnp.float32).astype(jnp.bfloat16)

    def turned(v):
        return tuple(mm_t(eye, part).astype(jnp.bfloat16) for part in cut(v))

    gain = turned(
        jnp.concatenate([own_n - relaxed[0:8], 0.0 - relaxed[8:around]], axis=0)
    )
    wait_many(told_all, (nx - 1) * ny, all_recv)
    inv_parts = cut(info_all[...].reshape(coarse_rows, width))
    lane3 = lax.broadcasted_iota(jnp.int32, (n, 8, width), 2).astype(jnp.float32)
    row3 = lax.broadcasted_iota(jnp.int32, (n, 8, width), 1)
    labels = jnp.broadcast_to(info_all[...][:, modes : modes + 1, :], (n, 8, width))
    where3 = labels * float(modes) + row3.astype(jnp.float32)
    order = jnp.where(lane3 == where3, 1.0, 0.0)
    order = jnp.where(row3 < modes, order, 0.0).reshape(coarse_rows, width).astype(jnp.bfloat16)
    lane4 = lax.broadcasted_iota(jnp.int32, (n, 8, coarse_rows), 2).astype(jnp.float32)
    row4 = lax.broadcasted_iota(jnp.int32, (n, 8, coarse_rows), 1)
    labels4 = jnp.broadcast_to(info_all[...][:, modes : modes + 1, 0:1], (n, 8, coarse_rows))
    pick = jnp.where(lane4 == labels4 * 8.0 + row4.astype(jnp.float32), 1.0, 0.0)
    pick = jnp.where(row4 < modes, pick, 0.0).reshape(coarse_rows, coarse_rows).astype(jnp.bfloat16)
    for k, part in enumerate(inv_parts):
        solved[k] = mm_t(mm(pick, part).astype(jnp.bfloat16), order)

    def clipped(px, py):
        return jnp.clip(px, 0, nx - 1) * ny + jnp.clip(py, 0, ny - 1)

    def cross(px, py):
        return [
            clipped(px + dx, py + dy)
            for dx, dy in ((0, 0), (-1, 0), (1, 0), (0, -1), (0, 1))
        ]

    ids = cross(x, y)
    for _, (px, py) in sides:
        ids = ids + cross(px, py)
    lacking = jnp.zeros((reach.shape[0] - 8 * len(ids), coarse_rows), jnp.float32)
    solve = tuple(
        jnp.concatenate(
            [solved[k, pl.ds(pl.multiple_of(d * 8, 8), 8)] for d in ids] + [lacking], axis=0
        ).astype(jnp.bfloat16)
        for k in range(2)
    )

    def mm3_cut(a_cut, b_cut):
        return mm(a_cut[0], b_cut[0]) + (mm(a_cut[0], b_cut[1]) + mm(a_cut[1], b_cut[0]))

    gain_cut = cut(mm3_cut(gain, tuple(part[0:around] for part in solve)))

    from_sides(relaxed_near, relaxed_recv)
    for side, at, e, p in places():
        q = facing[side](at)
        reach[around * (1 + side) : around * (2 + side), p * blk : (p + 1) * blk] = 0.0 - mm_t(
            across(relaxed_near[side, :, q * blk : (q + 1) * blk]), edge[e]
        )
    loss_cut = cut(mm3_cut(turned(reach[...]), solve))

    q1 = r - operate(t, 1)
    g = gathered(0)
    r = q1 - mm3(loss_cut, g)
    s = smooth(r)
    put(s, 2)
    halo_start(2)
    precond = first + t + mm3(gain_cut, g) + s
    r = r - operate(s, 2)
    restrict(r, 1)
    t = smooth(r)
    put(t, 3)
    halo_start(3)
    precond = precond + t
    q2 = r - operate(t, 3)
    base = b - q2
    g = gathered(1)
    precond = precond + mm3(gain_cut, g)
    image = base + mm3(loss_cut, g)
    sums[...] = jnp.concatenate(
        [
            jnp.sum(b * precond, axis=0, keepdims=True),
            jnp.sum(precond * image, axis=0, keepdims=True),
            jnp.zeros((6, cases), jnp.float32),
        ],
        axis=0,
    )
    pairs = sums_all.at[:, 0:2]
    to_all(sums.at[0:2], pairs, 2)
    sums_all[pl.ds(me, 1)] = sums[...][None]
    for k in range(4):
        for (here, _), copy in zip(sides, halo_copies(k)):
            pl.when(here)(copy.wait_send)
    for (here, _), copy in zip(sides, near_copies()):
        pl.when(here)(copy.wait_send)
    for (here, _), copy in zip(sides, relaxed_copies()):
        pl.when(here)(copy.wait_send)
    for copy in at_column(told, told_all):
        copy.wait_send()
    wait_many(told_all, (nx - 1) * ny, all_send)
    for k in range(2):
        wait_many(theirs_all(k), n - 1, direct_send.at[k])
    wait_many(pairs, n - 1, direct_recv.at[2])
    total = jnp.sum(sums_all[:, 0:2], axis=0)
    alpha = total[0:1] / total[1:2]
    solution_ref[...] = (alpha * precond).reshape(rows, cols, blk, cases)
    residual_ref[...] = (b - alpha * image).reshape(rows, cols, blk, cases)
    wait_many(pairs, n - 1, direct_send.at[2])


def finish_kernel(s_ref, r_ref, sol_ref, res_ref, sems):
    copies = [
        pltpu.make_async_copy(src, dst, sems.at[k])
        for k, (src, dst) in enumerate(((s_ref, sol_ref), (r_ref, res_ref)))
    ]
    for copy in copies:
        copy.start()
    for copy in copies:
        copy.wait()


def fused(
    nx, ny,
    load_cases, matrix_tiles, block_cols, smoother_blocks, near_null, coarse_map, coarse_inverse
):
    rows, cols, blk, cases = load_cases.shape
    count = rows * cols
    modes = near_null.shape[2] // blk
    n = nx * ny
    width = -(-coarse_inverse.shape[1] // 128) * 128
    block_cols = jnp.transpose(block_cols, (1, 0, 2))
    smoother_blocks = jnp.transpose(smoother_blocks, (1, 0, 2))
    near_null = jnp.transpose(near_null, (1, 0, 2))
    vmem = pl.BlockSpec(memory_space=pltpu.VMEM)
    hbm = pl.BlockSpec(memory_space=pltpu.HBM)
    f32, bf16 = jnp.float32, jnp.bfloat16
    shape = jax.ShapeDtypeStruct(load_cases.shape, f32)
    held = pltpu.VMEM(load_cases.shape, f32)
    solved, residual = pl.pallas_call(
        functools.partial(step_kernel, nx, ny, modes),
        out_shape=(held, held),
        in_specs=[hbm] * 7,
        out_specs=(vmem, vmem),
        scratch_shapes=[
            pltpu.VMEM(load_cases.shape, f32),
            pltpu.VMEM(matrix_tiles.shape, f32),
            pltpu.SMEM(block_cols.shape, jnp.int32),
            pltpu.VMEM(smoother_blocks.shape, f32),
            pltpu.VMEM(near_null.shape, f32),
            pltpu.SMEM(coarse_map.shape, jnp.int32),
            pltpu.VMEM(coarse_inverse.shape, f32),
            pltpu.SemaphoreType.DMA((7,)),
            pltpu.VMEM((count, 2, blk, 128), f32),
            pltpu.VMEM((8, count * blk), f32),
            pltpu.VMEM((4, rows, cols, blk, cases), f32),
            pltpu.VMEM((4, cols, blk, cases), f32),
            pltpu.VMEM((4, cols, blk, cases), f32),
            pltpu.VMEM((4, rows, blk, cases), f32),
            pltpu.VMEM((4, rows, blk, cases), f32),
            pltpu.VMEM((count * blk, 3 * count * blk), bf16),
            pltpu.VMEM((2 * (rows + cols), blk, 3 * blk), bf16),
            pltpu.VMEM((count, blk, 3 * blk), bf16),
            pltpu.VMEM((8, width), f32),
            pltpu.VMEM((n, 8, width), f32),
            pltpu.VMEM((4, 8, count * blk), f32),
            pltpu.VMEM((2, 8, cases), f32),
            pltpu.VMEM((2, n, 8, cases), f32),
            pltpu.VMEM((8, cases), f32),
            pltpu.VMEM((n, 8, cases), f32),
            pltpu.VMEM((40, count * blk), f32),
            pltpu.VMEM((40, count * blk), f32),
            pltpu.VMEM((4, 40, count * blk), f32),
            pltpu.VMEM((256, count * blk), f32),
            pltpu.VMEM((2, n * 8, n * 8), f32),
            pltpu.SemaphoreType.DMA((4, 4)),
            pltpu.SemaphoreType.DMA((4, 4)),
            pltpu.SemaphoreType.DMA((4,)),
            pltpu.SemaphoreType.DMA((4,)),
            pltpu.SemaphoreType.DMA((4,)),
            pltpu.SemaphoreType.DMA((4,)),
            pltpu.SemaphoreType.DMA((ny,)),
            pltpu.SemaphoreType.DMA((ny,)),
            pltpu.SemaphoreType.DMA,
            pltpu.SemaphoreType.DMA,
            pltpu.SemaphoreType.DMA((3,)),
            pltpu.SemaphoreType.DMA((3,)),
            pltpu.SemaphoreType.REGULAR,
        ],
        compiler_params=pltpu.CompilerParams(
            collective_id=0, has_side_effects=True, vmem_limit_bytes=32 * 2**20
        ),
    )(
        *(
            pltpu.with_memory_space_constraint(v, pltpu.HBM)
            for v in (
                load_cases, matrix_tiles, block_cols, smoother_blocks, near_null, coarse_map,
                coarse_inverse,
            )
        )
    )
    return pl.pallas_call(
        finish_kernel,
        out_shape=(shape, shape),
        in_specs=[vmem, vmem],
        out_specs=(hbm, hbm),
        scratch_shapes=[pltpu.SemaphoreType.DMA((2,))],
        compiler_params=pltpu.CompilerParams(vmem_limit_bytes=32 * 2**20),
    )(
        *(pltpu.with_memory_space_constraint(v, pltpu.VMEM) for v in (solved, residual))
    )


def per_device(
    load_cases, matrix_tiles, block_cols, smoother_blocks, near_null, coarse_map, coarse_inverse
):
    agg_rows, agg_cols, block_size, case_count = load_cases.shape
    mode_count = near_null.shape[2] // block_size
    coarse_total = coarse_inverse.shape[1]
    coarse_aggs = coarse_total // mode_count
    modes = near_null.reshape(agg_rows, agg_cols, mode_count, block_size)
    inverse_blocks = smoother_blocks.reshape(agg_rows, agg_cols, block_size, block_size)

    steps = ((0, 0), (-1, 0), (1, 0), (0, -1), (0, 1))
    tiles = matrix_tiles.reshape(agg_rows, agg_cols, block_size, -1, block_size)
    row_at = jnp.arange(agg_rows, dtype=jnp.int32)[:, None, None]
    col_at = jnp.arange(agg_cols, dtype=jnp.int32)[None, :, None]
    stencil = []
    for dx, dy in steps:
        named = block_cols == (row_at + 1 + dx) * (agg_cols + 2) + col_at + 1 + dy
        stencil.append(jnp.sum(jnp.where(named[:, :, None, :, None], tiles, 0.0), axis=3))

    def operate(vector_field):
        extended = padded(vector_field, (("gx", 0), ("gy", 1)), 1)
        total = 0.0
        for tile, (dx, dy) in zip(stencil, steps):
            cells = extended[1 + dx : 1 + dx + agg_rows, 1 + dy : 1 + dy + agg_cols]
            total = total + jnp.einsum("ijbk,ijkr->ijbr", tile, cells, precision=highest)
        return total

    def smooth(defect):
        return relax_weight * jnp.einsum(
            "ijab,ijbr->ijar", inverse_blocks, defect, precision=highest
        )

    def correct(defect):
        contrib = jnp.einsum("ijkb,ijbr->ijkr", modes, defect, precision=highest)
        own_part = jnp.sum(contrib, axis=(0, 1))
        my_label = coarse_map[0, 0]
        label_value = jnp.reshape(my_label.astype(jnp.float32), (1,))
        pieces, labels = (
            lax.all_gather(own_part[None], ("gx", "gy"), axis=0, tiled=True),
            lax.all_gather(label_value, ("gx", "gy"), axis=0, tiled=True),
        )
        label_ids = labels.astype(jnp.int32)
        placing = (label_ids[:, None] == jnp.arange(coarse_aggs, dtype=jnp.int32)[None, :]).astype(
            jnp.float32
        )
        ordered = jnp.einsum("dc,dkr->ckr", placing, pieces, precision=highest).reshape(
            coarse_total, case_count
        )
        own_rows = jnp.dot(coarse_inverse, ordered, precision=highest)
        solved = lax.all_gather(own_rows, ("gx", "gy"), axis=0, tiled=True)
        mine = lax.dynamic_slice_in_dim(solved, my_label * mode_count, mode_count, 0)
        coarse_back = jnp.broadcast_to(
            mine[None, None], (agg_rows, agg_cols, mode_count, case_count)
        )
        return jnp.einsum("ijkb,ijkr->ijbr", modes, coarse_back, precision=highest)

    first = smooth(load_cases)
    first = first + correct(load_cases - operate(first))
    precond = first + smooth(load_cases - operate(first))
    defect = load_cases - operate(precond)
    update = smooth(defect)
    update = update + correct(defect - operate(update))
    update = update + smooth(defect - operate(update))
    precond = precond + update
    local_aligned = jnp.sum(load_cases * precond, axis=(0, 1, 2))
    aligned = lax.psum(local_aligned, ("gx", "gy"))
    image = operate(precond)
    curved = lax.psum(jnp.sum(precond * image, axis=(0, 1, 2)), ("gx", "gy"))
    alpha = aligned / curved
    solution = alpha * precond
    residual = load_cases - alpha * image
    return (solution, residual)


def solution(mesh):
    nx, ny = mesh.shape["gx"], mesh.shape["gy"]
    step = functools.partial(fused, nx, ny) if nx * ny <= 128 else per_device
    placed = (
        P("gx", "gy", None, None),
        P("gx", "gy", None, None),
        P("gx", "gy", None),
        P("gx", "gy", None),
        P("gx", "gy", None),
        P("gx", "gy"),
        P(("gx", "gy"), None),
    )
    return jax.shard_map(
        step,
        mesh=mesh,
        in_specs=placed,
        out_specs=(P("gx", "gy", None, None), P("gx", "gy", None, None)),
        check_vma=False,
    )
```

```python
import functools

import jax
import jax.numpy as jnp
from jax import lax
from jax.experimental import pallas as pl
from jax.experimental.pallas import tpu as pltpu
from jax.sharding import PartitionSpec as P

relax_weight = 0.8
highest = lax.Precision.HIGHEST


def padded(cells, sides, width):
    for axis, dim in sides:
        count = lax.axis_size(axis)
        ends = count - 1
        head = lax.slice_in_dim(cells, 0, width, axis=dim)
        tail = lax.slice_in_dim(cells, cells.shape[dim] - width, cells.shape[dim], axis=dim)
        cells = jnp.concatenate(
            [
                lax.ppermute(tail, axis, [(i, (i + 1) % count) for i in range(ends)]),
                cells,
                lax.ppermute(head, axis, [((i + 1) % count, i) for i in range(ends)]),
            ],
            axis=dim,
        )
    return cells


def cut(v):
    hi = v.astype(jnp.bfloat16)
    return hi, (v - hi.astype(jnp.float32)).astype(jnp.bfloat16)


def stacked(v):
    hi, lo = cut(v)
    return jnp.concatenate([hi, lo, hi], axis=0)


def mm(a, b):
    return lax.dot_general(a, b, (((1,), (0,)), ((), ())), preferred_element_type=jnp.float32)


def mm_t(a, b, precision=None):
    return lax.dot_general(
        a, b, (((1,), (1,)), ((), ())), precision=precision, preferred_element_type=jnp.float32
    )


def mm3(a_cut, b):
    hi, lo = cut(b)
    return mm(a_cut[0], hi) + (mm(a_cut[0], lo) + mm(a_cut[1], hi))


def flipped(v, mask):
    bit = 1
    while bit <= mask:
        if mask & bit:
            v = v + bit - 2 * bit * lax.rem(v // bit, 2)
        bit *= 2
    return v


def far_first(nx, ny):
    def hops(pair):
        mx, my = pair
        return bin(mx >> 1).count("1") + my + 0.1 * (mx & 1)

    pairs = [(mx, my) for mx in range(nx) for my in range(ny) if mx or my]
    return sorted(pairs, key=hops, reverse=True)


def step_kernel(
    nx, ny, modes,
    b_hbm, a_hbm, cols_hbm, s_hbm, n_hbm, map_hbm, inv_hbm,
    solution_ref, residual_ref,
    b_ref, a_ref, cols_ref, s_ref, n_ref, map_ref, inv_ref, loaded,
    blocks, nulls, field, up, down, left, right, local, edge, smoother, info, info_all, near, coarse, coarse_all,
    sums, sums_all, spread, relaxed, relaxed_near, reach, solved, pulls, pulls_near, pushed, pulled,
    halo_send, halo_recv, near_send, near_recv, relaxed_send, relaxed_recv, pulls_send, pulls_recv, push_send, push_recv, col_send, col_recv,
    plane_send, plane_recv, pair_send, pair_recv, direct_send, direct_recv, entered,
):
    rows, cols, blk, cases = b_ref.shape
    count = rows * cols
    size = count * blk
    n = nx * ny
    width = info.shape[1]
    coarse_rows = n * 8
    around = spread.shape[0]
    x, y = lax.axis_index("gx"), lax.axis_index("gy")
    me = x * ny + y
    sides = (
        (x > 0, (x - 1, y)),
        (x < nx - 1, (x + 1, y)),
        (y > 0, (x, y - 1)),
        (y < ny - 1, (x, y + 1)),
    )
    halos = (up, down, left, right)
    order_of_peers = far_first(nx, ny)
    peers_x = [flipped(x, m) for m in range(nx)]
    peers_y = [flipped(y, m) for m in range(ny)]
    barrier = pltpu.get_barrier_semaphore()

    loads = [
        pltpu.make_async_copy(src, dst, loaded.at[i])
        for i, (src, dst) in enumerate(
            (
                (s_hbm, s_ref), (b_hbm, b_ref), (n_hbm, n_ref), (inv_hbm, inv_ref),
                (map_hbm, map_ref), (cols_hbm, cols_ref), (a_hbm, a_ref),
            )
        )
    ]
    for load in loads:
        load.start()

    coarse_all[...] = jnp.zeros_like(coarse_all)
    info_all[...] = jnp.zeros_like(info_all)

    lines = [pair for pair in order_of_peers if 0 in pair]
    for mx, my in lines:
        pl.semaphore_signal(
            barrier, inc=1, device_id=(peers_x[mx], peers_y[my]),
            device_id_type=pl.DeviceIdType.MESH,
        )

    spread[...] = jnp.zeros_like(spread)
    reach[...] = jnp.zeros_like(reach)
    pulls[...] = jnp.zeros_like(pulls)
    nulls[...] = jnp.zeros_like(nulls)
    info[...] = jnp.zeros_like(info)
    local[...] = jnp.zeros_like(local)
    for side, (here, _) in enumerate(sides):

        @pl.when(jnp.logical_not(here))
        def _():
            halos[side][...] = jnp.zeros_like(halos[side])
            near[side] = jnp.zeros_like(near[side])
            relaxed_near[side] = jnp.zeros_like(relaxed_near[side])
            pulls_near[side] = jnp.zeros_like(pulls_near[side])
            pulled[side] = jnp.zeros_like(pulled[side])

    told, told_all = info.at[0 : modes + 1], info_all.at[:, 0 : modes + 1]

    def at_column(src, dst):
        return [
            pltpu.make_async_remote_copy(
                src_ref=src, dst_ref=dst.at[me], send_sem=col_send.at[j],
                recv_sem=col_recv.at[ny - j],
                device_id=(x, lax.rem(y + j, ny)), device_id_type=pl.DeviceIdType.MESH,
            )
            for j in range(1, ny)
        ]

    def block(mx):
        return info_all.at[pl.ds(peers_x[mx] * ny, ny), 0 : modes + 1]

    def plane_copy(mx):
        return pltpu.make_async_remote_copy(
            src_ref=block(0), dst_ref=block(0), send_sem=plane_send.at[mx // 2],
            recv_sem=plane_recv.at[mx // 2], device_id=(peers_x[mx], y),
            device_id_type=pl.DeviceIdType.MESH,
        )

    def to_sibling(mx):
        pltpu.make_async_remote_copy(
            src_ref=block(mx), dst_ref=block(mx), send_sem=pair_send, recv_sem=pair_recv,
            device_id=(peers_x[1], y), device_id_type=pl.DeviceIdType.MESH,
        ).start()

    plane = (*range(nx - 2, 0, -2),)

    def told_pass():
        for j in range(1, ny):
            pltpu.make_async_copy(told, told, col_recv.at[j]).wait()
        for mx in plane:
            plane_copy(mx).start()
        to_sibling(0)

    def told_share():
        for mx in plane[::-1]:
            pltpu.make_async_copy(block(mx), block(mx), plane_recv.at[mx // 2]).wait()
            to_sibling(mx)

    def wait_many(dst, tiles, sem):
        some = dst.at[pl.ds(0, tiles)]
        pltpu.make_async_copy(some, some, sem).wait()

    def to_all(src, dst, k):
        for mx, my in order_of_peers:
            pltpu.make_async_remote_copy(
                src_ref=src, dst_ref=dst.at[me], send_sem=direct_send.at[k],
                recv_sem=direct_recv.at[k], device_id=(peers_x[mx], peers_y[my]),
                device_id_type=pl.DeviceIdType.MESH,
            ).start()

    def halo_copies(k):
        now = field.at[k]
        out = (
            (now.at[0], down.at[k], 1),
            (now.at[rows - 1], up.at[k], 0),
            (now.at[:, 0], right.at[k], 3),
            (now.at[:, cols - 1], left.at[k], 2),
        )
        return [
            pltpu.make_async_remote_copy(
                src_ref=src, dst_ref=dst,
                send_sem=halo_send.at[k, side], recv_sem=halo_recv.at[k, lands],
                device_id=peer, device_id_type=pl.DeviceIdType.MESH,
            )
            for side, ((src, dst, lands), (_, peer)) in enumerate(zip(out, sides))
        ]

    def halo_start(k):
        for (here, _), copy in zip(sides, halo_copies(k)):
            pl.when(here)(copy.start)

    def halo_wait(k, side):
        buf = halos[side].at[k]
        pl.when(sides[side][0])(pltpu.make_async_copy(buf, buf, halo_recv.at[k, side]).wait)

    def to_sides(src, dst, send, recv, split=False):
        return [
            pltpu.make_async_remote_copy(
                src_ref=src.at[side] if split else src, dst_ref=dst.at[lands],
                send_sem=send.at[side], recv_sem=recv.at[lands],
                device_id=peer, device_id_type=pl.DeviceIdType.MESH,
            )
            for side, (lands, (_, peer)) in enumerate(zip((1, 0, 3, 2), sides))
        ]

    def near_copies():
        return to_sides(nulls, near, near_send, near_recv)

    def relaxed_copies():
        return to_sides(relaxed, relaxed_near, relaxed_send, relaxed_recv)

    def pulls_copies():
        return to_sides(pulls, pulls_near, pulls_send, pulls_recv, split=True)

    def push_copies():
        return to_sides(pushed, pulled, push_send, push_recv, split=True)

    def from_sides(dst, recv):
        for side, (here, _) in enumerate(sides):
            buf = dst.at[side]
            pl.when(here)(pltpu.make_async_copy(buf, buf, recv.at[side]).wait)

    loads[0].wait()
    for i in range(rows):
        for j in range(cols):
            p = i * cols + j
            for c in range(0, blk * blk, 128):
                blocks[p, 0, c // 128 : c // 128 + 1] = s_ref[j, i : i + 1, c : c + 128]
            flat = blocks[p, 0, 0 : blk * blk // 128]
            for half in range(128 // blk):
                blocks[p, 1, pl.ds(half, blk * blk // 128, stride=128 // blk), 0:blk] = flat[
                    :, half * blk : (half + 1) * blk
                ]
    for p in range(count):
        hi, lo = cut(relax_weight * blocks[p, 1, :, 0:blk])
        smoother[p] = jnp.concatenate([hi, hi, lo], axis=1)

    def smooth(v):
        return jnp.concatenate(
            [mm(smoother[p], stacked(v[p * blk : (p + 1) * blk])) for p in range(count)], axis=0
        )

    def put(v, k):
        field[k] = v.reshape(rows, cols, blk, cases)

    loads[1].wait()
    b = b_ref[...].reshape(size, cases)
    first = smooth(b)
    put(first, 0)

    for load in loads[2:5]:
        load.wait()
    for i in range(rows):
        for j in range(cols):
            p = i * cols + j
            for k in range(modes):
                nulls[k : k + 1, p * blk : (p + 1) * blk] = n_ref[
                    j, i : i + 1, k * blk : (k + 1) * blk
                ]
    info[0:modes, 0 : inv_ref.shape[1]] = inv_ref[...]
    info[modes : modes + 1, :] = jnp.full((1, width), map_ref[0, 0].astype(jnp.float32))

    pl.semaphore_wait(barrier, len(lines))
    for (here, _), copy in zip(sides, near_copies()):
        pl.when(here)(copy.start)
    for copy in at_column(told, told_all):
        copy.start()
    halo_start(0)
    for mx in range(1, nx):
        pl.semaphore_signal(
            entered, inc=1, device_id=(peers_x[mx], y), device_id_type=pl.DeviceIdType.MESH
        )
    info_all[pl.ds(me, 1)] = info[...][None]

    loads[5].wait()
    loads[6].wait()
    for i in range(rows):
        for j in range(cols):
            p = i * cols + j
            tiles = [a_ref[i, j, :, s * blk : (s + 1) * blk] for s in range(5)]
            names = [cols_ref[j, i, s] for s in range(5)]
            for d, (di, dj) in enumerate(((0, 0), (-1, 0), (1, 0), (0, -1), (0, 1))):
                e = (i + 1 + di) * (cols + 2) + j + 1 + dj
                tile = tiles[0] * (names[0] == e).astype(jnp.float32)
                for s in range(1, 5):
                    tile = tile + tiles[s] * (names[s] == e).astype(jnp.float32)
                hi, lo = cut(tile)
                ii, jj = i + di, j + dj
                if 0 <= ii < rows and 0 <= jj < cols:
                    q = ii * cols + jj
                    for k, part in enumerate((hi, hi, lo)):
                        at = k * size + q * blk
                        local[p * blk : (p + 1) * blk, at : at + blk] = part
                else:
                    at = (0, j, cols + j, 2 * cols + i, 2 * cols + rows + i)[d]
                    edge[at] = jnp.concatenate([hi, hi, lo], axis=1)

    def places():
        for j in range(cols):
            yield 0, j, j, j
        for j in range(cols):
            yield 1, j, cols + j, (rows - 1) * cols + j
        for i in range(rows):
            yield 2, i, 2 * cols + i, i * cols
        for i in range(rows):
            yield 3, i, 2 * cols + rows + i, i * cols + cols - 1

    def operate(v, k):
        inner = mm(local[...], stacked(v))
        parts = [inner[p * blk : (p + 1) * blk] for p in range(count)]
        for side in (2, 3, 0, 1):
            halo_wait(k, side)
            for at_side, at, e, p in places():
                if at_side == side:
                    parts[p] = parts[p] + mm(edge[e], stacked(halos[side][k, at]))
        return jnp.concatenate(parts, axis=0)

    own_n = nulls[...]
    own_hi, own_lo = cut(own_n)
    own_cat = jnp.concatenate([own_hi, own_hi, own_lo], axis=1)

    def mine(k):
        return coarse.at[k, 0:modes]

    def theirs_all(k):
        return coarse_all.at[k, :, 0:modes]

    def publish(g, k):
        coarse[k] = g
        to_all(mine(k), theirs_all(k), k)
        coarse_all[k, pl.ds(me, 1)] = g[None]

    def gathered(k):
        wait_many(theirs_all(k), n - 1, direct_recv.at[k])
        return coarse_all[k].reshape(coarse_rows, cases)

    def across(v):
        hi, lo = cut(v)
        return jnp.concatenate([hi, lo, hi], axis=1)

    facing = (
        lambda at: (rows - 1) * cols + at,
        lambda at: at,
        lambda at: at * cols + cols - 1,
        lambda at: at * cols,
    )
    spread[0:8] = mm_t(across(own_n), local[...])
    from_sides(near, near_recv)
    for side, at, e, p in places():
        q = facing[side](at)
        spread[8 * (1 + side) : 8 * (2 + side), p * blk : (p + 1) * blk] = mm_t(
            across(near[side, :, q * blk : (q + 1) * blk]), edge[e]
        )
    for p in range(count):
        relaxed[:, p * blk : (p + 1) * blk] = mm_t(
            across(spread[:, p * blk : (p + 1) * blk]), smoother[p]
        )
    for (here, _), copy in zip(sides, relaxed_copies()):
        pl.when(here)(copy.start)
    told_pass()

    reach[0:around] = spread[...] - mm_t(across(relaxed[...]), local[...])
    eye = (
        lax.broadcasted_iota(jnp.int32, (size, size), 0)
        == lax.broadcasted_iota(jnp.int32, (size, size), 1)
    ).astype(jnp.float32).astype(jnp.bfloat16)

    def turned(v):
        return tuple(mm_t(eye, part).astype(jnp.bfloat16) for part in cut(v))

    gain = turned(
        jnp.concatenate([own_n - relaxed[0:8], 0.0 - relaxed[8:around]], axis=0)
    )
    for side, at, e, p in places():
        q = facing[side](at)
        hi, lo = own_hi[:, p * blk : (p + 1) * blk], own_lo[:, p * blk : (p + 1) * blk]
        tile, rest = edge[e, :, 0:blk], edge[e, :, 2 * blk : 3 * blk]
        pulls[side, :, q * blk : (q + 1) * blk] = mm(hi, tile) + (mm(hi, rest) + mm(lo, tile))
    for (here, _), copy in zip(sides, pulls_copies()):
        pl.when(here)(copy.start)

    r = b - operate(first, 0)
    pl.semaphore_wait(entered, nx - 1)
    publish(mm(own_cat, stacked(r)), 0)
    t = smooth(r)
    put(t, 1)
    halo_start(1)
    told_share()

    from_sides(relaxed_near, relaxed_recv)
    for side, at, e, p in places():
        q = facing[side](at)
        reach[around * (1 + side) : around * (2 + side), p * blk : (p + 1) * blk] = 0.0 - mm_t(
            across(relaxed_near[side, :, q * blk : (q + 1) * blk]), edge[e]
        )
    reach_turned = turned(reach[...])
    wait_many(told_all, nx // 2 * ny, pair_recv)
    inv_parts = cut(info_all[...].reshape(coarse_rows, width))
    lane3 = lax.broadcasted_iota(jnp.int32, (n, 8, width), 2).astype(jnp.float32)
    row3 = lax.broadcasted_iota(jnp.int32, (n, 8, width), 1)
    labels = jnp.broadcast_to(info_all[...][:, modes : modes + 1, :], (n, 8, width))
    where3 = labels * float(modes) + row3.astype(jnp.float32)
    order = jnp.where(lane3 == where3, 1.0, 0.0)
    order = jnp.where(row3 < modes, order, 0.0).reshape(coarse_rows, width).astype(jnp.bfloat16)
    lane4 = lax.broadcasted_iota(jnp.int32, (n, 8, coarse_rows), 2).astype(jnp.float32)
    row4 = lax.broadcasted_iota(jnp.int32, (n, 8, coarse_rows), 1)
    labels4 = jnp.broadcast_to(info_all[...][:, modes : modes + 1, 0:1], (n, 8, coarse_rows))
    pick = jnp.where(lane4 == labels4 * 8.0 + row4.astype(jnp.float32), 1.0, 0.0)
    pick = jnp.where(row4 < modes, pick, 0.0).reshape(coarse_rows, coarse_rows).astype(jnp.bfloat16)
    for k, part in enumerate(inv_parts):
        solved[k] = mm_t(mm(pick, part).astype(jnp.bfloat16), order)

    def clipped(px, py):
        return jnp.clip(px, 0, nx - 1) * ny + jnp.clip(py, 0, ny - 1)

    def cross(px, py):
        return [
            clipped(px + dx, py + dy)
            for dx, dy in ((0, 0), (-1, 0), (1, 0), (0, -1), (0, 1))
        ]

    ids = cross(x, y)
    for _, (px, py) in sides:
        ids = ids + cross(px, py)
    lacking = jnp.zeros((reach.shape[0] - 8 * len(ids), coarse_rows), jnp.float32)
    solve = tuple(
        jnp.concatenate(
            [solved[k, pl.ds(pl.multiple_of(d * 8, 8), 8)] for d in ids] + [lacking], axis=0
        ).astype(jnp.bfloat16)
        for k in range(2)
    )

    def mm3_cut(a_cut, b_cut):
        return mm(a_cut[0], b_cut[0]) + (mm(a_cut[0], b_cut[1]) + mm(a_cut[1], b_cut[0]))

    gain_cut = cut(mm3_cut(gain, tuple(part[0:around] for part in solve)))

    loss_cut = cut(mm3_cut(reach_turned, solve))

    from_sides(pulls_near, pulls_recv)
    inner_pull = mm(own_hi, local[:, 0:size]) + (
        mm(own_hi, local[:, 2 * size : 3 * size]) + mm(own_lo, local[:, 0:size])
    )
    pull_hi, pull_lo = cut(
        jnp.concatenate([pulls_near[...].reshape(32, size), inner_pull], axis=0)
    )
    pull_cat = jnp.concatenate([pull_hi, pull_hi, pull_lo], axis=1)

    q1 = r - operate(t, 1)
    g = gathered(0)
    r = q1 - mm3(loss_cut, g)
    s = smooth(r)
    products = mm(pull_cat, stacked(s))
    for side in range(4):
        pushed[side] = products[8 * side : 8 * side + 8]
    for (here, _), copy in zip(sides, push_copies()):
        pl.when(here)(copy.start)
    put(s, 2)
    halo_start(2)
    mine_now = mm(own_cat, stacked(r)) - products[32:40]
    precond = first + t + mm3(gain_cut, g) + s
    from_sides(pulled, push_recv)
    publish(mine_now - ((pulled[0] + pulled[1]) + (pulled[2] + pulled[3])), 1)
    r = r - operate(s, 2)
    t = smooth(r)
    put(t, 3)
    halo_start(3)
    precond = precond + t
    q2 = r - operate(t, 3)
    base = b - q2
    g = gathered(1)
    precond = precond + mm3(gain_cut, g)
    image = base + mm3(loss_cut, g)
    sums[...] = jnp.concatenate(
        [
            jnp.sum(b * precond, axis=0, keepdims=True),
            jnp.sum(precond * image, axis=0, keepdims=True),
            jnp.zeros((6, cases), jnp.float32),
        ],
        axis=0,
    )
    pairs = sums_all.at[:, 0:2]
    to_all(sums.at[0:2], pairs, 2)
    sums_all[pl.ds(me, 1)] = sums[...][None]
    for k in range(4):
        for (here, _), copy in zip(sides, halo_copies(k)):
            pl.when(here)(copy.wait_send)
    for (here, _), copy in zip(sides, near_copies()):
        pl.when(here)(copy.wait_send)
    for copies in (relaxed_copies(), pulls_copies(), push_copies()):
        for (here, _), copy in zip(sides, copies):
            pl.when(here)(copy.wait_send)
    for copy in at_column(told, told_all):
        copy.wait_send()
    for mx in plane:
        plane_copy(mx).wait_send()
    wait_many(told_all, nx // 2 * ny, pair_send)
    for k in range(2):
        wait_many(theirs_all(k), n - 1, direct_send.at[k])
    wait_many(pairs, n - 1, direct_recv.at[2])
    total = jnp.sum(sums_all[:, 0:2], axis=0)
    alpha = total[0:1] / total[1:2]
    solution_ref[...] = (alpha * precond).reshape(rows, cols, blk, cases)
    residual_ref[...] = (b - alpha * image).reshape(rows, cols, blk, cases)
    wait_many(pairs, n - 1, direct_send.at[2])


def finish_kernel(s_ref, r_ref, sol_ref, res_ref, sems):
    copies = [
        pltpu.make_async_copy(src, dst, sems.at[k])
        for k, (src, dst) in enumerate(((s_ref, sol_ref), (r_ref, res_ref)))
    ]
    for copy in copies:
        copy.start()
    for copy in copies:
        copy.wait()


def fused(
    nx, ny,
    load_cases, matrix_tiles, block_cols, smoother_blocks, near_null, coarse_map, coarse_inverse
):
    rows, cols, blk, cases = load_cases.shape
    count = rows * cols
    modes = near_null.shape[2] // blk
    n = nx * ny
    width = -(-coarse_inverse.shape[1] // 128) * 128
    block_cols = jnp.transpose(block_cols, (1, 0, 2))
    smoother_blocks = jnp.transpose(smoother_blocks, (1, 0, 2))
    near_null = jnp.transpose(near_null, (1, 0, 2))
    vmem = pl.BlockSpec(memory_space=pltpu.VMEM)
    hbm = pl.BlockSpec(memory_space=pltpu.HBM)
    f32, bf16 = jnp.float32, jnp.bfloat16
    shape = jax.ShapeDtypeStruct(load_cases.shape, f32)
    held = pltpu.VMEM(load_cases.shape, f32)
    solved, residual = pl.pallas_call(
        functools.partial(step_kernel, nx, ny, modes),
        out_shape=(held, held),
        in_specs=[hbm] * 7,
        out_specs=(vmem, vmem),
        scratch_shapes=[
            pltpu.VMEM(load_cases.shape, f32),
            pltpu.VMEM(matrix_tiles.shape, f32),
            pltpu.SMEM(block_cols.shape, jnp.int32),
            pltpu.VMEM(smoother_blocks.shape, f32),
            pltpu.VMEM(near_null.shape, f32),
            pltpu.SMEM(coarse_map.shape, jnp.int32),
            pltpu.VMEM(coarse_inverse.shape, f32),
            pltpu.SemaphoreType.DMA((7,)),
            pltpu.VMEM((count, 2, blk, 128), f32),
            pltpu.VMEM((8, count * blk), f32),
            pltpu.VMEM((4, rows, cols, blk, cases), f32),
            pltpu.VMEM((4, cols, blk, cases), f32),
            pltpu.VMEM((4, cols, blk, cases), f32),
            pltpu.VMEM((4, rows, blk, cases), f32),
            pltpu.VMEM((4, rows, blk, cases), f32),
            pltpu.VMEM((count * blk, 3 * count * blk), bf16),
            pltpu.VMEM((2 * (rows + cols), blk, 3 * blk), bf16),
            pltpu.VMEM((count, blk, 3 * blk), bf16),
            pltpu.VMEM((8, width), f32),
            pltpu.VMEM((n, 8, width), f32),
            pltpu.VMEM((4, 8, count * blk), f32),
            pltpu.VMEM((2, 8, cases), f32),
            pltpu.VMEM((2, n, 8, cases), f32),
            pltpu.VMEM((8, cases), f32),
            pltpu.VMEM((n, 8, cases), f32),
            pltpu.VMEM((40, count * blk), f32),
            pltpu.VMEM((40, count * blk), f32),
            pltpu.VMEM((4, 40, count * blk), f32),
            pltpu.VMEM((256, count * blk), f32),
            pltpu.VMEM((2, n * 8, n * 8), f32),
            pltpu.VMEM((4, 8, count * blk), f32),
            pltpu.VMEM((4, 8, count * blk), f32),
            pltpu.VMEM((4, 8, cases), f32),
            pltpu.VMEM((4, 8, cases), f32),
            pltpu.SemaphoreType.DMA((4, 4)),
            pltpu.SemaphoreType.DMA((4, 4)),
            pltpu.SemaphoreType.DMA((4,)),
            pltpu.SemaphoreType.DMA((4,)),
            pltpu.SemaphoreType.DMA((4,)),
            pltpu.SemaphoreType.DMA((4,)),
            pltpu.SemaphoreType.DMA((4,)),
            pltpu.SemaphoreType.DMA((4,)),
            pltpu.SemaphoreType.DMA((4,)),
            pltpu.SemaphoreType.DMA((4,)),
            pltpu.SemaphoreType.DMA((ny,)),
            pltpu.SemaphoreType.DMA((ny,)),
            pltpu.SemaphoreType.DMA((nx // 2,)),
            pltpu.SemaphoreType.DMA((nx // 2,)),
            pltpu.SemaphoreType.DMA,
            pltpu.SemaphoreType.DMA,
            pltpu.SemaphoreType.DMA((3,)),
            pltpu.SemaphoreType.DMA((3,)),
            pltpu.SemaphoreType.REGULAR,
        ],
        compiler_params=pltpu.CompilerParams(
            collective_id=0, has_side_effects=True, vmem_limit_bytes=32 * 2**20
        ),
    )(
        *(
            pltpu.with_memory_space_constraint(v, pltpu.HBM)
            for v in (
                load_cases, matrix_tiles, block_cols, smoother_blocks, near_null, coarse_map,
                coarse_inverse,
            )
        )
    )
    return pl.pallas_call(
        finish_kernel,
        out_shape=(shape, shape),
        in_specs=[vmem, vmem],
        out_specs=(hbm, hbm),
        scratch_shapes=[pltpu.SemaphoreType.DMA((2,))],
        compiler_params=pltpu.CompilerParams(vmem_limit_bytes=32 * 2**20),
    )(
        *(pltpu.with_memory_space_constraint(v, pltpu.VMEM) for v in (solved, residual))
    )


def per_device(
    load_cases, matrix_tiles, block_cols, smoother_blocks, near_null, coarse_map, coarse_inverse
):
    agg_rows, agg_cols, block_size, case_count = load_cases.shape
    mode_count = near_null.shape[2] // block_size
    coarse_total = coarse_inverse.shape[1]
    coarse_aggs = coarse_total // mode_count
    modes = near_null.reshape(agg_rows, agg_cols, mode_count, block_size)
    inverse_blocks = smoother_blocks.reshape(agg_rows, agg_cols, block_size, block_size)

    steps = ((0, 0), (-1, 0), (1, 0), (0, -1), (0, 1))
    tiles = matrix_tiles.reshape(agg_rows, agg_cols, block_size, -1, block_size)
    row_at = jnp.arange(agg_rows, dtype=jnp.int32)[:, None, None]
    col_at = jnp.arange(agg_cols, dtype=jnp.int32)[None, :, None]
    stencil = []
    for dx, dy in steps:
        named = block_cols == (row_at + 1 + dx) * (agg_cols + 2) + col_at + 1 + dy
        stencil.append(jnp.sum(jnp.where(named[:, :, None, :, None], tiles, 0.0), axis=3))

    def operate(vector_field):
        extended = padded(vector_field, (("gx", 0), ("gy", 1)), 1)
        total = 0.0
        for tile, (dx, dy) in zip(stencil, steps):
            cells = extended[1 + dx : 1 + dx + agg_rows, 1 + dy : 1 + dy + agg_cols]
            total = total + jnp.einsum("ijbk,ijkr->ijbr", tile, cells, precision=highest)
        return total

    def smooth(defect):
        return relax_weight * jnp.einsum(
            "ijab,ijbr->ijar", inverse_blocks, defect, precision=highest
        )

    def correct(defect):
        contrib = jnp.einsum("ijkb,ijbr->ijkr", modes, defect, precision=highest)
        own_part = jnp.sum(contrib, axis=(0, 1))
        my_label = coarse_map[0, 0]
        label_value = jnp.reshape(my_label.astype(jnp.float32), (1,))
        pieces, labels = (
            lax.all_gather(own_part[None], ("gx", "gy"), axis=0, tiled=True),
            lax.all_gather(label_value, ("gx", "gy"), axis=0, tiled=True),
        )
        label_ids = labels.astype(jnp.int32)
        placing = (label_ids[:, None] == jnp.arange(coarse_aggs, dtype=jnp.int32)[None, :]).astype(
            jnp.float32
        )
        ordered = jnp.einsum("dc,dkr->ckr", placing, pieces, precision=highest).reshape(
            coarse_total, case_count
        )
        own_rows = jnp.dot(coarse_inverse, ordered, precision=highest)
        solved = lax.all_gather(own_rows, ("gx", "gy"), axis=0, tiled=True)
        mine = lax.dynamic_slice_in_dim(solved, my_label * mode_count, mode_count, 0)
        coarse_back = jnp.broadcast_to(
            mine[None, None], (agg_rows, agg_cols, mode_count, case_count)
        )
        return jnp.einsum("ijkb,ijkr->ijbr", modes, coarse_back, precision=highest)

    first = smooth(load_cases)
    first = first + correct(load_cases - operate(first))
    precond = first + smooth(load_cases - operate(first))
    defect = load_cases - operate(precond)
    update = smooth(defect)
    update = update + correct(defect - operate(update))
    update = update + smooth(defect - operate(update))
    precond = precond + update
    local_aligned = jnp.sum(load_cases * precond, axis=(0, 1, 2))
    aligned = lax.psum(local_aligned, ("gx", "gy"))
    image = operate(precond)
    curved = lax.psum(jnp.sum(precond * image, axis=(0, 1, 2)), ("gx", "gy"))
    alpha = aligned / curved
    solution = alpha * precond
    residual = load_cases - alpha * image
    return (solution, residual)


def solution(mesh):
    nx, ny = mesh.shape["gx"], mesh.shape["gy"]
    step = functools.partial(fused, nx, ny) if nx * ny <= 128 else per_device
    placed = (
        P("gx", "gy", None, None),
        P("gx", "gy", None, None),
        P("gx", "gy", None),
        P("gx", "gy", None),
        P("gx", "gy", None),
        P("gx", "gy"),
        P(("gx", "gy"), None),
    )
    return jax.shard_map(
        step,
        mesh=mesh,
        in_specs=placed,
        out_specs=(P("gx", "gy", None, None), P("gx", "gy", None, None)),
        check_vma=False,
    )
```

```python
import functools

import jax
import jax.numpy as jnp
from jax import lax
from jax.experimental import pallas as pl
from jax.experimental.pallas import tpu as pltpu
from jax.sharding import PartitionSpec as P

relax_weight = 0.8
highest = lax.Precision.HIGHEST


def padded(cells, sides, width):
    for axis, dim in sides:
        count = lax.axis_size(axis)
        ends = count - 1
        head = lax.slice_in_dim(cells, 0, width, axis=dim)
        tail = lax.slice_in_dim(cells, cells.shape[dim] - width, cells.shape[dim], axis=dim)
        cells = jnp.concatenate(
            [
                lax.ppermute(tail, axis, [(i, (i + 1) % count) for i in range(ends)]),
                cells,
                lax.ppermute(head, axis, [((i + 1) % count, i) for i in range(ends)]),
            ],
            axis=dim,
        )
    return cells


def cut(v):
    hi = v.astype(jnp.bfloat16)
    return hi, (v - hi.astype(jnp.float32)).astype(jnp.bfloat16)


def stacked(v):
    hi, lo = cut(v)
    return jnp.concatenate([hi, lo, hi], axis=0)


def mm(a, b):
    return lax.dot_general(a, b, (((1,), (0,)), ((), ())), preferred_element_type=jnp.float32)


def mm_t(a, b, precision=None):
    return lax.dot_general(
        a, b, (((1,), (1,)), ((), ())), precision=precision, preferred_element_type=jnp.float32
    )


def mm3(a_cut, b):
    hi, lo = cut(b)
    return mm(a_cut[0], hi) + (mm(a_cut[0], lo) + mm(a_cut[1], hi))


def flipped(v, mask):
    bit = 1
    while bit <= mask:
        if mask & bit:
            v = v + bit - 2 * bit * lax.rem(v // bit, 2)
        bit *= 2
    return v


def far_first(nx, ny):
    def hops(pair):
        mx, my = pair
        return bin(mx >> 1).count("1") + my + 0.1 * (mx & 1)

    pairs = [(mx, my) for mx in range(nx) for my in range(ny) if mx or my]
    return sorted(pairs, key=hops, reverse=True)


def step_kernel(
    nx, ny, modes,
    b_hbm, a_hbm, cols_hbm, s_hbm, n_hbm, map_hbm, inv_hbm,
    solution_ref, residual_ref,
    b_ref, a_ref, cols_ref, s_ref, n_ref, map_ref, inv_ref, loaded,
    blocks, nulls, field, up, down, left, right, local, edge, smoother, info, info_all, near, coarse, coarse_all,
    sums, sums_all, spread, relaxed, relaxed_near, reach, solved, pulls, pulls_near, pushed, pulled,
    halo_send, halo_recv, near_send, near_recv, relaxed_send, relaxed_recv, pulls_send, pulls_recv, push_send, push_recv, col_send, col_recv,
    plane_send, plane_recv, pair_send, pair_recv, direct_send, direct_recv, entered,
):
    rows, cols, blk, cases = b_ref.shape
    count = rows * cols
    size = count * blk
    n = nx * ny
    width = info.shape[1]
    coarse_rows = n * 8
    around = spread.shape[0]
    x, y = lax.axis_index("gx"), lax.axis_index("gy")
    me = x * ny + y
    sides = (
        (x > 0, (x - 1, y)),
        (x < nx - 1, (x + 1, y)),
        (y > 0, (x, y - 1)),
        (y < ny - 1, (x, y + 1)),
    )
    halos = (up, down, left, right)
    order_of_peers = far_first(nx, ny)
    peers_x = [flipped(x, m) for m in range(nx)]
    peers_y = [flipped(y, m) for m in range(ny)]
    barrier = pltpu.get_barrier_semaphore()

    loads = [
        pltpu.make_async_copy(src, dst, loaded.at[i])
        for i, (src, dst) in enumerate(
            (
                (s_hbm, s_ref), (b_hbm, b_ref), (n_hbm, n_ref), (inv_hbm, inv_ref),
                (map_hbm, map_ref), (cols_hbm, cols_ref), (a_hbm, a_ref),
            )
        )
    ]
    for load in loads:
        load.start()

    coarse_all[...] = jnp.zeros_like(coarse_all)
    info_all[...] = jnp.zeros_like(info_all)

    lines = [pair for pair in order_of_peers if 0 in pair]
    for mx, my in lines:
        pl.semaphore_signal(
            barrier, inc=1, device_id=(peers_x[mx], peers_y[my]),
            device_id_type=pl.DeviceIdType.MESH,
        )

    spread[...] = jnp.zeros_like(spread)
    reach[...] = jnp.zeros_like(reach)
    pulls[...] = jnp.zeros_like(pulls)
    nulls[...] = jnp.zeros_like(nulls)
    info[...] = jnp.zeros_like(info)
    local[...] = jnp.zeros_like(local)
    for side, (here, _) in enumerate(sides):

        @pl.when(jnp.logical_not(here))
        def _():
            halos[side][...] = jnp.zeros_like(halos[side])
            near[side] = jnp.zeros_like(near[side])
            relaxed_near[side] = jnp.zeros_like(relaxed_near[side])
            pulls_near[side] = jnp.zeros_like(pulls_near[side])
            pulled[side] = jnp.zeros_like(pulled[side])

    told, told_all = info.at[0 : modes + 1], info_all.at[:, 0 : modes + 1]

    def at_column(src, dst):
        return [
            pltpu.make_async_remote_copy(
                src_ref=src, dst_ref=dst.at[me], send_sem=col_send.at[j],
                recv_sem=col_recv.at[ny - j],
                device_id=(x, lax.rem(y + j, ny)), device_id_type=pl.DeviceIdType.MESH,
            )
            for j in range(1, ny)
        ]

    def block(mx):
        return info_all.at[pl.ds(peers_x[mx] * ny, ny), 0 : modes + 1]

    def plane_copy(mx):
        return pltpu.make_async_remote_copy(
            src_ref=block(0), dst_ref=block(0), send_sem=plane_send.at[mx // 2],
            recv_sem=plane_recv.at[mx // 2], device_id=(peers_x[mx], y),
            device_id_type=pl.DeviceIdType.MESH,
        )

    def to_sibling(mx):
        pltpu.make_async_remote_copy(
            src_ref=block(mx), dst_ref=block(mx), send_sem=pair_send, recv_sem=pair_recv,
            device_id=(peers_x[1], y), device_id_type=pl.DeviceIdType.MESH,
        ).start()

    plane = (*range(nx - 2, 0, -2),)

    def told_pass():
        for j in range(1, ny):
            pltpu.make_async_copy(told, told, col_recv.at[j]).wait()
        for mx in plane:
            plane_copy(mx).start()
        to_sibling(0)

    def told_share():
        for mx in plane[::-1]:
            pltpu.make_async_copy(block(mx), block(mx), plane_recv.at[mx // 2]).wait()
            to_sibling(mx)

    def wait_many(dst, tiles, sem):
        some = dst.at[pl.ds(0, tiles)]
        pltpu.make_async_copy(some, some, sem).wait()

    def to_all(src, dst, k):
        for mx, my in order_of_peers:
            pltpu.make_async_remote_copy(
                src_ref=src, dst_ref=dst.at[me], send_sem=direct_send.at[k],
                recv_sem=direct_recv.at[k], device_id=(peers_x[mx], peers_y[my]),
                device_id_type=pl.DeviceIdType.MESH,
            ).start()

    def halo_copies(k):
        now = field.at[k]
        out = (
            (now.at[0], down.at[k], 1),
            (now.at[rows - 1], up.at[k], 0),
            (now.at[:, 0], right.at[k], 3),
            (now.at[:, cols - 1], left.at[k], 2),
        )
        return [
            pltpu.make_async_remote_copy(
                src_ref=src, dst_ref=dst,
                send_sem=halo_send.at[k, side], recv_sem=halo_recv.at[k, lands],
                device_id=peer, device_id_type=pl.DeviceIdType.MESH,
            )
            for side, ((src, dst, lands), (_, peer)) in enumerate(zip(out, sides))
        ]

    def halo_start(k):
        for (here, _), copy in zip(sides, halo_copies(k)):
            pl.when(here)(copy.start)

    def halo_wait(k, side):
        buf = halos[side].at[k]
        pl.when(sides[side][0])(pltpu.make_async_copy(buf, buf, halo_recv.at[k, side]).wait)

    def to_sides(src, dst, send, recv, split=False):
        return [
            pltpu.make_async_remote_copy(
                src_ref=src.at[side] if split else src, dst_ref=dst.at[lands],
                send_sem=send.at[side], recv_sem=recv.at[lands],
                device_id=peer, device_id_type=pl.DeviceIdType.MESH,
            )
            for side, (lands, (_, peer)) in enumerate(zip((1, 0, 3, 2), sides))
        ]

    def near_copies():
        return to_sides(nulls, near, near_send, near_recv)

    def relaxed_copies():
        return to_sides(relaxed, relaxed_near, relaxed_send, relaxed_recv)

    def pulls_copies():
        return to_sides(pulls, pulls_near, pulls_send, pulls_recv, split=True)

    def push_copies():
        return to_sides(pushed, pulled, push_send, push_recv, split=True)

    def from_sides(dst, recv):
        for side, (here, _) in enumerate(sides):
            buf = dst.at[side]
            pl.when(here)(pltpu.make_async_copy(buf, buf, recv.at[side]).wait)

    loads[0].wait()
    for i in range(rows):
        for j in range(cols):
            p = i * cols + j
            for c in range(0, blk * blk, 128):
                blocks[p, 0, c // 128 : c // 128 + 1] = s_ref[j, i : i + 1, c : c + 128]
            flat = blocks[p, 0, 0 : blk * blk // 128]
            for half in range(128 // blk):
                blocks[p, 1, pl.ds(half, blk * blk // 128, stride=128 // blk), 0:blk] = flat[
                    :, half * blk : (half + 1) * blk
                ]
    for p in range(count):
        hi, lo = cut(relax_weight * blocks[p, 1, :, 0:blk])
        smoother[p] = jnp.concatenate([hi, hi, lo], axis=1)

    def smooth(v):
        return jnp.concatenate(
            [mm(smoother[p], stacked(v[p * blk : (p + 1) * blk])) for p in range(count)], axis=0
        )

    def put(v, k):
        field[k] = v.reshape(rows, cols, blk, cases)

    loads[1].wait()
    b = b_ref[...].reshape(size, cases)
    first = smooth(b)
    put(first, 0)

    for load in loads[2:5]:
        load.wait()
    for i in range(rows):
        for j in range(cols):
            p = i * cols + j
            for k in range(modes):
                nulls[k : k + 1, p * blk : (p + 1) * blk] = n_ref[
                    j, i : i + 1, k * blk : (k + 1) * blk
                ]
    info[0:modes, 0 : inv_ref.shape[1]] = inv_ref[...]
    info[modes : modes + 1, :] = jnp.full((1, width), map_ref[0, 0].astype(jnp.float32))

    pl.semaphore_wait(barrier, len(lines))
    for (here, _), copy in zip(sides, near_copies()):
        pl.when(here)(copy.start)
    for copy in at_column(told, told_all):
        copy.start()
    halo_start(0)
    for mx in range(1, nx):
        pl.semaphore_signal(
            entered, inc=1, device_id=(peers_x[mx], y), device_id_type=pl.DeviceIdType.MESH
        )
    info_all[pl.ds(me, 1)] = info[...][None]

    loads[5].wait()
    loads[6].wait()
    for i in range(rows):
        for j in range(cols):
            p = i * cols + j
            tiles = [a_ref[i, j, :, s * blk : (s + 1) * blk] for s in range(5)]
            names = [cols_ref[j, i, s] for s in range(5)]
            for d, (di, dj) in enumerate(((0, 0), (-1, 0), (1, 0), (0, -1), (0, 1))):
                e = (i + 1 + di) * (cols + 2) + j + 1 + dj
                tile = tiles[0] * (names[0] == e).astype(jnp.float32)
                for s in range(1, 5):
                    tile = tile + tiles[s] * (names[s] == e).astype(jnp.float32)
                hi, lo = cut(tile)
                ii, jj = i + di, j + dj
                if 0 <= ii < rows and 0 <= jj < cols:
                    q = ii * cols + jj
                    for k, part in enumerate((hi, hi, lo)):
                        at = k * size + q * blk
                        local[p * blk : (p + 1) * blk, at : at + blk] = part
                else:
                    at = (0, j, cols + j, 2 * cols + i, 2 * cols + rows + i)[d]
                    edge[at] = jnp.concatenate([hi, hi, lo], axis=1)

    def places():
        for j in range(cols):
            yield 0, j, j, j
        for j in range(cols):
            yield 1, j, cols + j, (rows - 1) * cols + j
        for i in range(rows):
            yield 2, i, 2 * cols + i, i * cols
        for i in range(rows):
            yield 3, i, 2 * cols + rows + i, i * cols + cols - 1

    def own_part(v):
        return mm(local[...], stacked(v))

    def operate(v, k):
        return beyond(own_part(v), k)

    def beyond(inner, k):
        parts = [inner[p * blk : (p + 1) * blk] for p in range(count)]
        for side in (2, 3, 0, 1):
            halo_wait(k, side)
            for at_side, at, e, p in places():
                if at_side == side:
                    parts[p] = parts[p] + mm(edge[e], stacked(halos[side][k, at]))
        return jnp.concatenate(parts, axis=0)

    own_n = nulls[...]
    own_hi, own_lo = cut(own_n)
    own_cat = jnp.concatenate([own_hi, own_hi, own_lo], axis=1)

    def mine(k):
        return coarse.at[k, 0:modes]

    def theirs_all(k):
        return coarse_all.at[k, :, 0:modes]

    def publish(g, k):
        coarse[k] = g
        to_all(mine(k), theirs_all(k), k)
        coarse_all[k, pl.ds(me, 1)] = g[None]

    def gathered(k):
        wait_many(theirs_all(k), n - 1, direct_recv.at[k])
        return coarse_all[k].reshape(coarse_rows, cases)

    def across(v):
        hi, lo = cut(v)
        return jnp.concatenate([hi, lo, hi], axis=1)

    facing = (
        lambda at: (rows - 1) * cols + at,
        lambda at: at,
        lambda at: at * cols + cols - 1,
        lambda at: at * cols,
    )
    spread[0:8] = mm_t(across(own_n), local[...])
    from_sides(near, near_recv)
    for side, at, e, p in places():
        q = facing[side](at)
        spread[8 * (1 + side) : 8 * (2 + side), p * blk : (p + 1) * blk] = mm_t(
            across(near[side, :, q * blk : (q + 1) * blk]), edge[e]
        )
    for p in range(count):
        relaxed[:, p * blk : (p + 1) * blk] = mm_t(
            across(spread[:, p * blk : (p + 1) * blk]), smoother[p]
        )
    for (here, _), copy in zip(sides, relaxed_copies()):
        pl.when(here)(copy.start)
    told_pass()

    reach[0:around] = spread[...] - mm_t(across(relaxed[...]), local[...])
    eye = (
        lax.broadcasted_iota(jnp.int32, (size, size), 0)
        == lax.broadcasted_iota(jnp.int32, (size, size), 1)
    ).astype(jnp.float32).astype(jnp.bfloat16)

    def turned(v):
        return tuple(mm_t(eye, part).astype(jnp.bfloat16) for part in cut(v))

    gain = turned(
        jnp.concatenate([own_n - relaxed[0:8], 0.0 - relaxed[8:around]], axis=0)
    )
    for side, at, e, p in places():
        q = facing[side](at)
        hi, lo = own_hi[:, p * blk : (p + 1) * blk], own_lo[:, p * blk : (p + 1) * blk]
        tile, rest = edge[e, :, 0:blk], edge[e, :, 2 * blk : 3 * blk]
        pulls[side, :, q * blk : (q + 1) * blk] = mm(hi, tile) + (mm(hi, rest) + mm(lo, tile))
    for (here, _), copy in zip(sides, pulls_copies()):
        pl.when(here)(copy.start)

    r = b - operate(first, 0)
    pl.semaphore_wait(entered, nx - 1)
    publish(mm(own_cat, stacked(r)), 0)
    t = smooth(r)
    put(t, 1)
    halo_start(1)
    told_share()

    from_sides(relaxed_near, relaxed_recv)
    for side, at, e, p in places():
        q = facing[side](at)
        reach[around * (1 + side) : around * (2 + side), p * blk : (p + 1) * blk] = 0.0 - mm_t(
            across(relaxed_near[side, :, q * blk : (q + 1) * blk]), edge[e]
        )
    reach_turned = turned(reach[...])
    wait_many(told_all, nx // 2 * ny, pair_recv)
    inv_parts = cut(info_all[...].reshape(coarse_rows, width))
    lane3 = lax.broadcasted_iota(jnp.int32, (n, 8, width), 2).astype(jnp.float32)
    row3 = lax.broadcasted_iota(jnp.int32, (n, 8, width), 1)
    labels = jnp.broadcast_to(info_all[...][:, modes : modes + 1, :], (n, 8, width))
    where3 = labels * float(modes) + row3.astype(jnp.float32)
    order = jnp.where(lane3 == where3, 1.0, 0.0)
    order = jnp.where(row3 < modes, order, 0.0).reshape(coarse_rows, width).astype(jnp.bfloat16)
    lane4 = lax.broadcasted_iota(jnp.int32, (n, 8, coarse_rows), 2).astype(jnp.float32)
    row4 = lax.broadcasted_iota(jnp.int32, (n, 8, coarse_rows), 1)
    labels4 = jnp.broadcast_to(info_all[...][:, modes : modes + 1, 0:1], (n, 8, coarse_rows))
    pick = jnp.where(lane4 == labels4 * 8.0 + row4.astype(jnp.float32), 1.0, 0.0)
    pick = jnp.where(row4 < modes, pick, 0.0).reshape(coarse_rows, coarse_rows).astype(jnp.bfloat16)
    for k, part in enumerate(inv_parts):
        solved[k] = mm_t(mm(pick, part).astype(jnp.bfloat16), order)

    def clipped(px, py):
        return jnp.clip(px, 0, nx - 1) * ny + jnp.clip(py, 0, ny - 1)

    def cross(px, py):
        return [
            clipped(px + dx, py + dy)
            for dx, dy in ((0, 0), (-1, 0), (1, 0), (0, -1), (0, 1))
        ]

    ids = cross(x, y)
    for _, (px, py) in sides:
        ids = ids + cross(px, py)
    lacking = jnp.zeros((reach.shape[0] - 8 * len(ids), coarse_rows), jnp.float32)
    solve = tuple(
        jnp.concatenate(
            [solved[k, pl.ds(pl.multiple_of(d * 8, 8), 8)] for d in ids] + [lacking], axis=0
        ).astype(jnp.bfloat16)
        for k in range(2)
    )

    def mm3_cut(a_cut, b_cut):
        return mm(a_cut[0], b_cut[0]) + (mm(a_cut[0], b_cut[1]) + mm(a_cut[1], b_cut[0]))

    gain_cut = cut(mm3_cut(gain, tuple(part[0:around] for part in solve)))

    loss_cut = cut(mm3_cut(reach_turned, solve))

    from_sides(pulls_near, pulls_recv)
    inner_pull = mm(own_hi, local[:, 0:size]) + (
        mm(own_hi, local[:, 2 * size : 3 * size]) + mm(own_lo, local[:, 0:size])
    )
    pull_hi, pull_lo = cut(
        jnp.concatenate([pulls_near[...].reshape(32, size), inner_pull], axis=0)
    )
    pull_cat = jnp.concatenate([pull_hi, pull_hi, pull_lo], axis=1)

    q1 = r - operate(t, 1)
    g = gathered(0)
    r = q1 - mm3(loss_cut, g)
    s = smooth(r)
    products = mm(pull_cat, stacked(s))
    for side in range(4):
        pushed[side] = products[8 * side : 8 * side + 8]
    for (here, _), copy in zip(sides, push_copies()):
        pl.when(here)(copy.start)
    put(s, 2)
    halo_start(2)
    mine_now = mm(own_cat, stacked(r)) - products[32:40]
    precond = first + t + mm3(gain_cut, g) + s
    from_sides(pulled, push_recv)
    publish(mine_now - ((pulled[0] + pulled[1]) + (pulled[2] + pulled[3])), 1)
    r = r - operate(s, 2)
    t = smooth(r)
    put(t, 3)
    halo_start(3)
    precond = precond + t
    inner = (b - r) + own_part(t)
    g = gathered(1)
    precond = precond + mm3(gain_cut, g)
    aligned = jnp.sum(b * precond, axis=0, keepdims=True)
    image = beyond(inner + mm3(loss_cut, g), 3)
    sums[...] = jnp.concatenate(
        [
            aligned,
            jnp.sum(precond * image, axis=0, keepdims=True),
            jnp.zeros((6, cases), jnp.float32),
        ],
        axis=0,
    )
    pairs = sums_all.at[:, 0:2]
    to_all(sums.at[0:2], pairs, 2)
    sums_all[pl.ds(me, 1)] = sums[...][None]
    for k in range(4):
        for (here, _), copy in zip(sides, halo_copies(k)):
            pl.when(here)(copy.wait_send)
    for (here, _), copy in zip(sides, near_copies()):
        pl.when(here)(copy.wait_send)
    for copies in (relaxed_copies(), pulls_copies(), push_copies()):
        for (here, _), copy in zip(sides, copies):
            pl.when(here)(copy.wait_send)
    for copy in at_column(told, told_all):
        copy.wait_send()
    for mx in plane:
        plane_copy(mx).wait_send()
    wait_many(told_all, nx // 2 * ny, pair_send)
    for k in range(2):
        wait_many(theirs_all(k), n - 1, direct_send.at[k])
    wait_many(pairs, n - 1, direct_recv.at[2])
    total = jnp.sum(sums_all[:, 0:2], axis=0)
    alpha = total[0:1] / total[1:2]
    solution_ref[...] = (alpha * precond).reshape(rows, cols, blk, cases)
    residual_ref[...] = (b - alpha * image).reshape(rows, cols, blk, cases)
    wait_many(pairs, n - 1, direct_send.at[2])


def finish_kernel(s_ref, r_ref, sol_ref, res_ref, sems):
    copies = [
        pltpu.make_async_copy(src, dst, sems.at[k])
        for k, (src, dst) in enumerate(((s_ref, sol_ref), (r_ref, res_ref)))
    ]
    for copy in copies:
        copy.start()
    for copy in copies:
        copy.wait()


def fused(
    nx, ny,
    load_cases, matrix_tiles, block_cols, smoother_blocks, near_null, coarse_map, coarse_inverse
):
    rows, cols, blk, cases = load_cases.shape
    count = rows * cols
    modes = near_null.shape[2] // blk
    n = nx * ny
    width = -(-coarse_inverse.shape[1] // 128) * 128
    block_cols = jnp.transpose(block_cols, (1, 0, 2))
    smoother_blocks = jnp.transpose(smoother_blocks, (1, 0, 2))
    near_null = jnp.transpose(near_null, (1, 0, 2))
    vmem = pl.BlockSpec(memory_space=pltpu.VMEM)
    hbm = pl.BlockSpec(memory_space=pltpu.HBM)
    f32, bf16 = jnp.float32, jnp.bfloat16
    shape = jax.ShapeDtypeStruct(load_cases.shape, f32)
    held = pltpu.VMEM(load_cases.shape, f32)
    solved, residual = pl.pallas_call(
        functools.partial(step_kernel, nx, ny, modes),
        out_shape=(held, held),
        in_specs=[hbm] * 7,
        out_specs=(vmem, vmem),
        scratch_shapes=[
            pltpu.VMEM(load_cases.shape, f32),
            pltpu.VMEM(matrix_tiles.shape, f32),
            pltpu.SMEM(block_cols.shape, jnp.int32),
            pltpu.VMEM(smoother_blocks.shape, f32),
            pltpu.VMEM(near_null.shape, f32),
            pltpu.SMEM(coarse_map.shape, jnp.int32),
            pltpu.VMEM(coarse_inverse.shape, f32),
            pltpu.SemaphoreType.DMA((7,)),
            pltpu.VMEM((count, 2, blk, 128), f32),
            pltpu.VMEM((8, count * blk), f32),
            pltpu.VMEM((4, rows, cols, blk, cases), f32),
            pltpu.VMEM((4, cols, blk, cases), f32),
            pltpu.VMEM((4, cols, blk, cases), f32),
            pltpu.VMEM((4, rows, blk, cases), f32),
            pltpu.VMEM((4, rows, blk, cases), f32),
            pltpu.VMEM((count * blk, 3 * count * blk), bf16),
            pltpu.VMEM((2 * (rows + cols), blk, 3 * blk), bf16),
            pltpu.VMEM((count, blk, 3 * blk), bf16),
            pltpu.VMEM((8, width), f32),
            pltpu.VMEM((n, 8, width), f32),
            pltpu.VMEM((4, 8, count * blk), f32),
            pltpu.VMEM((2, 8, cases), f32),
            pltpu.VMEM((2, n, 8, cases), f32),
            pltpu.VMEM((8, cases), f32),
            pltpu.VMEM((n, 8, cases), f32),
            pltpu.VMEM((40, count * blk), f32),
            pltpu.VMEM((40, count * blk), f32),
            pltpu.VMEM((4, 40, count * blk), f32),
            pltpu.VMEM((256, count * blk), f32),
            pltpu.VMEM((2, n * 8, n * 8), f32),
            pltpu.VMEM((4, 8, count * blk), f32),
            pltpu.VMEM((4, 8, count * blk), f32),
            pltpu.VMEM((4, 8, cases), f32),
            pltpu.VMEM((4, 8, cases), f32),
            pltpu.SemaphoreType.DMA((4, 4)),
            pltpu.SemaphoreType.DMA((4, 4)),
            pltpu.SemaphoreType.DMA((4,)),
            pltpu.SemaphoreType.DMA((4,)),
            pltpu.SemaphoreType.DMA((4,)),
            pltpu.SemaphoreType.DMA((4,)),
            pltpu.SemaphoreType.DMA((4,)),
            pltpu.SemaphoreType.DMA((4,)),
            pltpu.SemaphoreType.DMA((4,)),
            pltpu.SemaphoreType.DMA((4,)),
            pltpu.SemaphoreType.DMA((ny,)),
            pltpu.SemaphoreType.DMA((ny,)),
            pltpu.SemaphoreType.DMA((nx // 2,)),
            pltpu.SemaphoreType.DMA((nx // 2,)),
            pltpu.SemaphoreType.DMA,
            pltpu.SemaphoreType.DMA,
            pltpu.SemaphoreType.DMA((3,)),
            pltpu.SemaphoreType.DMA((3,)),
            pltpu.SemaphoreType.REGULAR,
        ],
        compiler_params=pltpu.CompilerParams(
            collective_id=0, has_side_effects=True, vmem_limit_bytes=32 * 2**20
        ),
    )(
        *(
            pltpu.with_memory_space_constraint(v, pltpu.HBM)
            for v in (
                load_cases, matrix_tiles, block_cols, smoother_blocks, near_null, coarse_map,
                coarse_inverse,
            )
        )
    )
    return pl.pallas_call(
        finish_kernel,
        out_shape=(shape, shape),
        in_specs=[vmem, vmem],
        out_specs=(hbm, hbm),
        scratch_shapes=[pltpu.SemaphoreType.DMA((2,))],
        compiler_params=pltpu.CompilerParams(vmem_limit_bytes=32 * 2**20),
    )(
        *(pltpu.with_memory_space_constraint(v, pltpu.VMEM) for v in (solved, residual))
    )


def per_device(
    load_cases, matrix_tiles, block_cols, smoother_blocks, near_null, coarse_map, coarse_inverse
):
    agg_rows, agg_cols, block_size, case_count = load_cases.shape
    mode_count = near_null.shape[2] // block_size
    coarse_total = coarse_inverse.shape[1]
    coarse_aggs = coarse_total // mode_count
    modes = near_null.reshape(agg_rows, agg_cols, mode_count, block_size)
    inverse_blocks = smoother_blocks.reshape(agg_rows, agg_cols, block_size, block_size)

    steps = ((0, 0), (-1, 0), (1, 0), (0, -1), (0, 1))
    tiles = matrix_tiles.reshape(agg_rows, agg_cols, block_size, -1, block_size)
    row_at = jnp.arange(agg_rows, dtype=jnp.int32)[:, None, None]
    col_at = jnp.arange(agg_cols, dtype=jnp.int32)[None, :, None]
    stencil = []
    for dx, dy in steps:
        named = block_cols == (row_at + 1 + dx) * (agg_cols + 2) + col_at + 1 + dy
        stencil.append(jnp.sum(jnp.where(named[:, :, None, :, None], tiles, 0.0), axis=3))

    def operate(vector_field):
        extended = padded(vector_field, (("gx", 0), ("gy", 1)), 1)
        total = 0.0
        for tile, (dx, dy) in zip(stencil, steps):
            cells = extended[1 + dx : 1 + dx + agg_rows, 1 + dy : 1 + dy + agg_cols]
            total = total + jnp.einsum("ijbk,ijkr->ijbr", tile, cells, precision=highest)
        return total

    def smooth(defect):
        return relax_weight * jnp.einsum(
            "ijab,ijbr->ijar", inverse_blocks, defect, precision=highest
        )

    def correct(defect):
        contrib = jnp.einsum("ijkb,ijbr->ijkr", modes, defect, precision=highest)
        own_part = jnp.sum(contrib, axis=(0, 1))
        my_label = coarse_map[0, 0]
        label_value = jnp.reshape(my_label.astype(jnp.float32), (1,))
        pieces, labels = (
            lax.all_gather(own_part[None], ("gx", "gy"), axis=0, tiled=True),
            lax.all_gather(label_value, ("gx", "gy"), axis=0, tiled=True),
        )
        label_ids = labels.astype(jnp.int32)
        placing = (label_ids[:, None] == jnp.arange(coarse_aggs, dtype=jnp.int32)[None, :]).astype(
            jnp.float32
        )
        ordered = jnp.einsum("dc,dkr->ckr", placing, pieces, precision=highest).reshape(
            coarse_total, case_count
        )
        own_rows = jnp.dot(coarse_inverse, ordered, precision=highest)
        solved = lax.all_gather(own_rows, ("gx", "gy"), axis=0, tiled=True)
        mine = lax.dynamic_slice_in_dim(solved, my_label * mode_count, mode_count, 0)
        coarse_back = jnp.broadcast_to(
            mine[None, None], (agg_rows, agg_cols, mode_count, case_count)
        )
        return jnp.einsum("ijkb,ijkr->ijbr", modes, coarse_back, precision=highest)

    first = smooth(load_cases)
    first = first + correct(load_cases - operate(first))
    precond = first + smooth(load_cases - operate(first))
    defect = load_cases - operate(precond)
    update = smooth(defect)
    update = update + correct(defect - operate(update))
    update = update + smooth(defect - operate(update))
    precond = precond + update
    local_aligned = jnp.sum(load_cases * precond, axis=(0, 1, 2))
    aligned = lax.psum(local_aligned, ("gx", "gy"))
    image = operate(precond)
    curved = lax.psum(jnp.sum(precond * image, axis=(0, 1, 2)), ("gx", "gy"))
    alpha = aligned / curved
    solution = alpha * precond
    residual = load_cases - alpha * image
    return (solution, residual)


def solution(mesh):
    nx, ny = mesh.shape["gx"], mesh.shape["gy"]
    step = functools.partial(fused, nx, ny) if nx * ny <= 128 else per_device
    placed = (
        P("gx", "gy", None, None),
        P("gx", "gy", None, None),
        P("gx", "gy", None),
        P("gx", "gy", None),
        P("gx", "gy", None),
        P("gx", "gy"),
        P(("gx", "gy"), None),
    )
    return jax.shard_map(
        step,
        mesh=mesh,
        in_specs=placed,
        out_specs=(P("gx", "gy", None, None), P("gx", "gy", None, None)),
        check_vma=False,
    )
```

```python
import functools

import jax
import jax.numpy as jnp
from jax import lax
from jax.experimental import pallas as pl
from jax.experimental.pallas import tpu as pltpu
from jax.sharding import PartitionSpec as P

relax_weight = 0.8
highest = lax.Precision.HIGHEST


def padded(cells, sides, width):
    for axis, dim in sides:
        count = lax.axis_size(axis)
        ends = count - 1
        head = lax.slice_in_dim(cells, 0, width, axis=dim)
        tail = lax.slice_in_dim(cells, cells.shape[dim] - width, cells.shape[dim], axis=dim)
        cells = jnp.concatenate(
            [
                lax.ppermute(tail, axis, [(i, (i + 1) % count) for i in range(ends)]),
                cells,
                lax.ppermute(head, axis, [((i + 1) % count, i) for i in range(ends)]),
            ],
            axis=dim,
        )
    return cells


def cut(v):
    hi = v.astype(jnp.bfloat16)
    return hi, (v - hi.astype(jnp.float32)).astype(jnp.bfloat16)


def stacked(v):
    hi, lo = cut(v)
    return jnp.concatenate([hi, lo, hi], axis=0)


def mm(a, b):
    return lax.dot_general(a, b, (((1,), (0,)), ((), ())), preferred_element_type=jnp.float32)


def mm_t(a, b, precision=None):
    return lax.dot_general(
        a, b, (((1,), (1,)), ((), ())), precision=precision, preferred_element_type=jnp.float32
    )


def mm3(a_cut, b):
    hi, lo = cut(b)
    return mm(a_cut[0], hi) + (mm(a_cut[0], lo) + mm(a_cut[1], hi))


def flipped(v, mask):
    bit = 1
    while bit <= mask:
        if mask & bit:
            v = v + bit - 2 * bit * lax.rem(v // bit, 2)
        bit *= 2
    return v


def far_first(nx, ny):
    def hops(pair):
        mx, my = pair
        return bin(mx >> 1).count("1") + my + 0.1 * (mx & 1)

    pairs = [(mx, my) for mx in range(nx) for my in range(ny) if mx or my]
    return sorted(pairs, key=hops, reverse=True)


def step_kernel(
    nx, ny, modes,
    b_hbm, a_hbm, cols_hbm, s_hbm, n_hbm, map_hbm, inv_hbm,
    solution_ref, residual_ref,
    b_ref, a_ref, cols_ref, s_ref, n_ref, map_ref, inv_ref, loaded,
    blocks, nulls, field, up, down, left, right, local, edge, smoother, info, info_all, near, coarse, coarse_all,
    sums, sums_all, spread, relaxed, relaxed_near, reach, solved, pulls, pulls_near, pushed, pulled,
    halo_send, halo_recv, near_send, near_recv, relaxed_send, relaxed_recv, pulls_send, pulls_recv, push_send, push_recv, col_send, col_recv,
    plane_send, plane_recv, pair_send, pair_recv, direct_send, direct_recv, entered,
):
    rows, cols, blk, cases = b_ref.shape
    count = rows * cols
    size = count * blk
    n = nx * ny
    width = info.shape[1]
    coarse_rows = n * 8
    around = spread.shape[0]
    x, y = lax.axis_index("gx"), lax.axis_index("gy")
    me = x * ny + y
    sides = (
        (x > 0, (x - 1, y)),
        (x < nx - 1, (x + 1, y)),
        (y > 0, (x, y - 1)),
        (y < ny - 1, (x, y + 1)),
    )
    halos = (up, down, left, right)
    order_of_peers = far_first(nx, ny)
    peers_x = [flipped(x, m) for m in range(nx)]
    peers_y = [flipped(y, m) for m in range(ny)]
    barrier = pltpu.get_barrier_semaphore()

    loads = [
        pltpu.make_async_copy(src, dst, loaded.at[i])
        for i, (src, dst) in enumerate(
            (
                (s_hbm, s_ref), (b_hbm, b_ref), (n_hbm, n_ref), (inv_hbm, inv_ref),
                (map_hbm, map_ref), (cols_hbm, cols_ref), (a_hbm, a_ref),
            )
        )
    ]
    for load in loads[0:2]:
        load.start()

    coarse_all[...] = jnp.zeros_like(coarse_all)
    info_all[...] = jnp.zeros_like(info_all)

    lines = [pair for pair in order_of_peers if 0 in pair]
    for mx, my in lines[::-1]:
        pl.semaphore_signal(
            barrier, inc=1, device_id=(peers_x[mx], peers_y[my]),
            device_id_type=pl.DeviceIdType.MESH,
        )

    for load in loads[2:]:
        load.start()
    spread[...] = jnp.zeros_like(spread)
    reach[...] = jnp.zeros_like(reach)
    pulls[...] = jnp.zeros_like(pulls)
    nulls[...] = jnp.zeros_like(nulls)
    info[...] = jnp.zeros_like(info)
    local[...] = jnp.zeros_like(local)
    for side, (here, _) in enumerate(sides):

        @pl.when(jnp.logical_not(here))
        def _():
            halos[side][...] = jnp.zeros_like(halos[side])
            near[side] = jnp.zeros_like(near[side])
            relaxed_near[side] = jnp.zeros_like(relaxed_near[side])
            pulls_near[side] = jnp.zeros_like(pulls_near[side])
            pulled[side] = jnp.zeros_like(pulled[side])

    told, told_all = info.at[0 : modes + 1], info_all.at[:, 0 : modes + 1]

    def at_column(src, dst):
        return [
            pltpu.make_async_remote_copy(
                src_ref=src, dst_ref=dst.at[me], send_sem=col_send.at[j],
                recv_sem=col_recv.at[ny - j],
                device_id=(x, lax.rem(y + j, ny)), device_id_type=pl.DeviceIdType.MESH,
            )
            for j in range(1, ny)
        ]

    def block(mx):
        return info_all.at[pl.ds(peers_x[mx] * ny, ny), 0 : modes + 1]

    def plane_copy(mx):
        return pltpu.make_async_remote_copy(
            src_ref=block(0), dst_ref=block(0), send_sem=plane_send.at[mx // 2],
            recv_sem=plane_recv.at[mx // 2], device_id=(peers_x[mx], y),
            device_id_type=pl.DeviceIdType.MESH,
        )

    def to_sibling(mx):
        pltpu.make_async_remote_copy(
            src_ref=block(mx), dst_ref=block(mx), send_sem=pair_send, recv_sem=pair_recv,
            device_id=(peers_x[1], y), device_id_type=pl.DeviceIdType.MESH,
        ).start()

    plane = (*range(nx - 2, 0, -2),)

    def told_pass():
        for j in range(1, ny):
            pltpu.make_async_copy(told, told, col_recv.at[j]).wait()
        for mx in plane:
            plane_copy(mx).start()
        to_sibling(0)

    def told_share():
        for mx in plane[::-1]:
            pltpu.make_async_copy(block(mx), block(mx), plane_recv.at[mx // 2]).wait()
            to_sibling(mx)

    def wait_many(dst, tiles, sem):
        some = dst.at[pl.ds(0, tiles)]
        pltpu.make_async_copy(some, some, sem).wait()

    def to_all(src, dst, k):
        for mx, my in order_of_peers:
            pltpu.make_async_remote_copy(
                src_ref=src, dst_ref=dst.at[me], send_sem=direct_send.at[k],
                recv_sem=direct_recv.at[k], device_id=(peers_x[mx], peers_y[my]),
                device_id_type=pl.DeviceIdType.MESH,
            ).start()

    def halo_copies(k):
        now = field.at[k]
        out = (
            (now.at[0], down.at[k], 1),
            (now.at[rows - 1], up.at[k], 0),
            (now.at[:, 0], right.at[k], 3),
            (now.at[:, cols - 1], left.at[k], 2),
        )
        return [
            pltpu.make_async_remote_copy(
                src_ref=src, dst_ref=dst,
                send_sem=halo_send.at[k, side], recv_sem=halo_recv.at[k, lands],
                device_id=peer, device_id_type=pl.DeviceIdType.MESH,
            )
            for side, ((src, dst, lands), (_, peer)) in enumerate(zip(out, sides))
        ]

    def halo_start(k):
        for (here, _), copy in zip(sides, halo_copies(k)):
            pl.when(here)(copy.start)

    def halo_wait(k, side):
        buf = halos[side].at[k]
        pl.when(sides[side][0])(pltpu.make_async_copy(buf, buf, halo_recv.at[k, side]).wait)

    def to_sides(src, dst, send, recv, split=False):
        return [
            pltpu.make_async_remote_copy(
                src_ref=src.at[side] if split else src, dst_ref=dst.at[lands],
                send_sem=send.at[side], recv_sem=recv.at[lands],
                device_id=peer, device_id_type=pl.DeviceIdType.MESH,
            )
            for side, (lands, (_, peer)) in enumerate(zip((1, 0, 3, 2), sides))
        ]

    def near_copies():
        return to_sides(nulls, near, near_send, near_recv)

    def relaxed_copies():
        return to_sides(relaxed, relaxed_near, relaxed_send, relaxed_recv)

    def pulls_copies():
        return to_sides(pulls, pulls_near, pulls_send, pulls_recv, split=True)

    def push_copies():
        return to_sides(pushed, pulled, push_send, push_recv, split=True)

    def from_sides(dst, recv):
        for side, (here, _) in enumerate(sides):
            buf = dst.at[side]
            pl.when(here)(pltpu.make_async_copy(buf, buf, recv.at[side]).wait)

    loads[0].wait()
    for i in range(rows):
        for j in range(cols):
            p = i * cols + j
            for c in range(0, blk * blk, 128):
                blocks[p, 0, c // 128 : c // 128 + 1] = s_ref[j, i : i + 1, c : c + 128]
            flat = blocks[p, 0, 0 : blk * blk // 128]
            for half in range(128 // blk):
                blocks[p, 1, pl.ds(half, blk * blk // 128, stride=128 // blk), 0:blk] = flat[
                    :, half * blk : (half + 1) * blk
                ]
    for p in range(count):
        hi, lo = cut(relax_weight * blocks[p, 1, :, 0:blk])
        smoother[p] = jnp.concatenate([hi, hi, lo], axis=1)

    def smooth(v):
        return jnp.concatenate(
            [mm(smoother[p], stacked(v[p * blk : (p + 1) * blk])) for p in range(count)], axis=0
        )

    def put(v, k):
        field[k] = v.reshape(rows, cols, blk, cases)

    loads[1].wait()
    b = b_ref[...].reshape(size, cases)
    first = smooth(b)
    put(first, 0)

    for load in loads[2:5]:
        load.wait()
    for i in range(rows):
        for j in range(cols):
            p = i * cols + j
            for k in range(modes):
                nulls[k : k + 1, p * blk : (p + 1) * blk] = n_ref[
                    j, i : i + 1, k * blk : (k + 1) * blk
                ]
    info[0:modes, 0 : inv_ref.shape[1]] = inv_ref[...]
    info[modes : modes + 1, :] = jnp.full((1, width), map_ref[0, 0].astype(jnp.float32))

    pl.semaphore_wait(barrier, len(lines))
    for (here, _), copy in zip(sides, near_copies()):
        pl.when(here)(copy.start)
    for copy in at_column(told, told_all):
        copy.start()
    halo_start(0)
    for mx in range(1, nx):
        pl.semaphore_signal(
            entered, inc=1, device_id=(peers_x[mx], y), device_id_type=pl.DeviceIdType.MESH
        )
    info_all[pl.ds(me, 1)] = info[...][None]

    loads[5].wait()
    loads[6].wait()
    for i in range(rows):
        for j in range(cols):
            p = i * cols + j
            tiles = [a_ref[i, j, :, s * blk : (s + 1) * blk] for s in range(5)]
            names = [cols_ref[j, i, s] for s in range(5)]
            for d, (di, dj) in enumerate(((0, 0), (-1, 0), (1, 0), (0, -1), (0, 1))):
                e = (i + 1 + di) * (cols + 2) + j + 1 + dj
                tile = tiles[0] * (names[0] == e).astype(jnp.float32)
                for s in range(1, 5):
                    tile = tile + tiles[s] * (names[s] == e).astype(jnp.float32)
                hi, lo = cut(tile)
                ii, jj = i + di, j + dj
                if 0 <= ii < rows and 0 <= jj < cols:
                    q = ii * cols + jj
                    for k, part in enumerate((hi, hi, lo)):
                        at = k * size + q * blk
                        local[p * blk : (p + 1) * blk, at : at + blk] = part
                else:
                    at = (0, j, cols + j, 2 * cols + i, 2 * cols + rows + i)[d]
                    edge[at] = jnp.concatenate([hi, hi, lo], axis=1)

    def places():
        for j in range(cols):
            yield 0, j, j, j
        for j in range(cols):
            yield 1, j, cols + j, (rows - 1) * cols + j
        for i in range(rows):
            yield 2, i, 2 * cols + i, i * cols
        for i in range(rows):
            yield 3, i, 2 * cols + rows + i, i * cols + cols - 1

    def own_part(v):
        return mm(local[...], stacked(v))

    def operate(v, k):
        return beyond(own_part(v), k)

    def beyond(inner, k):
        parts = [inner[p * blk : (p + 1) * blk] for p in range(count)]
        for side in (2, 3, 0, 1):
            halo_wait(k, side)
            for at_side, at, e, p in places():
                if at_side == side:
                    parts[p] = parts[p] + mm(edge[e], stacked(halos[side][k, at]))
        return jnp.concatenate(parts, axis=0)

    own_n = nulls[...]
    inner_first = own_part(first)
    own_hi, own_lo = cut(own_n)
    own_cat = jnp.concatenate([own_hi, own_hi, own_lo], axis=1)

    def mine(k):
        return coarse.at[k, 0:modes]

    def theirs_all(k):
        return coarse_all.at[k, :, 0:modes]

    def publish(g, k):
        coarse[k] = g
        to_all(mine(k), theirs_all(k), k)
        coarse_all[k, pl.ds(me, 1)] = g[None]

    def gathered(k):
        wait_many(theirs_all(k), n - 1, direct_recv.at[k])
        return coarse_all[k].reshape(coarse_rows, cases)

    def across(v):
        hi, lo = cut(v)
        return jnp.concatenate([hi, lo, hi], axis=1)

    facing = (
        lambda at: (rows - 1) * cols + at,
        lambda at: at,
        lambda at: at * cols + cols - 1,
        lambda at: at * cols,
    )
    spread[0:8] = mm_t(across(own_n), local[...])
    from_sides(near, near_recv)
    for side, at, e, p in places():
        q = facing[side](at)
        spread[8 * (1 + side) : 8 * (2 + side), p * blk : (p + 1) * blk] = mm_t(
            across(near[side, :, q * blk : (q + 1) * blk]), edge[e]
        )
    for p in range(count):
        relaxed[:, p * blk : (p + 1) * blk] = mm_t(
            across(spread[:, p * blk : (p + 1) * blk]), smoother[p]
        )
    for (here, _), copy in zip(sides, relaxed_copies()):
        pl.when(here)(copy.start)
    told_pass()

    reach[0:around] = spread[...] - mm_t(across(relaxed[...]), local[...])
    eye = (
        lax.broadcasted_iota(jnp.int32, (size, size), 0)
        == lax.broadcasted_iota(jnp.int32, (size, size), 1)
    ).astype(jnp.float32).astype(jnp.bfloat16)

    def turned(v):
        return tuple(mm_t(eye, part).astype(jnp.bfloat16) for part in cut(v))

    gain = turned(
        jnp.concatenate([own_n - relaxed[0:8], 0.0 - relaxed[8:around]], axis=0)
    )
    for side, at, e, p in places():
        q = facing[side](at)
        hi, lo = own_hi[:, p * blk : (p + 1) * blk], own_lo[:, p * blk : (p + 1) * blk]
        tile, rest = edge[e, :, 0:blk], edge[e, :, 2 * blk : 3 * blk]
        pulls[side, :, q * blk : (q + 1) * blk] = mm(hi, tile) + (mm(hi, rest) + mm(lo, tile))
    for (here, _), copy in zip(sides, pulls_copies()):
        pl.when(here)(copy.start)

    inner_pull = mm(own_hi, local[:, 0:size]) + (
        mm(own_hi, local[:, 2 * size : 3 * size]) + mm(own_lo, local[:, 0:size])
    )

    r = b - beyond(inner_first, 0)
    pl.semaphore_wait(entered, nx - 1)
    publish(mm(own_cat, stacked(r)), 0)
    t = smooth(r)
    put(t, 1)
    halo_start(1)
    told_share()

    from_sides(relaxed_near, relaxed_recv)
    for side, at, e, p in places():
        q = facing[side](at)
        reach[around * (1 + side) : around * (2 + side), p * blk : (p + 1) * blk] = 0.0 - mm_t(
            across(relaxed_near[side, :, q * blk : (q + 1) * blk]), edge[e]
        )
    reach_turned = turned(reach[...])
    wait_many(told_all, nx // 2 * ny, pair_recv)
    inv_parts = cut(info_all[...].reshape(coarse_rows, width))
    lane3 = lax.broadcasted_iota(jnp.int32, (n, 8, width), 2).astype(jnp.float32)
    row3 = lax.broadcasted_iota(jnp.int32, (n, 8, width), 1)
    labels = jnp.broadcast_to(info_all[...][:, modes : modes + 1, :], (n, 8, width))
    where3 = labels * float(modes) + row3.astype(jnp.float32)
    order = jnp.where(lane3 == where3, 1.0, 0.0)
    order = jnp.where(row3 < modes, order, 0.0).reshape(coarse_rows, width).astype(jnp.bfloat16)
    lane4 = lax.broadcasted_iota(jnp.int32, (n, 8, coarse_rows), 2).astype(jnp.float32)
    row4 = lax.broadcasted_iota(jnp.int32, (n, 8, coarse_rows), 1)
    labels4 = jnp.broadcast_to(info_all[...][:, modes : modes + 1, 0:1], (n, 8, coarse_rows))
    pick = jnp.where(lane4 == labels4 * 8.0 + row4.astype(jnp.float32), 1.0, 0.0)
    pick = jnp.where(row4 < modes, pick, 0.0).reshape(coarse_rows, coarse_rows).astype(jnp.bfloat16)
    for k, part in enumerate(inv_parts):
        solved[k] = mm_t(mm(pick, part).astype(jnp.bfloat16), order)

    def clipped(px, py):
        return jnp.clip(px, 0, nx - 1) * ny + jnp.clip(py, 0, ny - 1)

    def cross(px, py):
        return [
            clipped(px + dx, py + dy)
            for dx, dy in ((0, 0), (-1, 0), (1, 0), (0, -1), (0, 1))
        ]

    ids = cross(x, y)
    for _, (px, py) in sides:
        ids = ids + cross(px, py)
    lacking = jnp.zeros((reach.shape[0] - 8 * len(ids), coarse_rows), jnp.float32)
    solve = tuple(
        jnp.concatenate(
            [solved[k, pl.ds(pl.multiple_of(d * 8, 8), 8)] for d in ids] + [lacking], axis=0
        ).astype(jnp.bfloat16)
        for k in range(2)
    )

    def laid(v):
        hi, lo = cut(v)
        return jnp.concatenate([hi, hi, lo], axis=1)

    def mm3_cut(a_cut, b_cut):
        return mm(a_cut[0], b_cut[0]) + (mm(a_cut[0], b_cut[1]) + mm(a_cut[1], b_cut[0]))

    gain_laid = laid(mm3_cut(gain, tuple(part[0:around] for part in solve)))

    loss_laid = laid(mm3_cut(reach_turned, solve))

    from_sides(pulls_near, pulls_recv)
    pull_hi, pull_lo = cut(
        jnp.concatenate([pulls_near[...].reshape(32, size), inner_pull], axis=0)
    )
    pull_cat = jnp.concatenate([pull_hi, pull_hi, pull_lo], axis=1)

    q1 = r - operate(t, 1)
    g = gathered(0)
    r = q1 - mm(loss_laid, stacked(g))
    s = smooth(r)
    products = mm(pull_cat, stacked(s))
    for side in range(4):
        pushed[side] = products[8 * side : 8 * side + 8]
    for (here, _), copy in zip(sides, push_copies()):
        pl.when(here)(copy.start)
    put(s, 2)
    halo_start(2)
    mine_now = mm(own_cat, stacked(r)) - products[32:40]
    precond = first + t + mm(gain_laid, stacked(g)) + s
    from_sides(pulled, push_recv)
    publish(mine_now - ((pulled[0] + pulled[1]) + (pulled[2] + pulled[3])), 1)
    r = r - operate(s, 2)
    t = smooth(r)
    put(t, 3)
    halo_start(3)
    precond = precond + t
    inner = (b - r) + own_part(t)
    g = gathered(1)
    precond = precond + mm(gain_laid, stacked(g))
    aligned = jnp.sum(b * precond, axis=0, keepdims=True)
    image = beyond(inner + mm(loss_laid, stacked(g)), 3)
    sums[...] = jnp.concatenate(
        [
            aligned,
            jnp.sum(precond * image, axis=0, keepdims=True),
            jnp.zeros((6, cases), jnp.float32),
        ],
        axis=0,
    )
    pairs = sums_all.at[:, 0:2]
    to_all(sums.at[0:2], pairs, 2)
    sums_all[pl.ds(me, 1)] = sums[...][None]
    for k in range(4):
        for (here, _), copy in zip(sides, halo_copies(k)):
            pl.when(here)(copy.wait_send)
    for (here, _), copy in zip(sides, near_copies()):
        pl.when(here)(copy.wait_send)
    for copies in (relaxed_copies(), pulls_copies(), push_copies()):
        for (here, _), copy in zip(sides, copies):
            pl.when(here)(copy.wait_send)
    for copy in at_column(told, told_all):
        copy.wait_send()
    for mx in plane:
        plane_copy(mx).wait_send()
    wait_many(told_all, nx // 2 * ny, pair_send)
    for k in range(2):
        wait_many(theirs_all(k), n - 1, direct_send.at[k])
    wait_many(pairs, n - 1, direct_recv.at[2])
    total = jnp.sum(sums_all[:, 0:2], axis=0)
    alpha = total[0:1] / total[1:2]
    solution_ref[...] = (alpha * precond).reshape(rows, cols, blk, cases)
    residual_ref[...] = (b - alpha * image).reshape(rows, cols, blk, cases)
    wait_many(pairs, n - 1, direct_send.at[2])


def finish_kernel(s_ref, r_ref, sol_ref, res_ref, sems):
    copies = [
        pltpu.make_async_copy(src, dst, sems.at[k])
        for k, (src, dst) in enumerate(((s_ref, sol_ref), (r_ref, res_ref)))
    ]
    for copy in copies:
        copy.start()
    for copy in copies:
        copy.wait()


def fused(
    nx, ny,
    load_cases, matrix_tiles, block_cols, smoother_blocks, near_null, coarse_map, coarse_inverse
):
    rows, cols, blk, cases = load_cases.shape
    count = rows * cols
    modes = near_null.shape[2] // blk
    n = nx * ny
    width = -(-coarse_inverse.shape[1] // 128) * 128
    block_cols = jnp.transpose(block_cols, (1, 0, 2))
    smoother_blocks = jnp.transpose(smoother_blocks, (1, 0, 2))
    near_null = jnp.transpose(near_null, (1, 0, 2))
    vmem = pl.BlockSpec(memory_space=pltpu.VMEM)
    hbm = pl.BlockSpec(memory_space=pltpu.HBM)
    f32, bf16 = jnp.float32, jnp.bfloat16
    shape = jax.ShapeDtypeStruct(load_cases.shape, f32)
    held = pltpu.VMEM(load_cases.shape, f32)
    solved, residual = pl.pallas_call(
        functools.partial(step_kernel, nx, ny, modes),
        out_shape=(held, held),
        in_specs=[hbm] * 7,
        out_specs=(vmem, vmem),
        scratch_shapes=[
            pltpu.VMEM(load_cases.shape, f32),
            pltpu.VMEM(matrix_tiles.shape, f32),
            pltpu.SMEM(block_cols.shape, jnp.int32),
            pltpu.VMEM(smoother_blocks.shape, f32),
            pltpu.VMEM(near_null.shape, f32),
            pltpu.SMEM(coarse_map.shape, jnp.int32),
            pltpu.VMEM(coarse_inverse.shape, f32),
            pltpu.SemaphoreType.DMA((7,)),
            pltpu.VMEM((count, 2, blk, 128), f32),
            pltpu.VMEM((8, count * blk), f32),
            pltpu.VMEM((4, rows, cols, blk, cases), f32),
            pltpu.VMEM((4, cols, blk, cases), f32),
            pltpu.VMEM((4, cols, blk, cases), f32),
            pltpu.VMEM((4, rows, blk, cases), f32),
            pltpu.VMEM((4, rows, blk, cases), f32),
            pltpu.VMEM((count * blk, 3 * count * blk), bf16),
            pltpu.VMEM((2 * (rows + cols), blk, 3 * blk), bf16),
            pltpu.VMEM((count, blk, 3 * blk), bf16),
            pltpu.VMEM((8, width), f32),
            pltpu.VMEM((n, 8, width), f32),
            pltpu.VMEM((4, 8, count * blk), f32),
            pltpu.VMEM((2, 8, cases), f32),
            pltpu.VMEM((2, n, 8, cases), f32),
            pltpu.VMEM((8, cases), f32),
            pltpu.VMEM((n, 8, cases), f32),
            pltpu.VMEM((40, count * blk), f32),
            pltpu.VMEM((40, count * blk), f32),
            pltpu.VMEM((4, 40, count * blk), f32),
            pltpu.VMEM((256, count * blk), f32),
            pltpu.VMEM((2, n * 8, n * 8), f32),
            pltpu.VMEM((4, 8, count * blk), f32),
            pltpu.VMEM((4, 8, count * blk), f32),
            pltpu.VMEM((4, 8, cases), f32),
            pltpu.VMEM((4, 8, cases), f32),
            pltpu.SemaphoreType.DMA((4, 4)),
            pltpu.SemaphoreType.DMA((4, 4)),
            pltpu.SemaphoreType.DMA((4,)),
            pltpu.SemaphoreType.DMA((4,)),
            pltpu.SemaphoreType.DMA((4,)),
            pltpu.SemaphoreType.DMA((4,)),
            pltpu.SemaphoreType.DMA((4,)),
            pltpu.SemaphoreType.DMA((4,)),
            pltpu.SemaphoreType.DMA((4,)),
            pltpu.SemaphoreType.DMA((4,)),
            pltpu.SemaphoreType.DMA((ny,)),
            pltpu.SemaphoreType.DMA((ny,)),
            pltpu.SemaphoreType.DMA((nx // 2,)),
            pltpu.SemaphoreType.DMA((nx // 2,)),
            pltpu.SemaphoreType.DMA,
            pltpu.SemaphoreType.DMA,
            pltpu.SemaphoreType.DMA((3,)),
            pltpu.SemaphoreType.DMA((3,)),
            pltpu.SemaphoreType.REGULAR,
        ],
        compiler_params=pltpu.CompilerParams(
            collective_id=0, has_side_effects=True, vmem_limit_bytes=32 * 2**20
        ),
    )(
        *(
            pltpu.with_memory_space_constraint(v, pltpu.HBM)
            for v in (
                load_cases, matrix_tiles, block_cols, smoother_blocks, near_null, coarse_map,
                coarse_inverse,
            )
        )
    )
    return pl.pallas_call(
        finish_kernel,
        out_shape=(shape, shape),
        in_specs=[vmem, vmem],
        out_specs=(hbm, hbm),
        scratch_shapes=[pltpu.SemaphoreType.DMA((2,))],
        compiler_params=pltpu.CompilerParams(vmem_limit_bytes=32 * 2**20),
    )(
        *(pltpu.with_memory_space_constraint(v, pltpu.VMEM) for v in (solved, residual))
    )


def per_device(
    load_cases, matrix_tiles, block_cols, smoother_blocks, near_null, coarse_map, coarse_inverse
):
    agg_rows, agg_cols, block_size, case_count = load_cases.shape
    mode_count = near_null.shape[2] // block_size
    coarse_total = coarse_inverse.shape[1]
    coarse_aggs = coarse_total // mode_count
    modes = near_null.reshape(agg_rows, agg_cols, mode_count, block_size)
    inverse_blocks = smoother_blocks.reshape(agg_rows, agg_cols, block_size, block_size)

    steps = ((0, 0), (-1, 0), (1, 0), (0, -1), (0, 1))
    tiles = matrix_tiles.reshape(agg_rows, agg_cols, block_size, -1, block_size)
    row_at = jnp.arange(agg_rows, dtype=jnp.int32)[:, None, None]
    col_at = jnp.arange(agg_cols, dtype=jnp.int32)[None, :, None]
    stencil = []
    for dx, dy in steps:
        named = block_cols == (row_at + 1 + dx) * (agg_cols + 2) + col_at + 1 + dy
        stencil.append(jnp.sum(jnp.where(named[:, :, None, :, None], tiles, 0.0), axis=3))

    def operate(vector_field):
        extended = padded(vector_field, (("gx", 0), ("gy", 1)), 1)
        total = 0.0
        for tile, (dx, dy) in zip(stencil, steps):
            cells = extended[1 + dx : 1 + dx + agg_rows, 1 + dy : 1 + dy + agg_cols]
            total = total + jnp.einsum("ijbk,ijkr->ijbr", tile, cells, precision=highest)
        return total

    def smooth(defect):
        return relax_weight * jnp.einsum(
            "ijab,ijbr->ijar", inverse_blocks, defect, precision=highest
        )

    def correct(defect):
        contrib = jnp.einsum("ijkb,ijbr->ijkr", modes, defect, precision=highest)
        own_part = jnp.sum(contrib, axis=(0, 1))
        my_label = coarse_map[0, 0]
        label_value = jnp.reshape(my_label.astype(jnp.float32), (1,))
        pieces, labels = (
            lax.all_gather(own_part[None], ("gx", "gy"), axis=0, tiled=True),
            lax.all_gather(label_value, ("gx", "gy"), axis=0, tiled=True),
        )
        label_ids = labels.astype(jnp.int32)
        placing = (label_ids[:, None] == jnp.arange(coarse_aggs, dtype=jnp.int32)[None, :]).astype(
            jnp.float32
        )
        ordered = jnp.einsum("dc,dkr->ckr", placing, pieces, precision=highest).reshape(
            coarse_total, case_count
        )
        own_rows = jnp.dot(coarse_inverse, ordered, precision=highest)
        solved = lax.all_gather(own_rows, ("gx", "gy"), axis=0, tiled=True)
        mine = lax.dynamic_slice_in_dim(solved, my_label * mode_count, mode_count, 0)
        coarse_back = jnp.broadcast_to(
            mine[None, None], (agg_rows, agg_cols, mode_count, case_count)
        )
        return jnp.einsum("ijkb,ijkr->ijbr", modes, coarse_back, precision=highest)

    first = smooth(load_cases)
    first = first + correct(load_cases - operate(first))
    precond = first + smooth(load_cases - operate(first))
    defect = load_cases - operate(precond)
    update = smooth(defect)
    update = update + correct(defect - operate(update))
    update = update + smooth(defect - operate(update))
    precond = precond + update
    local_aligned = jnp.sum(load_cases * precond, axis=(0, 1, 2))
    aligned = lax.psum(local_aligned, ("gx", "gy"))
    image = operate(precond)
    curved = lax.psum(jnp.sum(precond * image, axis=(0, 1, 2)), ("gx", "gy"))
    alpha = aligned / curved
    solution = alpha * precond
    residual = load_cases - alpha * image
    return (solution, residual)


def solution(mesh):
    nx, ny = mesh.shape["gx"], mesh.shape["gy"]
    step = functools.partial(fused, nx, ny) if nx * ny <= 128 else per_device
    placed = (
        P("gx", "gy", None, None),
        P("gx", "gy", None, None),
        P("gx", "gy", None),
        P("gx", "gy", None),
        P("gx", "gy", None),
        P("gx", "gy"),
        P(("gx", "gy"), None),
    )
    return jax.shard_map(
        step,
        mesh=mesh,
        in_specs=placed,
        out_specs=(P("gx", "gy", None, None), P("gx", "gy", None, None)),
        check_vma=False,
    )
```
